32 devices in a mesh: seq: 8 (over y, x, core), tp: 4 (over z).
Axes of the slice: x: 2, y: 2, z: 4, core: 2. Of those that a mesh axis runs over, the one named last changes fastest.
Arguments:
- patches: bfloat16 [2048, 1024], P('seq', 'tp'), may hold values from -6 to 6
- byte_embed: bfloat16 [16384, 1024], P('seq', 'tp'), may hold values from -6 to 6
- seq_lengths: int32 [6], replicated, may hold values from 1 to 1024, 2048 in all
- norm_global: float32 [1024], replicated, may hold values from 0.5 to 1.5
- proj_gate: bfloat16 [1024, 2048], P(None, 'tp'), may hold values from -0.1875 to 0.1875
- proj_inner: bfloat16 [1024, 2048], P(None, 'tp'), may hold values from -0.1875 to 0.1875
- proj_state: bfloat16 [1024, 256], replicated, may hold values from -0.1875 to 0.1875
- proj_step: bfloat16 [1024, 32], P(None, 'tp'), may hold values from -0.1875 to 0.1875
- step_bias: float32 [32], P('tp'), may hold values from -3 to 0.5
- decay_log: float32 [32], P('tp'), may hold values from -7 to -1
- conv_inner: float32 [4, 2048], P(None, 'tp'), may hold values from -3 to 3
- conv_state: float32 [4, 256], replicated, may hold values from -3 to 3
- skip_gain: float32 [32], P('tp'), may hold values from 0.5 to 1.5
- mixer_gain: float32 [2048], P('tp'), may hold values from 0.5 to 1.5
- proj_mixer: bfloat16 [2048, 1024], P('tp'), may hold values from -0.125 to 0.125
- norm_attn: float32 [1024], replicated, may hold values from 0.5 to 1.5
- attn_input: bfloat16 [3, 1024, 1024], P(None, None, 'tp'), may hold values from -0.1875 to 0.1875
- attn_output: bfloat16 [1024, 1024], P('tp'), may hold values from -0.375 to 0.375
- norm_ffn: float32 [1024], replicated, may hold values from 0.5 to 1.5
- expand_weight: bfloat16 [2, 1024, 4096], P(None, None, 'tp'), may hold values from -0.1875 to 0.1875
- shrink_weight: bfloat16 [4096, 1024], P('tp'), may hold values from -0.09375 to 0.09375
- grad_output: bfloat16 [16384, 1024], P('seq', 'tp'), may hold values from -6 to 6
Outputs:
- layer_output: bfloat16 [16384, 1024], P('seq', 'tp')
- embed_grad: float32 [16384, 1024], P('seq', 'tp')
- patch_grad: float32 [2048, 1024], P('seq', 'tp')
- norm_global_grad: float32 [1024], replicated
- proj_gate_grad: float32 [1024, 2048], P(None, 'tp')
- proj_inner_grad: float32 [1024, 2048], P(None, 'tp')
- proj_state_grad: float32 [1024, 256], replicated
- proj_step_grad: float32 [1024, 32], P(None, 'tp')
- step_bias_grad: float32 [32], P('tp')
- decay_log_grad: float32 [32], P('tp')
- conv_inner_grad: float32 [4, 2048], P(None, 'tp')
- conv_state_grad: float32 [4, 256], replicated
- skip_gain_grad: float32 [32], P('tp')
- mixer_gain_grad: float32 [2048], P('tp')
- proj_mixer_grad: float32 [2048, 1024], P('tp')
- norm_attn_grad: float32 [1024], replicated
- attn_input_grad: float32 [3, 1024, 1024], P(None, None, 'tp')
- attn_output_grad: float32 [1024, 1024], P('tp')
- norm_ffn_grad: float32 [1024], replicated
- expand_grad: float32 [2, 1024, 4096], P(None, None, 'tp')
- shrink_grad: float32 [4096, 1024], P('tp')
The draws below stay inside these ranges and needn't reach their ends.
Inputs may be any that keep to these rules, and one draw needn't show every extreme that they name: `seq_lengths`: lengths of the packed sequences in patches; they sum to 2048 and the longest is exactly 1024.
All inputs are finite; a program needn't handle non-finite values.
Results may differ from the reference program's by a relative error of at most 0.023.
The reference program's roundings to bfloat16 on the way (of `normed`, `normed_mix`, `attn_normed`, `context`, `ffn_normed` and `activ`) count: a program that leaves them out, or rounds other values in their place, can miss the bound.
Values may be sent and summed in bfloat16 or wider, within the bound.
No kernel may reach another device: no remote copies, remote signals or barrier semaphores. Data moves between devices by JAX's collectives and lax.ppermute only.
A program may use at most 256 MiB of HBM per device.

```python
import math
import jax
import jax.numpy as jnp
import numpy as np
from jax import lax

D = 1024
HEADS_M = 32
HEAD_DIM = 64
STATE = 128
HEADS_A = 16
FF = 4096
CONV = 4
PATCH = 8
NSEQS = 6
PATCH_DEV = 256
DI = 2048
PATCHES = 2048
BYTES = 16384


def block_levels(key, dims, cuts, smallest, largest):
    def one(dim, parts):
        draws = jax.random.uniform(jax.random.fold_in(jax.random.fold_in(key, 6), dim), (parts,), jnp.float32, smallest / len(cuts), largest / len(cuts))
        return jnp.repeat(jnp.exp(draws), dims[dim] // parts).reshape((-1,) + (1,) * (len(dims) - dim - 1))

    level = one(*cuts[0])
    for cut in cuts[1:]:
        level = level * one(*cut)
    return level


def profile(amount, total, most, slope):
    loads = [(1 << 20) // math.isqrt(grade ** slope) + 1 for grade in range(2, amount + 1)]
    spare, counts = total - most - (amount - 1), [1] * (amount - 1)
    while spare > 0:
        candidates = [i for i in range(amount - 1) if counts[i] < most]
        pool, left = sum([loads[i] for i in candidates]), spare
        for i in candidates:
            extra = min(most - counts[i], max(1, left * loads[i] // pool), spare)
            counts[i] = counts[i] + extra
            spare = spare - extra
    return np.array([most] + counts)


def uneven_parts(key, count, total, limit, lean):
    if count == 2:
        one = jax.random.randint(key, (), max(1, total - limit), min(limit, total - 1) + 1)
        return jnp.stack([one, total - one])
    tallies = jnp.asarray(profile(count, total, limit, lean), jnp.int32)
    pairs = (count - 1) // 2
    source_of, receiver = tallies[1:1 + 2 * pairs:2], tallies[2:2 + 2 * pairs:2]
    slack = jnp.minimum(source_of - 1, limit - receiver)
    shifted = jax.random.randint(jax.random.fold_in(key, 1), (pairs,), 0, 1 << 20) % (slack + 1)
    tallies = tallies.at[1:1 + 2 * pairs:2].set(source_of - shifted).at[2:2 + 2 * pairs:2].set(receiver + shifted)
    return tallies[jax.random.permutation(jax.random.fold_in(key, 2), count)]


def centred(stream_key, dims, scale, limit, cuts=(), held_as=jnp.bfloat16):
    loudness = block_levels(stream_key, dims, cuts, -0.22, 0.18) if cuts else 1.0
    drawn = jax.random.normal(stream_key, dims, jnp.float32) * scale * loudness
    return jnp.minimum(jnp.maximum(drawn, -limit), limit).astype(held_as)


def setup_inputs(seed: int = 0) -> dict:
    splits = jax.random.split(jax.random.key(seed), 23)
    return {
        "patches": centred(splits[0], (PATCHES, D), 1.0, 6.0, ((0, 8), (1, 4))),
        "byte_embed": centred(splits[1], (BYTES, D), 1.0, 6.0, ((0, 8), (1, 4))),
        "seq_lengths": uneven_parts(splits[2], NSEQS, PATCHES, PATCHES // 2, 2).astype(jnp.int32),
        "norm_global": jnp.clip(1.0 + 0.1 * jax.random.normal(splits[3], (D,), jnp.float32), 0.5, 1.5),
        "proj_gate": centred(splits[4], (D, DI), D ** -0.5, 0.1875, ((1, 4),)),
        "proj_inner": centred(splits[5], (D, DI), D ** -0.5, 0.1875, ((1, 4),)),
        "proj_state": centred(splits[6], (D, 2 * STATE), D ** -0.5, 0.1875),
        "proj_step": centred(splits[7], (D, HEADS_M), D ** -0.5, 0.1875, ((1, 4),)),
        "step_bias": jnp.clip(-3.0 + 3.5 * jax.random.uniform(splits[8], (HEADS_M,), jnp.float32) ** block_levels(splits[8], (HEADS_M,), ((0, 4),), -0.2, 0.2), -3.0, 0.5),
        "decay_log": jnp.clip(-7.0 + 6.0 * jax.random.uniform(splits[9], (HEADS_M,), jnp.float32) ** block_levels(splits[9], (HEADS_M,), ((0, 4),), -0.2, 0.2), -7.0, -1.0),
        "conv_inner": centred(splits[10], (CONV, DI), CONV ** -0.5, 3.0, ((1, 4),), jnp.float32),
        "conv_state": centred(splits[11], (CONV, 2 * STATE), CONV ** -0.5, 3.0, (), jnp.float32),
        "skip_gain": jnp.clip(0.5 + 1.0 * jax.random.uniform(splits[12], (HEADS_M,), jnp.float32) ** block_levels(splits[12], (HEADS_M,), ((0, 4),), -0.2, 0.2), 0.5, 1.5),
        "mixer_gain": jnp.clip(1.0 + 0.1 * jax.random.normal(splits[13], (DI,), jnp.float32), 0.5, 1.5),
        "proj_mixer": centred(splits[14], (DI, D), DI ** -0.5, 0.125, ((0, 4),)),
        "norm_attn": jnp.clip(1.0 + 0.1 * jax.random.normal(splits[15], (D,), jnp.float32), 0.5, 1.5),
        "attn_input": centred(splits[16], (3, D, D), D ** -0.5, 0.1875, ((2, 4),)),
        "attn_output": centred(splits[17], (D, D), (D // 4) ** -0.5, 0.375, ((0, 4),)),
        "norm_ffn": jnp.clip(1.0 + 0.1 * jax.random.normal(splits[18], (D,), jnp.float32), 0.5, 1.5),
        "expand_weight": centred(splits[19], (2, D, FF), D ** -0.5, 0.1875, ((2, 4),)),
        "shrink_weight": centred(splits[20], (FF, D), FF ** -0.5, 0.09375, ((0, 4),)),
        "grad_output": centred(splits[21], (BYTES, D), 1.0, 6.0, ((0, 8), (1, 4))),
    }


epsilon = 1e-05
highest = lax.Precision.HIGHEST

@jax.custom_vjp
def low(v):
    return lax.optimization_barrier(v.astype(jnp.bfloat16)).astype(jnp.float32)

@jax.custom_vjp
def low_back(v):
    return v

def low_keep(v):
    return (low(v), None)

def low_pass(kept, grad):
    return (grad,)

def back_keep(v):
    return (v, None)

def back_low(kept, grad):
    return (low(grad),)
low.defvjp(low_keep, low_pass)
low_back.defvjp(back_keep, back_low)

def matmul(left, right):
    return jnp.dot(left, right, precision=highest, preferred_element_type=jnp.float32)

def rms_scale(values):
    return values * lax.rsqrt(lax.optimization_barrier(jnp.mean(values * values, axis=-1, keepdims=True)) + epsilon)

def sequence_first(positions, lengths):
    offsets = (jnp.cumsum(lengths) - lengths).astype(jnp.int32)
    chosen = jnp.where(offsets[None, :] <= positions[:, None], offsets[None, :], 0)
    return lax.optimization_barrier(jnp.max(chosen, axis=1)).astype(jnp.int32)

def causal_conv(padded, weight, positions, first):
    count = positions.shape[0]
    total = jnp.zeros((count, padded.shape[1]), jnp.float32)
    for offset in range(CONV):
        lag = CONV - 1 - offset
        keep = (positions - lag >= first).astype(jnp.float32)[:, None]
        total = total + weight[offset][None, :] * padded[offset:offset + count] * keep
    return total

def front_part(padded, step_raw, conv_weight, step_bias, decay_log, positions, first):
    activated = jax.nn.silu(causal_conv(padded, conv_weight, positions, first))
    inner = activated.shape[1] - 2 * STATE
    count = positions.shape[0]
    inner_vals = activated[:, :inner].reshape(count, inner // HEAD_DIM, HEAD_DIM)
    bmatrix = activated[:, inner:inner + STATE]
    cmatrix = activated[:, inner + STATE:]
    steps = jax.nn.softplus(step_raw + step_bias[None, :])
    rates = -jnp.exp(decay_log)
    return (inner_vals, bmatrix, cmatrix, steps, rates)

def block_summary(inner_vals, bmatrix, steps, rates, positions, first):
    logs = jnp.cumsum(steps * rates[None, :], axis=0)
    final = logs[-1]
    in_last = (first == first[-1]).astype(jnp.float32)[:, None]
    weights = jnp.exp(final[None, :] - logs) * in_last * steps
    carried = jnp.exp(final) * (first[-1] < positions[0]).astype(jnp.float32)
    states = jnp.einsum('sh,shp,sn->hpn', weights, inner_vals, bmatrix, precision=highest)
    return (carried, states)

def block_output(inner_vals, bmatrix, cmatrix, steps, rates, skip_gain, incoming, positions, first):
    logs = jnp.cumsum(steps * rates[None, :], axis=0)
    count = positions.shape[0]
    same = (first[:, None] == first[None, :]) & (positions[None, :] <= positions[:, None])
    diff = logs.T[:, :, None] - logs.T[:, None, :]
    decay = jnp.where(same[None], jnp.exp(jnp.where(same[None], diff, 0.0)), 0.0)
    inner_prod = jnp.dot(cmatrix, bmatrix.T, precision=highest, preferred_element_type=jnp.float32)
    mixing = decay * inner_prod[None] * steps.T[:, None, :]
    within = jnp.einsum('hts,shp->thp', mixing, inner_vals, precision=highest)
    carry = jnp.exp(logs) * (first < positions[0]).astype(jnp.float32)[:, None]
    remote = jnp.einsum('tn,hpn->thp', cmatrix, incoming, precision=highest) * carry[:, :, None]
    result = within + remote + skip_gain[None, :, None] * inner_vals
    return result.reshape(count, -1)

def mamba_branch(patches, lengths, norm_global, proj_gate, proj_inner, proj_state, proj_step, step_bias, decay_log, conv_inner, conv_state, skip_gain, mixer_gain, proj_mixer):
    count = patches.shape[0]
    positions = jnp.arange(count, dtype=jnp.int32)
    first = sequence_first(positions, lengths)
    normed = low(rms_scale(patches) * norm_global[None, :])
    gate_vals = low_back(matmul(normed, proj_gate))
    inner_raw = low_back(matmul(normed, proj_inner))
    state_raw = low_back(matmul(normed, proj_state))
    step_raw = low_back(matmul(normed, proj_step))
    raw = jnp.concatenate([inner_raw, state_raw], axis=1)
    padded = jnp.concatenate([jnp.zeros((CONV - 1, raw.shape[1]), jnp.float32), raw], axis=0)
    conv_weight = jnp.concatenate([conv_inner, conv_state], axis=1)
    inner_vals, bmatrix, cmatrix, steps, rates = front_part(padded, step_raw, conv_weight, step_bias, decay_log, positions, first)
    blocks = count // PATCH_DEV

    def one_block(incoming, pieces):
        inner_part, bmat_part, cmat_part, steps_part, pos_part, first_part = pieces
        carried, states = block_summary(inner_part, bmat_part, steps_part, rates, pos_part, first_part)
        result = block_output(inner_part, bmat_part, cmat_part, steps_part, rates, skip_gain, incoming, pos_part, first_part)
        return (carried[:, None, None] * incoming + states, result)
    pieces = (inner_vals.reshape(blocks, PATCH_DEV, HEADS_M, HEAD_DIM), bmatrix.reshape(blocks, PATCH_DEV, STATE), cmatrix.reshape(blocks, PATCH_DEV, STATE), steps.reshape(blocks, PATCH_DEV, HEADS_M), positions.reshape(blocks, PATCH_DEV), first.reshape(blocks, PATCH_DEV))
    start = jnp.zeros((HEADS_M, HEAD_DIM, STATE), jnp.float32)
    ending, results = lax.scan(jax.checkpoint(one_block), start, pieces)
    mixed = results.reshape(count, -1)
    gated = mixed * jax.nn.silu(gate_vals)
    normed_mix = low(rms_scale(gated) * mixer_gain[None, :])
    return patches + low_back(matmul(normed_mix, proj_mixer))

def local_block(rows_in, norm_attn, attn_input, attn_output, norm_ffn, expand_weight, shrink_weight):
    count = rows_in.shape[0]
    head_size = D // HEADS_A
    shape_four = (count // PATCH, PATCH, HEADS_A, head_size)
    attn_in = low(rows_in)
    attn_normed = low(rms_scale(attn_in) * norm_attn[None, :])
    query = low(low_back(matmul(attn_normed, attn_input[0]))).reshape(shape_four)
    keys = low(low_back(matmul(attn_normed, attn_input[1]))).reshape(shape_four)
    values = low(low_back(matmul(attn_normed, attn_input[2]))).reshape(shape_four)
    scores = low_back(jnp.einsum('bqhd,bkhd->bhqk', query, keys, precision=highest) * head_size ** (-0.5))
    causal = jnp.arange(PATCH)[:, None] >= jnp.arange(PATCH)[None, :]
    masked = jnp.where(causal, scores, -1e+30)
    expo = jnp.exp(masked - lax.optimization_barrier(jnp.max(masked, axis=-1, keepdims=True)))
    probs = low(expo / lax.optimization_barrier(jnp.sum(expo, axis=-1, keepdims=True)))
    context = low(low_back(jnp.einsum('bhqk,bkhd->bqhd', probs, values, precision=highest))).reshape(count, D)
    hidden_in = rows_in + low_back(matmul(context, attn_output))
    ffn_in = low(hidden_in)
    ffn_normed = low(rms_scale(ffn_in) * norm_ffn[None, :])
    gate_ffn = low_back(matmul(ffn_normed, expand_weight[0]))
    up_ffn = low_back(matmul(ffn_normed, expand_weight[1]))
    activ = low(jax.nn.silu(gate_ffn) * up_ffn)
    return hidden_in + low_back(matmul(activ, shrink_weight))

def reference(patches, byte_embed, seq_lengths, norm_global, proj_gate, proj_inner, proj_state, proj_step, step_bias, decay_log, conv_inner, conv_state, skip_gain, mixer_gain, proj_mixer, norm_attn, attn_input, attn_output, norm_ffn, expand_weight, shrink_weight, grad_output):
    floats = (patches, byte_embed, norm_global, proj_gate, proj_inner, proj_state, proj_step, step_bias, decay_log, conv_inner, conv_state, skip_gain, mixer_gain, proj_mixer, norm_attn, attn_input, attn_output, norm_ffn, expand_weight, shrink_weight)
    floats = tuple((item.astype(jnp.float32) for item in floats))

    def forward(patch_vals, byte_vals, norm_g, gate_w, inner_w, state_w, step_w, bias_s, decay_l, conv_i, conv_s, skip_g, mix_g, mix_w, norm_a, attn_w, attn_o, norm_f, expand_w, shrink_w):
        global_out = mamba_branch(patch_vals, seq_lengths, norm_g, gate_w, inner_w, state_w, step_w, bias_s, decay_l, conv_i, conv_s, skip_g, mix_g, mix_w)
        rows_in = byte_vals + jnp.repeat(global_out, PATCH, axis=0)
        size = PATCH * PATCH_DEV
        blocks = rows_in.reshape(-1, size, D)

        def one_local(block):
            return local_block(block, norm_a, attn_w, attn_o, norm_f, expand_w, shrink_w)
        outputs = lax.map(jax.checkpoint(one_local), blocks)
        return outputs.reshape(-1, D)
    result, pullback = jax.vjp(forward, *floats)
    grads = pullback(grad_output.astype(jnp.float32))
    return (result.astype(jnp.bfloat16), grads[1], grads[0], grads[2], grads[3], grads[4], grads[5], grads[6], grads[7], grads[8], grads[9], grads[10], grads[11], grads[12], grads[13], grads[14], grads[15], grads[16], grads[17], grads[18], grads[19])
```

```python
import functools

import jax
import jax.numpy as jnp
from jax import lax
from jax.experimental import pallas as pl
from jax.experimental.pallas import tpu as pltpu
from jax.sharding import Mesh, PartitionSpec as P

D = 1024
HEAD_DIM = 64
STATE = 128
HEADS_A = 16
CONV = 4
PATCH = 8
DI = 2048
GROUP = 8
TILE = 128
HIDDEN = 512

epsilon = 1e-05
highest = lax.Precision.HIGHEST
F32 = jnp.float32
BF16 = jnp.bfloat16
SEQ = ("g", "s")


def mm(left, right):
    return lax.dot_general(left, right, (((1,), (0,)), ((), ())), preferred_element_type=F32)


def mm_nt(left, right):
    return lax.dot_general(left, right, (((1,), (1,)), ((), ())), preferred_element_type=F32)


def mm_tn(left, right):
    return lax.dot_general(left, right, (((0,), (0,)), ((), ())), preferred_element_type=F32)


def inverse_rms(values):
    return lax.rsqrt(jnp.mean(values * values, axis=-1, keepdims=True) + epsilon)


def params(limit=60):
    return pltpu.CompilerParams(
        dimension_semantics=("arbitrary",), vmem_limit_bytes=limit * 1024 * 1024
    )


def whole(shape):
    return pl.BlockSpec(shape, lambda j: (0,) * len(shape))


def head_mask(width):
    lane = lax.broadcasted_iota(jnp.int32, (1, width), 1) // (D // HEADS_A)
    return [lane == h for h in range(width // (D // HEADS_A))]


def split_heads(tile, masks):
    zero = jnp.zeros_like(tile)
    return jnp.concatenate([jnp.where(m, tile, zero) for m in masks], axis=0)


def tile_mask(heads):
    row = lax.broadcasted_iota(jnp.int32, (heads * TILE, TILE), 0) % TILE
    col = lax.broadcasted_iota(jnp.int32, (heads * TILE, TILE), 1)
    return (row // PATCH == col // PATCH) & (col <= row)


def tile_probs(query_split, keys, keep):
    scores = mm_nt(query_split, keys) * ((D // HEADS_A) ** -0.5)
    scores = jnp.where(keep, scores, -1e30)
    expo = jnp.exp(scores - jnp.max(scores, axis=-1, keepdims=True))
    return expo / jnp.sum(expo, axis=-1, keepdims=True)


def beside(stacked, heads):
    return jnp.concatenate([stacked[h * TILE : (h + 1) * TILE] for h in range(heads)], axis=1)


def attention_forward_kernel(
    embed_ref, global_ref, gain_ref, weight_ref, hidden_ref, input_ref, normed_ref, qkv_ref, context_ref
):
    step = pl.program_id(0)
    blocks, rows, width = embed_ref.shape
    parts = weight_ref.shape[0]
    deep = D // parts

    @pl.when(step == 0)
    def _():
        embed = jnp.concatenate([embed_ref[i] for i in range(blocks)], axis=1).astype(F32)
        spread = jnp.broadcast_to(global_ref[...], (rows // PATCH, PATCH, D)).reshape(rows, D)
        total = embed + spread
        hidden_ref[...] = total
        low = total.astype(BF16)
        input_ref[...] = low
        values = low.astype(F32)
        normed_ref[...] = (values * inverse_rms(values) * gain_ref[...]).astype(BF16)

    normed = normed_ref[...]
    for k in range(3):
        weight = weight_ref[:, 0, k * deep : (k + 1) * deep, :].reshape(D, width)
        qkv_ref[0, k] = mm(normed, weight).astype(BF16)
    masks = head_mask(width)
    heads = len(masks)
    keep = tile_mask(heads)
    for r in range(rows // TILE):
        at = slice(r * TILE, (r + 1) * TILE)
        query = split_heads(qkv_ref[0, 0, at], masks)
        probs = tile_probs(query, qkv_ref[0, 1, at], keep).astype(BF16)
        values = split_heads(qkv_ref[0, 2, at], masks)
        context_ref[0, at] = mm(beside(probs, heads), values).astype(BF16)
    context = context_ref[0]
    piece = width // parts
    for c in range(D // width):
        low = 3 * deep + c * piece
        weight = weight_ref[:, 0, low : low + piece, :].reshape(width, width)
        cols = slice(c * width, (c + 1) * width)
        hidden_ref[:, cols] += mm(context, weight)


def attention_forward(embed, global_rows, gain, weights):
    blocks, rows, width = embed.shape
    parts, tps, depth, _ = weights.shape
    return pl.pallas_call(
        attention_forward_kernel,
        grid=(tps,),
        in_specs=[
            whole((blocks, rows, width)),
            whole((rows // PATCH, 1, D)),
            whole((1, D)),
            pl.BlockSpec((parts, 1, depth, width), lambda j: (0, j, 0, 0)),
        ],
        out_specs=[
            whole((rows, D)),
            whole((rows, D)),
            whole((rows, D)),
            pl.BlockSpec((1, 3, rows, width), lambda j: (j, 0, 0, 0)),
            pl.BlockSpec((1, rows, width), lambda j: (j, 0, 0)),
        ],
        out_shape=[
            jax.ShapeDtypeStruct((rows, D), F32),
            jax.ShapeDtypeStruct((rows, D), BF16),
            jax.ShapeDtypeStruct((rows, D), BF16),
            jax.ShapeDtypeStruct((tps, 3, rows, width), BF16),
            jax.ShapeDtypeStruct((tps, rows, width), BF16),
        ],
        compiler_params=params(),
        name="attention_forward",
        cost_estimate=pl.CostEstimate(
            flops=2 * rows * D * D * 4, bytes_accessed=14 << 20, transcendentals=rows * 2048
        ),
    )(embed, global_rows, gain, weights)


def feed_forward_kernel(
    hidden_ref,
    cot_ref,
    gain_ref,
    expand_ref,
    shrink_ref,
    layer_ref,
    grad_ref,
    gain_grad_ref,
    expand_grad_ref,
    shrink_grad_ref,
    normed_ref,
    turned_ref,
    cot_scratch,
    out_acc,
    normed_acc,
):
    step = pl.program_id(0)
    rows = hidden_ref.shape[0]
    blocks, _, width = cot_ref.shape
    parts = expand_ref.shape[0]
    deep = D // parts
    wide = expand_ref.shape[-1]

    @pl.when(step == 0)
    def _():
        values = hidden_ref[...].astype(BF16).astype(F32)
        normed = (values * inverse_rms(values) * gain_ref[...]).astype(BF16)
        normed_ref[...] = normed
        turned_ref[...] = normed.astype(F32).T.astype(BF16)
        for i in range(blocks):
            cot_scratch[:, i * width : (i + 1) * width] = cot_ref[i]
        out_acc[...] = jnp.zeros_like(out_acc)
        normed_acc[...] = jnp.zeros_like(normed_acc)

    normed = normed_ref[...]
    cot = cot_scratch[...]
    gate_weight = expand_ref[:, 0, :deep, :].reshape(D, wide)
    up_weight = expand_ref[:, 0, deep:, :].reshape(D, wide)
    down_weight = shrink_ref[...].reshape(wide, D)
    gate = mm(normed, gate_weight)
    up = mm(normed, up_weight)
    sigma = 1.0 / (1.0 + jnp.exp(-gate))
    swish = gate * sigma
    activ = (swish * up).astype(BF16)
    out_acc[...] += mm(activ, down_weight)
    shrink_grad_ref[...] = mm_tn(activ, cot).astype(BF16).reshape(shrink_grad_ref.shape)
    dactiv = mm_nt(cot, down_weight)
    dgate = (dactiv * up * sigma * (1.0 + gate * (1.0 - sigma))).astype(BF16)
    dup = (dactiv * swish).astype(BF16)
    normed_acc[...] += mm_nt(dgate, gate_weight) + mm_nt(dup, up_weight)
    turned = turned_ref[...]
    expand_grad_ref[:, 0, :deep, :] = mm(turned, dgate).astype(BF16).reshape(parts, deep, wide)
    expand_grad_ref[:, 0, deep:, :] = mm(turned, dup).astype(BF16).reshape(parts, deep, wide)

    @pl.when(step == pl.num_programs(0) - 1)
    def _():
        layer = (hidden_ref[...] + out_acc[...]).astype(BF16)
        for i in range(blocks):
            layer_ref[i] = layer[:, i * width : (i + 1) * width]
        values = hidden_ref[...].astype(BF16).astype(F32)
        scale = inverse_rms(values)
        normal = values * scale
        grad = normed_acc[...]
        gain_grad_ref[...] = jnp.sum(grad * normal, axis=0, keepdims=True)
        scaled = grad * gain_ref[...]
        back = scale * (scaled - normal * jnp.mean(scaled * normal, axis=-1, keepdims=True))
        grad_ref[...] = cot_scratch[...].astype(F32) + back


def feed_forward(hidden, cot, gain, weights):
    rows = hidden.shape[0]
    blocks, _, width = cot.shape
    parts, tps, depth, total = weights.shape
    deep = D // parts
    wide = HIDDEN
    count = total // wide
    held = wide // deep
    return pl.pallas_call(
        feed_forward_kernel,
        grid=(tps * count,),
        in_specs=[
            whole((rows, D)),
            whole((blocks, rows, width)),
            whole((1, D)),
            pl.BlockSpec((parts, 1, 2 * deep, wide), lambda j: (0, j // count, 0, j % count)),
            pl.BlockSpec((held, 1, deep, D), lambda j: (j % count, j // count, 2, 0)),
        ],
        out_specs=[
            whole((blocks, rows, width)),
            whole((rows, D)),
            whole((1, D)),
            pl.BlockSpec((parts, 1, 2 * deep, wide), lambda j: (0, j // count, 0, j % count)),
            pl.BlockSpec((held, 1, deep, D), lambda j: (j % count, j // count, 0, 0)),
        ],
        out_shape=[
            jax.ShapeDtypeStruct((blocks, rows, width), BF16),
            jax.ShapeDtypeStruct((rows, D), F32),
            jax.ShapeDtypeStruct((1, D), F32),
            jax.ShapeDtypeStruct((parts, tps, 2 * deep, total), BF16),
            jax.ShapeDtypeStruct((parts, tps, deep, D), BF16),
        ],
        scratch_shapes=[
            pltpu.VMEM((rows, D), BF16),
            pltpu.VMEM((D, rows), BF16),
            pltpu.VMEM((rows, D), BF16),
            pltpu.VMEM((rows, D), F32),
            pltpu.VMEM((rows, D), F32),
        ],
        compiler_params=params(),
        name="feed_forward",
        cost_estimate=pl.CostEstimate(
            flops=18 * rows * D * total * tps, bytes_accessed=56 << 20, transcendentals=rows * total * tps
        ),
    )(hidden, cot, gain, weights, weights)


def attention_backward_kernel(
    grad_ref,
    mixer_ref,
    input_ref,
    normed_ref,
    gain_ref,
    weight_ref,
    qkv_ref,
    context_ref,
    embed_ref,
    global_ref,
    dot_ref,
    gain_grad_ref,
    weight_grad_ref,
    turned_ref,
    low_ref,
    normed_acc,
    context_grad_ref,
    qkv_grad_ref,
):
    step = pl.program_id(0)
    rows = grad_ref.shape[0]
    blocks, _, width = embed_ref.shape
    parts = weight_ref.shape[0]
    deep = D // parts
    scaling = (D // HEADS_A) ** -0.5

    @pl.when(step == 0)
    def _():
        turned_ref[...] = normed_ref[...].astype(F32).T.astype(BF16)
        low_ref[...] = grad_ref[...].astype(BF16)
        normed_acc[...] = jnp.zeros_like(normed_acc)

    low = low_ref[...]
    context = context_ref[0]
    piece = width // parts
    total = jnp.zeros((rows, width), F32)
    for c in range(D // width):
        first = 3 * deep + c * piece
        weight = weight_ref[:, 0, first : first + piece, :].reshape(width, width)
        columns = low[:, c * width : (c + 1) * width]
        total = total + mm_nt(columns, weight)
        grad = mm_tn(context, columns).astype(BF16)
        weight_grad_ref[:, 0, first : first + piece, :] = grad.reshape(parts, piece, width)
    context_grad_ref[...] = total.astype(BF16)
    masks = head_mask(width)
    heads = len(masks)
    keep = tile_mask(heads)
    for r in range(rows // TILE):
        at = slice(r * TILE, (r + 1) * TILE)
        query = split_heads(qkv_ref[0, 0, at], masks)
        keys = qkv_ref[0, 1, at]
        probs = tile_probs(query, keys, keep)
        dcontext = split_heads(context_grad_ref[at], masks)
        dprobs = mm_nt(dcontext, qkv_ref[0, 2, at])
        dvalues = mm_tn(probs.astype(BF16), dcontext)
        inner = jnp.sum(dprobs * probs, axis=-1, keepdims=True)
        dscores = (probs * (dprobs - inner)).astype(BF16)
        dquery = mm(beside(dscores, heads), split_heads(keys, masks)) * scaling
        dkeys = mm_tn(dscores, query) * scaling
        qkv_grad_ref[at, :width] = dquery.astype(BF16)
        qkv_grad_ref[at, width : 2 * width] = dkeys.astype(BF16)
        qkv_grad_ref[at, 2 * width :] = dvalues.astype(BF16)
    turned = turned_ref[...]
    for k in range(3):
        part = qkv_grad_ref[:, k * width : (k + 1) * width]
        weight = weight_ref[:, 0, k * deep : (k + 1) * deep, :].reshape(D, width)
        normed_acc[...] += mm_nt(part, weight)
        grad = mm(turned, part).astype(BF16)
        weight_grad_ref[:, 0, k * deep : (k + 1) * deep, :] = grad.reshape(parts, deep, width)

    @pl.when(step == pl.num_programs(0) - 1)
    def _():
        values = input_ref[...].astype(F32)
        scale = inverse_rms(values)
        normal = values * scale
        grad = normed_acc[...]
        gain_grad_ref[...] = jnp.sum(grad * normal, axis=0, keepdims=True)
        scaled = grad * gain_ref[...]
        back = scale * (scaled - normal * jnp.mean(scaled * normal, axis=-1, keepdims=True))
        result = grad_ref[...] + back
        for i in range(blocks):
            embed_ref[i] = result[:, i * width : (i + 1) * width].astype(BF16)
        patch = jnp.sum(result.reshape(rows // PATCH, PATCH, D), axis=1)
        global_ref[...] = patch
        dot_ref[...] = jnp.sum(patch * mixer_ref[...], axis=1, keepdims=True)


def attention_backward(grad, mixer_rows, inputs, normed, gain, weights, qkv, context):
    rows = grad.shape[0]
    parts, tps, depth, width = weights.shape
    return pl.pallas_call(
        attention_backward_kernel,
        grid=(tps,),
        in_specs=[
            whole((rows, D)),
            whole((rows // PATCH, D)),
            whole((rows, D)),
            whole((rows, D)),
            whole((1, D)),
            pl.BlockSpec((parts, 1, depth, width), lambda j: (0, j, 0, 0)),
            pl.BlockSpec((1, 3, rows, width), lambda j: (j, 0, 0, 0)),
            pl.BlockSpec((1, rows, width), lambda j: (j, 0, 0)),
        ],
        out_specs=[
            whole((tps, rows, width)),
            whole((rows // PATCH, D)),
            whole((rows // PATCH, 1)),
            whole((1, D)),
            pl.BlockSpec((parts, 1, depth, width), lambda j: (0, j, 0, 0)),
        ],
        out_shape=[
            jax.ShapeDtypeStruct((tps, rows, width), BF16),
            jax.ShapeDtypeStruct((rows // PATCH, D), F32),
            jax.ShapeDtypeStruct((rows // PATCH, 1), F32),
            jax.ShapeDtypeStruct((1, D), F32),
            jax.ShapeDtypeStruct((parts, tps, depth, width), BF16),
        ],
        scratch_shapes=[
            pltpu.VMEM((D, rows), BF16),
            pltpu.VMEM((rows, D), BF16),
            pltpu.VMEM((rows, D), F32),
            pltpu.VMEM((rows, width), BF16),
            pltpu.VMEM((rows, 3 * width), BF16),
        ],
        compiler_params=params(),
        name="attention_backward",
        cost_estimate=pl.CostEstimate(
            flops=4 * rows * D * D * 4, bytes_accessed=26 << 20, transcendentals=rows * 2048
        ),
    )(grad, mixer_rows, inputs, normed, gain, weights, qkv, context)


def shifted(block, distance):
    devices = range(lax.axis_size(SEQ))
    route = [(i - distance, i) for i in devices if i - distance in devices]
    return lax.ppermute(block, SEQ, route)


def rms_scale(values):
    return values * inverse_rms(values)


def sequence_first(positions, lengths):
    offsets = jnp.cumsum(lengths) - lengths
    chosen = jnp.where(offsets[None, :] <= positions[:, None], offsets[None, :], 0)
    return jnp.max(chosen, axis=1)


def causal_conv(padded, weight, positions, first):
    count = positions.shape[0]
    total = jnp.zeros((count, padded.shape[1]), jnp.float32)
    for offset in range(CONV):
        lag = CONV - 1 - offset
        keep = (positions - lag >= first).astype(jnp.float32)[:, None]
        total = total + weight[offset][None, :] * padded[offset : offset + count] * keep
    return total


def front_part(padded, step_raw, conv_weight, step_bias, decay_log, positions, first):
    activated = jax.nn.silu(causal_conv(padded, conv_weight, positions, first))
    inner = activated.shape[1] - 2 * STATE
    count = positions.shape[0]
    inner_vals = activated[:, :inner].reshape(count, inner // HEAD_DIM, HEAD_DIM)
    bmatrix = activated[:, inner : inner + STATE]
    cmatrix = activated[:, inner + STATE :]
    steps = jax.nn.softplus(step_raw + step_bias[None, :])
    rates = -jnp.exp(decay_log)
    return (inner_vals, bmatrix, cmatrix, steps, rates)


def block_summary(inner_vals, bmatrix, steps, rates, positions, first):
    logs = jnp.cumsum(steps * rates[None, :], axis=0)
    final = logs[-1]
    in_last = (first == first[-1]).astype(jnp.float32)[:, None]
    weights = jnp.exp(final[None, :] - logs) * in_last * steps
    carried = jnp.exp(final) * (first[-1] < positions[0]).astype(jnp.float32)
    states = jnp.einsum("sh,shp,sn->hpn", weights, inner_vals, bmatrix, precision=highest)
    return (carried, states)


def block_output(inner_vals, bmatrix, cmatrix, steps, rates, skip_gain, incoming, positions, first):
    logs = jnp.cumsum(steps * rates[None, :], axis=0)
    count = positions.shape[0]
    same = (first[:, None] == first[None, :]) & (positions[None, :] <= positions[:, None])
    diff = logs.T[:, :, None] - logs.T[:, None, :]
    decay = jnp.where(same[None], jnp.exp(jnp.where(same[None], diff, 0.0)), 0.0)
    inner_prod = jnp.dot(cmatrix, bmatrix.T, precision=highest, preferred_element_type=jnp.float32)
    mixing = decay * inner_prod[None] * steps.T[:, None, :]
    within = jnp.einsum("hts,shp->thp", mixing, inner_vals, precision=highest)
    carry = jnp.exp(logs) * (first < positions[0]).astype(jnp.float32)[:, None]
    remote = jnp.einsum("tn,hpn->thp", cmatrix, incoming, precision=highest) * carry[:, :, None]
    result = within + remote + skip_gain[None, :, None] * inner_vals
    return result.reshape(count, -1)


def product(left, right, form):
    return jnp.einsum(form, left, right, preferred_element_type=jnp.float32)


def norm_backward(grad, values, gain):
    scale = inverse_rms(values)
    normed = values * scale
    scaled = grad * gain[None, :]
    result = scale * (scaled - normed * jnp.mean(scaled * normed, axis=-1, keepdims=True))
    return (result, jnp.sum(grad * normed, axis=0))


def chained(factors, states, here, reverse):
    count = factors.shape[0]
    order = jnp.arange(count)
    source, between = order[:, None], order[None, :]
    if reverse:
        crossed = (between > here) & (between < source)
        reaching = order > here
    else:
        crossed = (between < here) & (between > source)
        reaching = order < here
    chain = jnp.prod(jnp.where(crossed[:, :, None], factors[None], 1.0), axis=1)
    chain = chain * reaching[:, None].astype(F32)
    return jnp.sum(chain[:, :, None, None] * states, axis=0)


def spread_shard(array):
    size = array.shape[0] // GROUP
    return lax.dynamic_slice_in_dim(array, lax.axis_index("s") * size, size, 0)


def reduce_pieces(grads):
    own = lax.psum_scatter(grads, "s", scatter_dimension=0)
    own = lax.psum_scatter(own, "tp", scatter_dimension=0)
    if lax.axis_size("g") > 1:
        own = lax.psum(own, "g")
    return lax.all_gather(own, "s")


def shards(
    patches,
    byte_embed,
    seq_lengths,
    norm_global,
    proj_gate,
    proj_inner,
    proj_state,
    proj_step,
    step_bias,
    decay_log,
    conv_inner,
    conv_state,
    skip_gain,
    mixer_gain,
    proj_mixer,
    norm_attn,
    attn_input,
    attn_output,
    norm_ffn,
    expand_weight,
    shrink_weight,
    grad_output,
):
    count, quarter = patches.shape
    tps = lax.axis_size("tp")
    mine = lax.axis_index("tp")
    here = lax.axis_index("g") * lax.axis_size("s") + lax.axis_index("s")
    tail = CONV - 1
    inner_width = proj_inner.shape[1]
    share = count // tps
    total_rows = byte_embed.shape[0]
    rows = total_rows // tps

    narrow = D // GROUP
    slot = lax.axis_index("s")
    attn_in_part = lax.dynamic_slice_in_dim(attn_input, slot * narrow, narrow, 1)
    attn_out_part = spread_shard(attn_output)
    attn_out_part = attn_out_part.reshape(-1, tps, quarter).transpose(1, 0, 2)
    attn_part = jnp.concatenate(
        [attn_in_part.reshape(-1, quarter), attn_out_part.reshape(-1, quarter)], axis=0
    )
    attn_weights = lax.all_gather(attn_part, ("s", "tp")).reshape(GROUP, tps, -1, quarter)
    hidden_width = expand_weight.shape[2]
    expand_part = lax.dynamic_slice_in_dim(expand_weight, slot * narrow, narrow, 1)
    ffn_part = jnp.concatenate(
        [expand_part.reshape(-1, hidden_width), spread_shard(shrink_weight)], axis=0
    )
    ffn_weights = lax.all_gather(ffn_part, ("s", "tp")).reshape(GROUP, tps, -1, hidden_width)

    def to_rows(array):
        return lax.all_to_all(array.reshape(tps, rows, quarter), "tp", 0, 0)

    def to_columns(blocks):
        return lax.all_to_all(blocks, "tp", 0, 0).reshape(total_rows, quarter)

    positions = here * count + jnp.arange(count, dtype=jnp.int32)
    first = sequence_first(positions, seq_lengths)
    patch_rows = lax.all_gather(patches, "tp", axis=1, tiled=True)
    embed_rows = to_rows(byte_embed)
    cot_rows = to_rows(grad_output)
    global_in = patch_rows.astype(jnp.float32)
    normed = (rms_scale(global_in) * norm_global[None, :]).astype(jnp.bfloat16)
    gate_vals = product(normed, proj_gate, "rd,dc->rc")
    inner_raw = product(normed, proj_inner, "rd,dc->rc")
    state_raw = product(normed, proj_state, "rd,dc->rc")
    step_raw = product(normed, proj_step, "rd,dc->rc")
    raw = jnp.concatenate([inner_raw, state_raw], axis=1)
    before = shifted(raw[count - tail :], 1)
    padded = jnp.concatenate([before, raw], axis=0)
    conv_weight = jnp.concatenate([conv_inner, conv_state], axis=1)

    def front_local(padded_in, step_in, conv_in, bias_in, decay_in):
        return front_part(padded_in, step_in, conv_in, bias_in, decay_in, positions, first)

    def summary_local(inner_in, bmat_in, steps_in, rates_in):
        return block_summary(inner_in, bmat_in, steps_in, rates_in, positions, first)

    def output_local(inner_in, bmat_in, cmat_in, steps_in, rates_in, skip_in, incoming_in):
        return block_output(
            inner_in, bmat_in, cmat_in, steps_in, rates_in, skip_in, incoming_in, positions, first
        )

    front_vals, front_pull = jax.vjp(
        front_local, padded, step_raw, conv_weight, step_bias, decay_log
    )
    inner_vals, bmatrix, cmatrix, steps, rates = front_vals
    summary, summary_pull = jax.vjp(summary_local, inner_vals, bmatrix, steps, rates)
    carried, states = summary
    all_carried = lax.all_gather(carried, SEQ)
    incoming = chained(all_carried, lax.all_gather(states, SEQ), here, False)
    mixed, output_pull = jax.vjp(
        output_local, inner_vals, bmatrix, cmatrix, steps, rates, skip_gain, incoming
    )
    gate_act = jax.nn.silu(gate_vals)
    gated = mixed * gate_act
    squares = jnp.sum(gated * gated, axis=1, keepdims=True)
    partial = product((gated * mixer_gain[None, :]).astype(BF16), proj_mixer, "rc,cd->rd")
    summed = lax.psum_scatter(
        jnp.concatenate([partial, jnp.broadcast_to(squares, (count, 128))], axis=1),
        "tp",
        scatter_dimension=0,
        tiled=True,
    )
    own_squares = summed[:, D : D + 1]
    mixer_rows = summed[:, :D] * lax.rsqrt(own_squares / DI + epsilon)
    own_patches = lax.dynamic_slice_in_dim(patch_rows, mine * share, share, 0)
    global_out = own_patches.astype(F32) + mixer_rows

    hidden, attn_in, attn_normed, qkv, context = attention_forward(
        embed_rows, global_out[:, None, :], norm_attn[None, :], attn_weights
    )
    layer_blocks, hidden_grad, norm_ffn_part, expand_part, shrink_part = feed_forward(
        hidden, cot_rows, norm_ffn[None, :], ffn_weights
    )
    layer_output = to_columns(layer_blocks)
    embed_blocks, own_grad, row_dot, norm_attn_part, attn_part = attention_backward(
        hidden_grad, mixer_rows, attn_in, attn_normed, norm_attn[None, :], attn_weights, qkv, context
    )
    shrink_grad = reduce_pieces(shrink_part).reshape(-1, D).astype(F32)
    expand_grad = reduce_pieces(expand_part).reshape(GROUP, 2, narrow, hidden_width)
    expand_grad = expand_grad.transpose(1, 0, 2, 3).reshape(2, D, hidden_width).astype(F32)
    attn_grad = reduce_pieces(attn_part)
    attn_input_grad = attn_grad[:, : 3 * narrow].reshape(GROUP, 3, narrow, quarter)
    attn_input_grad = attn_input_grad.transpose(1, 0, 2, 3).reshape(3, D, quarter).astype(F32)
    attn_output_grad = attn_grad[:, 3 * narrow :].reshape(GROUP, tps, -1, quarter)
    attn_output_grad = attn_output_grad.transpose(0, 2, 1, 3).reshape(quarter, D).astype(F32)
    embed_grad = to_columns(embed_blocks).astype(F32)

    extras = jnp.concatenate([own_squares, row_dot], axis=1)
    mix_back_in = lax.all_gather(own_grad.astype(BF16), "tp", axis=0, tiled=True)
    all_extras = lax.all_gather(extras, "tp", axis=0, tiled=True)
    row_scale = lax.rsqrt(all_extras[:, :1] / DI + epsilon)
    row_mean = all_extras[:, 1:] / DI
    normed_mix = gated * row_scale
    mix_low = (normed_mix * mixer_gain[None, :]).astype(jnp.bfloat16)
    proj_mixer_grad = product(mix_low, mix_back_in, "rc,rd->cd")
    mix_low_grad = product(mix_back_in, proj_mixer, "rd,cd->rc")
    mixer_gain_grad = jnp.sum(mix_low_grad * normed_mix, axis=0)
    scaled_grad = mix_low_grad * mixer_gain[None, :]
    gated_grad = row_scale * (scaled_grad - normed_mix * row_mean)
    mixed_grad = gated_grad * gate_act
    sigma_gate = jax.nn.sigmoid(gate_vals)
    gate_vals_grad = gated_grad * mixed * sigma_gate * (1.0 + gate_vals * (1.0 - sigma_gate))
    inner_one, bmat_one, cmat_one, steps_one, rates_one, skip_gain_grad, incoming_grad = (
        output_pull(mixed_grad)
    )
    later_grad = chained(all_carried, lax.all_gather(incoming_grad, SEQ), here, True)
    carried_grad = jnp.sum(later_grad * incoming, axis=(1, 2))
    inner_two, bmat_two, steps_two, rates_two = summary_pull((carried_grad, later_grad))
    padded_grad, step_raw_grad, conv_grad, step_bias_grad, decay_log_grad = front_pull(
        (
            inner_one + inner_two,
            bmat_one + bmat_two,
            cmat_one,
            steps_one + steps_two,
            rates_one + rates_two,
        )
    )
    tail_grad = shifted(padded_grad[:tail], -1)
    raw_grad = padded_grad[tail:]
    raw_grad = jnp.concatenate(
        [raw_grad[: count - tail], raw_grad[count - tail :] + tail_grad], axis=0
    )
    gate_back = gate_vals_grad.astype(jnp.bfloat16)
    inner_back = raw_grad[:, :inner_width].astype(jnp.bfloat16)
    state_back = raw_grad[:, inner_width:].astype(jnp.bfloat16)
    step_back = step_raw_grad.astype(jnp.bfloat16)
    normed_grad_part = (
        product(gate_back, proj_gate, "rc,dc->rd")
        + product(inner_back, proj_inner, "rc,dc->rd")
        + product(step_back, proj_step, "rc,dc->rd")
        + product(state_back, proj_state, "rs,ds->rd")
    )
    part_in_grad, norm_global_part = norm_backward(normed_grad_part, global_in, norm_global)
    part_in_grad = lax.dynamic_update_slice_in_dim(
        part_in_grad,
        lax.dynamic_slice_in_dim(part_in_grad, mine * share, share, 0) + own_grad,
        mine * share,
        0,
    )
    patch_grad = lax.psum_scatter(part_in_grad, "tp", scatter_dimension=1, tiled=True)
    state_all = lax.all_gather(state_back, "tp")
    state_sum = jnp.sum(state_all.astype(F32), axis=0).astype(BF16)
    shared = lax.psum(
        (
            conv_grad[:, inner_width:],
            norm_attn_part[0],
            norm_ffn_part[0],
            norm_global_part,
        ),
        "tp",
    )
    proj_grads = lax.psum(
        (
            product(normed, gate_back, "rd,rc->dc").astype(BF16),
            product(normed, inner_back, "rd,rc->dc").astype(BF16),
            product(normed, state_sum, "rd,rc->dc").astype(BF16),
            proj_mixer_grad.astype(BF16),
        ),
        SEQ,
    )
    proj_gate_grad, proj_inner_grad, proj_state_grad, proj_mixer_grad = (
        g.astype(F32) for g in proj_grads
    )
    (
        conv_state_grad,
        norm_attn_grad,
        norm_ffn_grad,
        norm_global_grad,
        proj_step_grad,
        step_bias_grad,
        decay_log_grad,
        conv_inner_grad,
        skip_gain_grad,
        mixer_gain_grad,
    ) = lax.psum(
        shared
        + (
            product(normed, step_back, "rd,rc->dc"),
            step_bias_grad,
            decay_log_grad,
            conv_grad[:, :inner_width],
            skip_gain_grad,
            mixer_gain_grad,
        ),
        SEQ,
    )
    return (
        layer_output,
        embed_grad,
        patch_grad,
        norm_global_grad,
        proj_gate_grad,
        proj_inner_grad,
        proj_state_grad,
        proj_step_grad,
        step_bias_grad,
        decay_log_grad,
        conv_inner_grad,
        conv_state_grad,
        skip_gain_grad,
        mixer_gain_grad,
        proj_mixer_grad,
        norm_attn_grad,
        attn_input_grad,
        attn_output_grad,
        norm_ffn_grad,
        expand_grad,
        shrink_grad,
    )


def solution(mesh):
    seq, tps = mesh.shape["seq"], mesh.shape["tp"]
    fine = Mesh(mesh.devices.reshape(seq // GROUP, GROUP, tps), ("g", "s", "tp"))
    rows_cols = P(SEQ, "tp")
    last = P(None, "tp")
    lead = P("tp", None)
    return jax.shard_map(
        shards,
        mesh=fine,
        in_specs=(
            rows_cols,
            rows_cols,
            P(),
            P(),
            last,
            last,
            P(),
            last,
            P("tp"),
            P("tp"),
            last,
            P(),
            P("tp"),
            P("tp"),
            lead,
            P(),
            P(None, None, "tp"),
            lead,
            P(),
            P(None, None, "tp"),
            lead,
            rows_cols,
        ),
        out_specs=(
            rows_cols,
            rows_cols,
            rows_cols,
            P(),
            last,
            last,
            P(),
            last,
            P("tp"),
            P("tp"),
            last,
            P(),
            P("tp"),
            P("tp"),
            lead,
            P(),
            P(None, None, "tp"),
            lead,
            P(),
            P(None, None, "tp"),
            lead,
        ),
        check_vma=False,
    )
```

```python
import functools

import jax
import jax.numpy as jnp
from jax import lax
from jax.experimental import pallas as pl
from jax.experimental.pallas import tpu as pltpu
from jax.sharding import Mesh, PartitionSpec as P

D = 1024
HEAD_DIM = 64
STATE = 128
HEADS_A = 16
CONV = 4
PATCH = 8
DI = 2048
GROUP = 8
TILE = 128
PIECES = 2

epsilon = 1e-05
highest = lax.Precision.HIGHEST
F32 = jnp.float32
BF16 = jnp.bfloat16
SEQ = ("g", "a", "b", "c")
INNER = ("a", "b", "c")


def mm(left, right):
    return lax.dot_general(left, right, (((1,), (0,)), ((), ())), preferred_element_type=F32)


def mm_nt(left, right):
    return lax.dot_general(left, right, (((1,), (1,)), ((), ())), preferred_element_type=F32)


def mm_tn(left, right):
    return lax.dot_general(left, right, (((0,), (0,)), ((), ())), preferred_element_type=F32)


def inverse_rms(values):
    return lax.rsqrt(jnp.mean(values * values, axis=-1, keepdims=True) + epsilon)


def params(limit=60):
    return pltpu.CompilerParams(
        dimension_semantics=("arbitrary",), vmem_limit_bytes=limit * 1024 * 1024
    )


def whole(shape):
    return pl.BlockSpec(shape, lambda j: (0,) * len(shape))


def scalar_spec():
    return pl.BlockSpec(memory_space=pltpu.SMEM)


def halves_shape(tps, depth, wide):
    return jax.ShapeDtypeStruct((2, 2, tps, depth, wide), BF16)


def halves_spec(depth, wide):
    return pl.BlockSpec((2, 2, 1, depth, wide), lambda j: (0, 0, j, 0, 0))


def anywhere():
    return pl.BlockSpec(memory_space=pl.ANY)


def weight_specs(weights, first):
    parts, _, _, wide = weights.shape
    block = (parts, 1, D // GROUP, wide)
    return [
        pl.BlockSpec(block, functools.partial(lambda k, j: (0, j, k, 0), first + k))
        for k in range(3)
    ]


def attention_spec(weights):
    parts, _, _, wide = weights.shape
    return pl.BlockSpec((parts, 1, 2 * D // GROUP, wide), lambda j: (0, j, 0, 0))


def attention_view(weight_ref, k, width):
    deep = D // weight_ref.shape[0]
    rows = slice((k % 2) * deep, (k % 2 + 1) * deep)
    return weight_ref.at[:, 0, rows, (k // 2) * width : (k // 2 + 1) * width]


def head_mask(width):
    lane = lax.broadcasted_iota(jnp.int32, (1, width), 1) // (D // HEADS_A)
    return [lane == h for h in range(width // (D // HEADS_A))]


def split_heads(tile, masks):
    zero = jnp.zeros_like(tile)
    return jnp.concatenate([jnp.where(m, tile, zero) for m in masks], axis=0)


def tile_mask(heads):
    row = lax.broadcasted_iota(jnp.int32, (heads * TILE, TILE), 0) % TILE
    col = lax.broadcasted_iota(jnp.int32, (heads * TILE, TILE), 1)
    return (row // PATCH == col // PATCH) & (col <= row)


def tile_probs(query_split, keys, keep):
    scores = mm_nt(query_split, keys) * ((D // HEADS_A) ** -0.5)
    scores = jnp.where(keep, scores, -1e30)
    expo = jnp.exp(scores - jnp.max(scores, axis=-1, keepdims=True))
    return expo / jnp.sum(expo, axis=-1, keepdims=True)


def beside(stacked, heads):
    return jnp.concatenate([stacked[h * TILE : (h + 1) * TILE] for h in range(heads)], axis=1)


def attention_forward_kernel(
    embed_ref, global_ref, gain_ref, weight_ref, hidden_ref, input_ref, normed_ref, qkv_ref, context_ref
):
    step = pl.program_id(0)
    blocks, rows, width = embed_ref.shape
    parts = weight_ref.shape[0]

    @pl.when(step == 0)
    def _():
        embed = jnp.concatenate([embed_ref[i] for i in range(blocks)], axis=1).astype(F32)
        spread = jnp.broadcast_to(global_ref[...], (rows // PATCH, PATCH, D)).reshape(rows, D)
        total = embed + spread
        hidden_ref[...] = total
        low = total.astype(BF16)
        input_ref[...] = low
        values = low.astype(F32)
        normed_ref[...] = (values * inverse_rms(values) * gain_ref[...]).astype(BF16)

    normed = normed_ref[...]
    for k in range(3):
        weight = attention_view(weight_ref, k, width)[...].reshape(D, width)
        qkv_ref[0, k] = mm(normed, weight).astype(BF16)
    masks = head_mask(width)
    heads = len(masks)
    keep = tile_mask(heads)
    for r in range(rows // TILE):
        at = slice(r * TILE, (r + 1) * TILE)
        query = split_heads(qkv_ref[0, 0, at], masks)
        probs = tile_probs(query, qkv_ref[0, 1, at], keep).astype(BF16)
        values = split_heads(qkv_ref[0, 2, at], masks)
        context_ref[0, at] = mm(beside(probs, heads), values).astype(BF16)
    context = context_ref[0]
    piece = width // parts
    outward = attention_view(weight_ref, 3, width)
    for c in range(D // width):
        weight = outward[:, c * piece : (c + 1) * piece].reshape(width, width)
        cols = slice(c * width, (c + 1) * width)
        hidden_ref[:, cols] += mm(context, weight)


def attention_forward(embed, global_rows, gain, weights):
    blocks, rows, width = embed.shape
    tps = weights.shape[1]
    return pl.pallas_call(
        attention_forward_kernel,
        grid=(tps,),
        in_specs=[
            whole((blocks, rows, width)),
            whole((rows // PATCH, 1, D)),
            whole((1, D)),
            attention_spec(weights),
        ],
        out_specs=[
            whole((rows, D)),
            whole((rows, D)),
            whole((rows, D)),
            pl.BlockSpec((1, 3, rows, width), lambda j: (j, 0, 0, 0)),
            pl.BlockSpec((1, rows, width), lambda j: (j, 0, 0)),
        ],
        out_shape=[
            jax.ShapeDtypeStruct((rows, D), F32),
            jax.ShapeDtypeStruct((rows, D), BF16),
            jax.ShapeDtypeStruct((rows, D), BF16),
            jax.ShapeDtypeStruct((tps, 3, rows, width), BF16),
            jax.ShapeDtypeStruct((tps, rows, width), BF16),
        ],
        compiler_params=params(),
        name="attention_forward",
        cost_estimate=pl.CostEstimate(
            flops=2 * rows * D * D * 4, bytes_accessed=14 << 20, transcendentals=rows * 2048
        ),
    )(embed, global_rows, gain, weights)


def core_halves(core, grad):
    parts = grad.reshape((2, 2, 2, grad.shape[0] // GROUP) + grad.shape[1:])
    mine = jnp.where(core == 0, parts[:, :, 0], parts[:, :, 1])
    other = jnp.where(core == 0, parts[:, :, 1], parts[:, :, 0])
    return mine, other


def put_halves(core, grad, own_ref, other_ref, low, high, cols=slice(None)):
    own, other = core_halves(core, grad.astype(BF16))
    own_ref[:, :, 0, low:high, cols] = own
    other_ref[:, :, 0, low:high, cols] = other


def put_whole(core, grad, grad_ref, low, high):
    parts = grad_ref.shape[0]
    grad_ref[:, 0, low:high] = grad.astype(BF16).reshape((parts, -1) + grad.shape[1:])


def feed_forward_step(
    core_ref, weight_refs, cot, normed_ref, turned_ref, out_acc, normed_acc, put
):
    parts, _, _, wide = weight_refs[0].shape
    deep = D // parts
    core = core_ref[0]
    normed = normed_ref[...]
    gate_weight = weight_refs[0][:, 0].reshape(D, wide)
    up_weight = weight_refs[1][:, 0].reshape(D, wide)
    piece = wide // parts
    folds = D // wide
    down_weight = jnp.concatenate(
        [
            weight_refs[2][:, 0, i * piece : (i + 1) * piece].reshape(wide, wide)
            for i in range(folds)
        ],
        axis=1,
    )
    gate = mm(normed, gate_weight)
    up = mm(normed, up_weight)
    sigma = 1.0 / (1.0 + jnp.exp(-gate))
    swish = gate * sigma
    activ = (swish * up).astype(BF16)
    out_acc[...] += mm(activ, down_weight)
    shrink = mm_tn(activ, cot)
    for i in range(folds):
        low = 2 * deep + i * piece
        put(core, shrink[:, i * wide : (i + 1) * wide], low, low + piece)
    dactiv = mm_nt(cot, down_weight)
    dgate = (dactiv * up * sigma * (1.0 + gate * (1.0 - sigma))).astype(BF16)
    dup = (dactiv * swish).astype(BF16)
    normed_acc[...] += mm_nt(dgate, gate_weight) + mm_nt(dup, up_weight)
    turned = turned_ref[...]
    put(core, mm(turned, dgate), 0, deep)
    put(core, mm(turned, dup), deep, 2 * deep)


def feed_forward_first_kernel(
    core_ref,
    hidden_ref,
    cot_ref,
    gain_ref,
    gate_ref,
    up_ref,
    down_ref,
    normed_ref,
    turned_ref,
    cot_out,
    out_acc,
    normed_acc,
    own_ref,
    other_ref,
):
    blocks, _, width = cot_ref.shape

    @pl.when(pl.program_id(0) == 0)
    def _():
        values = hidden_ref[...].astype(BF16).astype(F32)
        normed = (values * inverse_rms(values) * gain_ref[...]).astype(BF16)
        normed_ref[...] = normed
        turned_ref[...] = normed.astype(F32).T.astype(BF16)
        for i in range(blocks):
            cot_out[:, i * width : (i + 1) * width] = cot_ref[i]
        out_acc[...] = hidden_ref[...]
        normed_acc[...] = jnp.zeros_like(normed_acc)

    def put(core, grad, low, high):
        put_halves(core, grad, own_ref, other_ref, low, high)

    feed_forward_step(
        core_ref,
        (gate_ref, up_ref, down_ref),
        cot_out[...],
        normed_ref,
        turned_ref,
        out_acc,
        normed_acc,
        put,
    )


def feed_forward_last_kernel(
    core_ref,
    hidden_ref,
    cot_ref,
    gain_ref,
    gate_ref,
    up_ref,
    down_ref,
    normed_ref,
    turned_ref,
    out_in,
    normed_in,
    token_ref,
    layer_ref,
    grad_ref,
    gain_grad_ref,
    weight_grad_ref,
    out_acc,
    normed_acc,
):
    step = pl.program_id(0)
    blocks, _, width = layer_ref.shape

    @pl.when(step == 0)
    def _():
        out_acc[...] = out_in[...]
        normed_acc[...] = normed_in[...]

    def put(core, grad, low, high):
        put_whole(core, grad, weight_grad_ref, low, high)

    feed_forward_step(
        core_ref,
        (gate_ref, up_ref, down_ref),
        cot_ref[...],
        normed_ref,
        turned_ref,
        out_acc,
        normed_acc,
        put,
    )

    @pl.when(step == pl.num_programs(0) - 1)
    def _():
        layer = out_acc[...].astype(BF16)
        for i in range(blocks):
            layer_ref[i] = layer[:, i * width : (i + 1) * width]
        values = hidden_ref[...].astype(BF16).astype(F32)
        scale = inverse_rms(values)
        normal = values * scale
        grad = normed_acc[...]
        gain_grad_ref[...] = jnp.sum(grad * normal, axis=0, keepdims=True)
        scaled = grad * gain_ref[...]
        back = scale * (scaled - normal * jnp.mean(scaled * normal, axis=-1, keepdims=True))
        grad_ref[...] = cot_ref[...].astype(F32) + back


def feed_forward_cost(rows, weights):
    _, tps, _, wide = weights.shape
    return pl.CostEstimate(
        flops=18 * rows * D * wide * tps,
        bytes_accessed=12 * D * wide * tps + 16 * rows * D,
        transcendentals=rows * wide * tps,
    )


def feed_forward_first(core, hidden, cot, gain, weights):
    rows = hidden.shape[0]
    _, tps, _, wide = weights.shape
    depth = 3 * D // GROUP
    return pl.pallas_call(
        feed_forward_first_kernel,
        grid=(tps,),
        in_specs=[
            scalar_spec(),
            whole((rows, D)),
            whole(cot.shape),
            whole((1, D)),
            *weight_specs(weights, 2),
        ],
        out_specs=[
            whole((rows, D)),
            whole((D, rows)),
            whole((rows, D)),
            whole((rows, D)),
            whole((rows, D)),
            halves_spec(depth, wide),
            halves_spec(depth, wide),
        ],
        out_shape=[
            jax.ShapeDtypeStruct((rows, D), BF16),
            jax.ShapeDtypeStruct((D, rows), BF16),
            jax.ShapeDtypeStruct((rows, D), BF16),
            jax.ShapeDtypeStruct((rows, D), F32),
            jax.ShapeDtypeStruct((rows, D), F32),
            halves_shape(tps, depth, wide),
            halves_shape(tps, depth, wide),
        ],
        compiler_params=params(),
        name="feed_forward_first",
        cost_estimate=feed_forward_cost(rows, weights),
    )(core, hidden, cot, gain, weights, weights, weights)


def feed_forward_last(
    core, hidden, cot, gain, weights, normed, turned, out_in, normed_in, token
):
    rows = hidden.shape[0]
    _, tps, _, wide = weights.shape
    depth = 3 * D // GROUP
    width = D // tps
    return pl.pallas_call(
        feed_forward_last_kernel,
        grid=(tps,),
        in_specs=[
            scalar_spec(),
            whole((rows, D)),
            whole((rows, D)),
            whole((1, D)),
            *weight_specs(weights, 0),
            whole((rows, D)),
            whole((D, rows)),
            whole((rows, D)),
            whole((rows, D)),
            anywhere(),
        ],
        out_specs=[
            whole((tps, rows, width)),
            whole((rows, D)),
            whole((1, D)),
            pl.BlockSpec((GROUP, 1, depth, wide), lambda j: (0, j, 0, 0)),
        ],
        out_shape=[
            jax.ShapeDtypeStruct((tps, rows, width), BF16),
            jax.ShapeDtypeStruct((rows, D), F32),
            jax.ShapeDtypeStruct((1, D), F32),
            jax.ShapeDtypeStruct((GROUP, tps, depth, wide), BF16),
        ],
        scratch_shapes=[pltpu.VMEM((rows, D), F32), pltpu.VMEM((rows, D), F32)],
        compiler_params=params(),
        name="feed_forward_last",
        cost_estimate=feed_forward_cost(rows, weights),
    )(core, hidden, cot, gain, weights, weights, weights, normed, turned, out_in, normed_in, token)


def attention_backward_kernel(
    core_ref,
    grad_ref,
    mixer_ref,
    input_ref,
    normed_ref,
    gain_ref,
    weight_ref,
    qkv_ref,
    context_ref,
    token_ref,
    layer_token_ref,
    embed_ref,
    global_ref,
    dot_ref,
    gain_grad_ref,
    own_ref,
    other_ref,
    turned_ref,
    low_ref,
    normed_acc,
    context_grad_ref,
    qkv_grad_ref,
):
    step = pl.program_id(0)
    rows = grad_ref.shape[0]
    blocks, _, width = embed_ref.shape
    parts = weight_ref.shape[0]
    deep = D // parts
    scaling = (D // HEADS_A) ** -0.5
    core = core_ref[0]

    @pl.when(step == 0)
    def _():
        turned_ref[...] = normed_ref[...].astype(F32).T.astype(BF16)
        low_ref[...] = grad_ref[...].astype(BF16)
        normed_acc[...] = jnp.zeros_like(normed_acc)

    low = low_ref[...]
    context = context_ref[0]
    piece = width // parts
    total = jnp.zeros((rows, width), F32)
    outward = attention_view(weight_ref, 3, width)
    for c in range(D // width):
        first = deep + c * piece
        weight = outward[:, c * piece : (c + 1) * piece].reshape(width, width)
        columns = low[:, c * width : (c + 1) * width]
        total = total + mm_nt(columns, weight)
        put_halves(
            core,
            mm_tn(context, columns),
            own_ref,
            other_ref,
            first,
            first + piece,
            slice(width, 2 * width),
        )
    context_grad_ref[...] = total.astype(BF16)
    masks = head_mask(width)
    heads = len(masks)
    keep = tile_mask(heads)
    for r in range(rows // TILE):
        at = slice(r * TILE, (r + 1) * TILE)
        query = split_heads(qkv_ref[0, 0, at], masks)
        keys = qkv_ref[0, 1, at]
        probs = tile_probs(query, keys, keep)
        dcontext = split_heads(context_grad_ref[at], masks)
        dprobs = mm_nt(dcontext, qkv_ref[0, 2, at])
        dvalues = mm_tn(probs.astype(BF16), dcontext)
        inner = jnp.sum(dprobs * probs, axis=-1, keepdims=True)
        dscores = (probs * (dprobs - inner)).astype(BF16)
        dquery = mm(beside(dscores, heads), split_heads(keys, masks)) * scaling
        dkeys = mm_tn(dscores, query) * scaling
        qkv_grad_ref[at, :width] = dquery.astype(BF16)
        qkv_grad_ref[at, width : 2 * width] = dkeys.astype(BF16)
        qkv_grad_ref[at, 2 * width :] = dvalues.astype(BF16)
    turned = turned_ref[...]
    for k in range(3):
        part = qkv_grad_ref[:, k * width : (k + 1) * width]
        weight = attention_view(weight_ref, k, width)[...].reshape(D, width)
        normed_acc[...] += mm_nt(part, weight)
        first = (k % 2) * deep
        put_halves(
            core,
            mm(turned, part),
            own_ref,
            other_ref,
            first,
            first + deep,
            slice((k // 2) * width, (k // 2 + 1) * width),
        )

    @pl.when(step == pl.num_programs(0) - 1)
    def _():
        values = input_ref[...].astype(F32)
        scale = inverse_rms(values)
        normal = values * scale
        grad = normed_acc[...]
        gain_grad_ref[...] = jnp.sum(grad * normal, axis=0, keepdims=True)
        scaled = grad * gain_ref[...]
        back = scale * (scaled - normal * jnp.mean(scaled * normal, axis=-1, keepdims=True))
        result = grad_ref[...] + back
        for i in range(blocks):
            embed_ref[i] = result[:, i * width : (i + 1) * width].astype(BF16)
        patch = jnp.sum(result.reshape(rows // PATCH, PATCH, D), axis=1)
        global_ref[...] = patch
        dot_ref[...] = jnp.sum(patch * mixer_ref[...], axis=1, keepdims=True)


def attention_backward(core, grad, mixer_rows, inputs, normed, gain, weights, qkv, context, tokens):
    rows = grad.shape[0]
    tps, _, width = context.shape
    depth = 2 * D // GROUP
    return pl.pallas_call(
        attention_backward_kernel,
        grid=(tps,),
        in_specs=[
            scalar_spec(),
            whole((rows, D)),
            whole((rows // PATCH, D)),
            whole((rows, D)),
            whole((rows, D)),
            whole((1, D)),
            attention_spec(weights),
            pl.BlockSpec((1, 3, rows, width), lambda j: (j, 0, 0, 0)),
            pl.BlockSpec((1, rows, width), lambda j: (j, 0, 0)),
            anywhere(),
            anywhere(),
        ],
        out_specs=[
            whole((tps, rows, width)),
            whole((rows // PATCH, D)),
            whole((rows // PATCH, 1)),
            whole((1, D)),
            halves_spec(depth, 2 * width),
            halves_spec(depth, 2 * width),
        ],
        out_shape=[
            jax.ShapeDtypeStruct((tps, rows, width), BF16),
            jax.ShapeDtypeStruct((rows // PATCH, D), F32),
            jax.ShapeDtypeStruct((rows // PATCH, 1), F32),
            jax.ShapeDtypeStruct((1, D), F32),
            halves_shape(tps, depth, 2 * width),
            halves_shape(tps, depth, 2 * width),
        ],
        scratch_shapes=[
            pltpu.VMEM((D, rows), BF16),
            pltpu.VMEM((rows, D), BF16),
            pltpu.VMEM((rows, D), F32),
            pltpu.VMEM((rows, width), BF16),
            pltpu.VMEM((rows, 3 * width), BF16),
        ],
        compiler_params=params(),
        name="attention_backward",
        cost_estimate=pl.CostEstimate(
            flops=4 * rows * D * D * 4, bytes_accessed=26 << 20, transcendentals=rows * 2048
        ),
    )(core, grad, mixer_rows, inputs, normed, gain, weights, qkv, context, *tokens)


def shifted(block, distance):
    devices = range(lax.axis_size(SEQ))
    route = [(i - distance, i) for i in devices if i - distance in devices]
    return lax.ppermute(block, SEQ, route)


def rms_scale(values):
    return values * inverse_rms(values)


def sequence_first(positions, lengths):
    offsets = jnp.cumsum(lengths) - lengths
    chosen = jnp.where(offsets[None, :] <= positions[:, None], offsets[None, :], 0)
    return jnp.max(chosen, axis=1)


def causal_conv(padded, weight, positions, first):
    count = positions.shape[0]
    total = jnp.zeros((count, padded.shape[1]), jnp.float32)
    for offset in range(CONV):
        lag = CONV - 1 - offset
        keep = (positions - lag >= first).astype(jnp.float32)[:, None]
        total = total + weight[offset][None, :] * padded[offset : offset + count] * keep
    return total


def front_part(padded, step_raw, conv_weight, step_bias, decay_log, positions, first):
    activated = jax.nn.silu(causal_conv(padded, conv_weight, positions, first))
    inner = activated.shape[1] - 2 * STATE
    count = positions.shape[0]
    inner_vals = activated[:, :inner].reshape(count, inner // HEAD_DIM, HEAD_DIM)
    bmatrix = activated[:, inner : inner + STATE]
    cmatrix = activated[:, inner + STATE :]
    steps = jax.nn.softplus(step_raw + step_bias[None, :])
    rates = -jnp.exp(decay_log)
    return (inner_vals, bmatrix, cmatrix, steps, rates)


def block_summary(inner_vals, bmatrix, steps, rates, positions, first):
    logs = jnp.cumsum(steps * rates[None, :], axis=0)
    final = logs[-1]
    in_last = (first == first[-1]).astype(jnp.float32)[:, None]
    weights = jnp.exp(final[None, :] - logs) * in_last * steps
    carried = jnp.exp(final) * (first[-1] < positions[0]).astype(jnp.float32)
    states = jnp.einsum("sh,shp,sn->hpn", weights, inner_vals, bmatrix, precision=highest)
    return (carried, states)


def block_output(inner_vals, bmatrix, cmatrix, steps, rates, skip_gain, incoming, positions, first):
    logs = jnp.cumsum(steps * rates[None, :], axis=0)
    count = positions.shape[0]
    same = (first[:, None] == first[None, :]) & (positions[None, :] <= positions[:, None])
    diff = logs.T[:, :, None] - logs.T[:, None, :]
    decay = jnp.where(same[None], jnp.exp(jnp.where(same[None], diff, 0.0)), 0.0)
    inner_prod = jnp.dot(cmatrix, bmatrix.T, precision=highest, preferred_element_type=jnp.float32)
    mixing = decay * inner_prod[None] * steps.T[:, None, :]
    within = jnp.einsum("hts,shp->thp", mixing, inner_vals, precision=highest)
    carry = jnp.exp(logs) * (first < positions[0]).astype(jnp.float32)[:, None]
    remote = jnp.einsum("tn,hpn->thp", cmatrix, incoming, precision=highest) * carry[:, :, None]
    result = within + remote + skip_gain[None, :, None] * inner_vals
    return result.reshape(count, -1)


def product(left, right, form):
    return jnp.einsum(form, left, right, preferred_element_type=jnp.float32)


def norm_backward(grad, values, gain):
    scale = inverse_rms(values)
    normed = values * scale
    scaled = grad * gain[None, :]
    result = scale * (scaled - normed * jnp.mean(scaled * normed, axis=-1, keepdims=True))
    return (result, jnp.sum(grad * normed, axis=0))


def high_low(values):
    high = values.astype(BF16)
    low = (values - high.astype(F32)).astype(BF16)
    return high, low


def reached(factors, states, distance):
    count = lax.axis_size(SEQ)
    heads = factors.shape[0]
    columns = jnp.broadcast_to(factors[:, None], (heads, STATE))
    high, low = high_low(columns)
    packed = jnp.concatenate([states.reshape(-1, STATE).astype(BF16), high, low], axis=0)
    total = jnp.zeros(states.shape, F32)
    chain = jnp.ones((heads, 1, 1), F32)
    for hop in range(1, count // 2 + 1):
        step = hop * distance
        route = [(i, i + step) for i in range(count) if 0 <= i + step < count]
        got = lax.ppermute(packed, SEQ, route).astype(F32)
        total = total + chain * got[: -2 * heads].reshape(states.shape)
        factor = (got[-2 * heads : -heads] + got[-heads:])[:, :1]
        chain = chain * factor[:, :, None]
    return total


def tied(array, *tokens):
    zero = sum(t[(0,) * t.ndim].astype(F32) * 0.0 for t in tokens)
    return (array.astype(F32) + zero).astype(array.dtype)


def swap(array, axis):
    return lax.ppermute(array, axis, [(0, 1), (1, 0)])


def picked(array, axis, index):
    return lax.dynamic_index_in_dim(array, index, axis, False)


def parallel_params(axes):
    return pltpu.CompilerParams(
        dimension_semantics=("arbitrary",) * axes, vmem_limit_bytes=32 * 1024 * 1024
    )


def first_sum_kernel(place_ref, *refs):
    ins, outs = refs[:8], refs[-4:]
    for k in range(4):
        total = ins[2 * k][...].astype(F32) + ins[2 * k + 1][...].astype(F32)
        outs[k][...] = total.reshape(outs[k].shape).astype(BF16)


def first_sum(place, own, got, tokens=()):
    _, _, tps, rows, cols = own.shape
    half = rows // 2
    block = (1, 1, 1, half, cols)
    maps = [
        lambda t, i, p: (i, 1 - p[1], t, 0, 0),
        lambda t, i, p: (i, p[1], t, 0, 0),
        lambda t, i, p: (1 - p[0], i, t, 1, 0),
        lambda t, i, p: (p[0], i, t, 1, 0),
    ]
    specs = [pl.BlockSpec(block, m) for m in maps for _ in range(2)]
    return pl.pallas_call(
        first_sum_kernel,
        grid_spec=pltpu.PrefetchScalarGridSpec(
            num_scalar_prefetch=1,
            grid=(tps, 2),
            in_specs=specs + [anywhere() for _ in tokens],
            out_specs=[
                pl.BlockSpec((1, 1, half, cols), lambda t, i, p: (i, t, 0, 0)) for _ in range(4)
            ],
        ),
        out_shape=[jax.ShapeDtypeStruct((2, tps, half, cols), BF16) for _ in range(4)],
        compiler_params=parallel_params(2),
        name="first_sum",
        cost_estimate=pl.CostEstimate(
            flops=own.size, bytes_accessed=6 * own.size, transcendentals=0
        ),
    )(place, *([own, got] * 4), *tokens)


def second_sum_kernel(place_ref, *refs):
    ins, outs = refs[:8], refs[-4:]
    for k in range(4):
        total = ins[2 * k][...].astype(F32) + ins[2 * k + 1][...].astype(F32)
        outs[k][...] = total.reshape(outs[k].shape).astype(BF16)


def second_sum(place, kept_one, got_one, kept_two, got_two, tokens=()):
    _, tps, half, cols = kept_one.shape
    block = (1, 1, half, cols)
    maps = [
        lambda t, p: (1 - p[0], t, 0, 0),
        lambda t, p: (p[0], t, 0, 0),
        lambda t, p: (1 - p[1], t, 0, 0),
        lambda t, p: (p[1], t, 0, 0),
    ]
    return pl.pallas_call(
        second_sum_kernel,
        grid_spec=pltpu.PrefetchScalarGridSpec(
            num_scalar_prefetch=1,
            grid=(tps,),
            in_specs=[pl.BlockSpec(block, m) for m in maps for _ in range(2)]
            + [anywhere() for _ in tokens],
            out_specs=[pl.BlockSpec((1, half, cols), lambda t, p: (t, 0, 0)) for _ in range(4)],
        ),
        out_shape=[jax.ShapeDtypeStruct((tps, half, cols), BF16) for _ in range(4)],
        compiler_params=parallel_params(1),
        name="second_sum",
        cost_estimate=pl.CostEstimate(
            flops=2 * kept_one.size, bytes_accessed=12 * kept_one.size, transcendentals=0
        ),
    )(place, *([kept_one, got_one] * 2), *([kept_two, got_two] * 2), *tokens)


def third_sum_kernel(one_ref, two_ref, three_ref, four_ref, *refs):
    out_ref = refs[-1]
    half = one_ref.shape[1]
    out_ref[0, :half] = (one_ref[0].astype(F32) + two_ref[0].astype(F32)).astype(BF16)
    out_ref[0, half:] = (three_ref[0].astype(F32) + four_ref[0].astype(F32)).astype(BF16)


def third_sum(kept_one, got_one, kept_two, got_two, tokens=()):
    tps, half, cols = kept_one.shape
    return pl.pallas_call(
        third_sum_kernel,
        grid=(tps,),
        in_specs=[pl.BlockSpec((1, half, cols), lambda t: (t, 0, 0)) for _ in range(4)]
        + [anywhere() for _ in tokens],
        out_specs=pl.BlockSpec((1, 2 * half, cols), lambda t: (t, 0, 0)),
        out_shape=jax.ShapeDtypeStruct((tps, 2 * half, cols), BF16),
        compiler_params=parallel_params(1),
        name="third_sum",
        cost_estimate=pl.CostEstimate(
            flops=2 * kept_one.size, bytes_accessed=12 * kept_one.size, transcendentals=0
        ),
    )(kept_one, got_one, kept_two, got_two, *tokens)


def reduce_first(place, own, other, tokens=()):
    return first_sum(place, own, swap(other, "c"), tokens)


def reduce_second(place, sums, tokens=()):
    send_one, keep_one, send_two, keep_two = sums
    return second_sum(
        place, keep_one, swap(send_one, "b"), keep_two, swap(send_two, "a"), tokens
    )


def reduce_third(sums, tokens=()):
    send_one, keep_one, send_two, keep_two = sums
    return third_sum(keep_one, swap(send_one, "a"), keep_two, swap(send_two, "b"), tokens)


def reduce_last(summed):
    part = lax.psum_scatter(summed, "tp", scatter_dimension=0)
    if lax.axis_size("g") > 1:
        part = lax.psum(part, "g")
    return lax.all_gather(part, INNER)


def shards(
    patches,
    byte_embed,
    seq_lengths,
    norm_global,
    proj_gate,
    proj_inner,
    proj_state,
    proj_step,
    step_bias,
    decay_log,
    conv_inner,
    conv_state,
    skip_gain,
    mixer_gain,
    proj_mixer,
    norm_attn,
    attn_input,
    attn_output,
    norm_ffn,
    expand_weight,
    shrink_weight,
    grad_output,
):
    count, quarter = patches.shape
    tps = lax.axis_size("tp")
    mine = lax.axis_index("tp")
    here = lax.axis_index(SEQ)
    core = lax.axis_index("c").reshape(1)
    tail = CONV - 1
    inner_width = proj_inner.shape[1]
    share = count // tps
    total_rows = byte_embed.shape[0]
    rows = total_rows // tps

    narrow = D // GROUP
    slot = lax.axis_index(INNER)

    def gather_weights(part):
        return lax.all_gather(part, INNER + ("tp",)).reshape((GROUP, tps) + part.shape)

    def folded(array, width):
        rows_in = array.shape[0]
        return array.reshape(rows_in, -1, width).transpose(1, 0, 2).reshape(-1, width)

    def unfolded(array, folds):
        blocks = array.reshape(GROUP, folds, -1, array.shape[-1])
        return blocks.transpose(0, 2, 1, 3).reshape(-1, folds * array.shape[-1])

    attn_in_part = lax.dynamic_slice_in_dim(attn_input, slot * narrow, narrow, 1)
    out_rows = attn_output.shape[0] // GROUP
    attn_out_part = lax.dynamic_slice_in_dim(attn_output, slot * out_rows, out_rows, 0)
    attn_out_part = folded(attn_out_part, quarter)
    hidden_width = expand_weight.shape[2]
    wide = hidden_width // PIECES
    down_rows = wide // GROUP
    ffn_parts = []
    for p in range(PIECES):
        up_part = lax.dynamic_slice(
            expand_weight, (0, slot * narrow, p * wide), (2, narrow, wide)
        )
        down_part = lax.dynamic_slice_in_dim(
            shrink_weight, p * wide + slot * down_rows, down_rows, 0
        )
        ffn_parts.append([up_part.reshape(-1, wide), folded(down_part, wide)])
    attn_parts = [
        jnp.concatenate([attn_in_part[0], attn_in_part[2]], axis=1),
        jnp.concatenate([attn_in_part[1], attn_out_part], axis=1),
    ]
    weights = gather_weights(jnp.concatenate(attn_parts + ffn_parts[0], axis=0))
    last_weights = gather_weights(jnp.concatenate(ffn_parts[1], axis=0))
    place = jnp.stack([lax.axis_index("a"), lax.axis_index("b")]).astype(jnp.int32)

    def to_rows(array):
        return lax.all_to_all(array.reshape(tps, rows, quarter), "tp", 0, 0)

    def to_columns(blocks):
        return lax.all_to_all(blocks, "tp", 0, 0).reshape(total_rows, quarter)

    positions = here * count + jnp.arange(count, dtype=jnp.int32)
    first = sequence_first(positions, seq_lengths)
    patch_rows = lax.all_gather(patches, "tp", axis=1, tiled=True)
    embed_rows = to_rows(byte_embed)
    cot_rows = to_rows(grad_output)
    global_in = patch_rows.astype(jnp.float32)
    normed = (rms_scale(global_in) * norm_global[None, :]).astype(jnp.bfloat16)
    gate_vals = product(normed, proj_gate, "rd,dc->rc")
    inner_raw = product(normed, proj_inner, "rd,dc->rc")
    state_raw = product(normed, proj_state, "rd,dc->rc")
    step_raw = product(normed, proj_step, "rd,dc->rc")
    raw = jnp.concatenate([inner_raw, state_raw], axis=1)
    before = shifted(raw[count - tail :], 1)
    padded = jnp.concatenate([before, raw], axis=0)
    conv_weight = jnp.concatenate([conv_inner, conv_state], axis=1)

    def front_local(padded_in, step_in, conv_in, bias_in, decay_in):
        return front_part(padded_in, step_in, conv_in, bias_in, decay_in, positions, first)

    def summary_local(inner_in, bmat_in, steps_in, rates_in):
        return block_summary(inner_in, bmat_in, steps_in, rates_in, positions, first)

    def output_local(inner_in, bmat_in, cmat_in, steps_in, rates_in, skip_in, incoming_in):
        return block_output(
            inner_in, bmat_in, cmat_in, steps_in, rates_in, skip_in, incoming_in, positions, first
        )

    front_vals, front_pull = jax.vjp(
        front_local, padded, step_raw, conv_weight, step_bias, decay_log
    )
    inner_vals, bmatrix, cmatrix, steps, rates = front_vals
    summary, summary_pull = jax.vjp(summary_local, inner_vals, bmatrix, steps, rates)
    carried, states = summary
    incoming = reached(carried, states, 1)
    mixed, output_pull = jax.vjp(
        output_local, inner_vals, bmatrix, cmatrix, steps, rates, skip_gain, incoming
    )
    gate_act = jax.nn.silu(gate_vals)
    gated = mixed * gate_act
    squares = jnp.sum(gated * gated, axis=1, keepdims=True)
    partial = product((gated * mixer_gain[None, :]).astype(BF16), proj_mixer, "rc,cd->rd")
    square_high, square_low = high_low(jnp.broadcast_to(squares, (count, 64)))
    partial = partial + embed_rows[0, 0, 0].astype(F32) * 0.0
    sent = jnp.concatenate([partial.astype(BF16), square_high, square_low], axis=1)
    summed = jnp.sum(
        lax.all_to_all(sent.reshape(tps, share, -1), "tp", 0, 0).astype(F32), axis=0
    )
    own_squares = summed[:, D : D + 1] + summed[:, D + 64 : D + 65]
    mixer_rows = summed[:, :D] * lax.rsqrt(own_squares / DI + epsilon)
    own_patches = lax.dynamic_slice_in_dim(patch_rows, mine * share, share, 0)
    global_out = own_patches.astype(F32) + mixer_rows

    hidden, attn_in, attn_normed, qkv, context = attention_forward(
        embed_rows, global_out[:, None, :], norm_attn[None, :], weights
    )
    ffn_normed, ffn_turned, cot_whole, out_acc, normed_acc, own_first, other_first = (
        feed_forward_first(core, hidden, cot_rows, norm_ffn[None, :], weights)
    )
    first_one = reduce_first(place, own_first, other_first)
    first_two = reduce_second(place, first_one)
    layer_blocks, hidden_grad, norm_ffn_part, last_grad = feed_forward_last(
        core,
        hidden,
        cot_whole,
        norm_ffn[None, :],
        last_weights,
        ffn_normed,
        ffn_turned,
        out_acc,
        normed_acc,
        first_two[0],
    )
    layer_output = to_columns(layer_blocks)
    first_three = reduce_third(first_two, (hidden_grad,))
    embed_blocks, own_grad, row_dot, norm_attn_part, own_attn, other_attn = attention_backward(
        core,
        hidden_grad,
        mixer_rows,
        attn_in,
        attn_normed,
        norm_attn[None, :],
        weights,
        qkv,
        context,
        (first_three, layer_output),
    )
    last_three = lax.psum_scatter(last_grad, INNER, scatter_dimension=0)
    attn_one = reduce_first(place, own_attn, other_attn)
    embed_grad = to_columns(embed_blocks).astype(F32)

    extra_high, extra_low = high_low(
        jnp.concatenate(
            [jnp.broadcast_to(v, (share, 32)) for v in (own_squares, row_dot)], axis=1
        )
    )
    returned = lax.all_gather(
        jnp.concatenate([own_grad.astype(BF16), extra_high, extra_low], axis=1),
        "tp",
        axis=0,
        tiled=True,
    )
    mix_back_in = returned[:, :D]
    extras = returned[:, D : D + 64].astype(F32) + returned[:, D + 64 :].astype(F32)
    all_squares, all_dots = tied(extras[:, :1], attn_one[0]), extras[:, 32:33]
    row_scale = lax.rsqrt(all_squares / DI + epsilon)
    row_mean = all_dots / DI
    normed_mix = gated * row_scale
    mix_low = (normed_mix * mixer_gain[None, :]).astype(jnp.bfloat16)
    proj_mixer_grad = product(mix_low, mix_back_in, "rc,rd->cd")
    mix_low_grad = product(mix_back_in, proj_mixer, "rd,cd->rc")
    mixer_gain_grad = jnp.sum(mix_low_grad * normed_mix, axis=0)
    scaled_grad = mix_low_grad * mixer_gain[None, :]
    gated_grad = row_scale * (scaled_grad - normed_mix * row_mean)
    mixed_grad = gated_grad * gate_act
    sigma_gate = jax.nn.sigmoid(gate_vals)
    gate_vals_grad = gated_grad * mixed * sigma_gate * (1.0 + gate_vals * (1.0 - sigma_gate))
    inner_one, bmat_one, cmat_one, steps_one, rates_one, skip_gain_grad, incoming_grad = (
        output_pull(mixed_grad)
    )
    attn_two = reduce_second(place, attn_one, (incoming_grad,))
    attn_three = reduce_third(attn_two)
    later_grad = reached(carried, tied(incoming_grad, attn_two[0]), -1)
    later_grad = tied(later_grad, attn_three)
    carried_grad = jnp.sum(later_grad * incoming, axis=(1, 2))
    inner_two, bmat_two, steps_two, rates_two = summary_pull((carried_grad, later_grad))
    padded_grad, step_raw_grad, conv_grad, step_bias_grad, decay_log_grad = front_pull(
        (
            inner_one + inner_two,
            bmat_one + bmat_two,
            cmat_one,
            steps_one + steps_two,
            rates_one + rates_two,
        )
    )
    tail_grad = shifted(padded_grad[:tail], -1)
    raw_grad = padded_grad[tail:]
    raw_grad = jnp.concatenate(
        [raw_grad[: count - tail], raw_grad[count - tail :] + tail_grad], axis=0
    )
    gate_back = gate_vals_grad.astype(jnp.bfloat16)
    inner_back = raw_grad[:, :inner_width].astype(jnp.bfloat16)
    state_back = raw_grad[:, inner_width:].astype(jnp.bfloat16)
    step_back = step_raw_grad.astype(jnp.bfloat16)
    normed_grad_part = (
        product(gate_back, proj_gate, "rc,dc->rd")
        + product(inner_back, proj_inner, "rc,dc->rd")
        + product(step_back, proj_step, "rc,dc->rd")
        + product(state_back, proj_state, "rs,ds->rd")
    )
    part_in_grad, norm_global_part = norm_backward(normed_grad_part, global_in, norm_global)
    part_in_grad = lax.dynamic_update_slice_in_dim(
        part_in_grad,
        lax.dynamic_slice_in_dim(part_in_grad, mine * share, share, 0) + own_grad,
        mine * share,
        0,
    )
    shared = jnp.concatenate(
        [
            conv_grad[:, inner_width:].reshape(-1),
            norm_attn_part[0],
            norm_ffn_part[0],
            norm_global_part,
        ]
    ).reshape(-1, quarter)
    shared_high, shared_low = high_low(shared)
    shared_rows = jnp.concatenate([shared_high, shared_low], axis=0)
    columns = part_in_grad.astype(BF16).reshape(count, tps, quarter).transpose(1, 0, 2)
    returned = lax.all_to_all(
        jnp.concatenate(
            [columns, jnp.broadcast_to(shared_rows[None], (tps,) + shared_rows.shape)], axis=1
        ),
        "tp",
        0,
        0,
    )
    returned = jnp.sum(returned.astype(F32), axis=0)
    patch_grad = returned[:count]
    shared = returned[count : count + shared.shape[0]] + returned[count + shared.shape[0] :]
    shared = shared.reshape(-1)
    held = conv_state.size
    shared = (
        shared[:held].reshape(conv_state.shape),
        shared[held : held + D],
        shared[held + D : held + 2 * D],
        shared[held + 2 * D :],
    )
    state_all = lax.all_gather(state_back, "tp")
    state_sum = jnp.sum(state_all.astype(F32), axis=0).astype(BF16)
    early_grads = lax.psum(
        (
            product(normed, gate_back, "rd,rc->dc").astype(BF16),
            proj_mixer_grad.astype(BF16),
        ),
        SEQ,
    )
    late_grads = lax.psum(
        (
            product(normed, inner_back, "rd,rc->dc").astype(BF16),
            product(normed, state_sum, "rd,rc->dc").astype(BF16),
        ),
        SEQ,
    )
    proj_grads = (early_grads[0], late_grads[0], late_grads[1], early_grads[1])
    proj_gate_grad, proj_inner_grad, proj_state_grad, proj_mixer_grad = (
        g.astype(F32) for g in proj_grads
    )
    (
        conv_state_grad,
        norm_attn_grad,
        norm_ffn_grad,
        norm_global_grad,
        proj_step_grad,
        step_bias_grad,
        decay_log_grad,
        conv_inner_grad,
        skip_gain_grad,
        mixer_gain_grad,
    ) = lax.psum(
        shared
        + (
            product(normed, step_back, "rd,rc->dc"),
            step_bias_grad,
            decay_log_grad,
            conv_grad[:, :inner_width],
            skip_gain_grad,
            mixer_gain_grad,
        ),
        SEQ,
    )
    ffn_depth, attn_depth = 3 * narrow, 2 * narrow
    all_grads = reduce_last(jnp.concatenate([first_three, last_three, attn_three], axis=1))
    ffn_grads = [all_grads[:, i * ffn_depth : (i + 1) * ffn_depth] for i in range(PIECES)]
    attn_grad = all_grads[:, PIECES * ffn_depth :]
    expand_grad = jnp.concatenate(
        [
            g[:, : 2 * narrow].reshape(GROUP, 2, narrow, wide).transpose(1, 0, 2, 3).reshape(2, D, wide)
            for g in ffn_grads
        ],
        axis=2,
    ).astype(F32)
    shrink_grad = jnp.concatenate(
        [unfolded(g[:, 2 * narrow :], D // wide) for g in ffn_grads], axis=0
    ).astype(F32)
    attn_input_grad = jnp.stack(
        [
            attn_grad[:, (k % 2) * narrow : (k % 2 + 1) * narrow, (k // 2) * quarter : (k // 2 + 1) * quarter]
            for k in range(3)
        ]
    ).reshape(3, D, quarter).astype(F32)
    attn_output_grad = unfolded(attn_grad[:, narrow:, quarter:], D // quarter).astype(F32)
    return (
        layer_output,
        embed_grad,
        patch_grad,
        norm_global_grad,
        proj_gate_grad,
        proj_inner_grad,
        proj_state_grad,
        proj_step_grad,
        step_bias_grad,
        decay_log_grad,
        conv_inner_grad,
        conv_state_grad,
        skip_gain_grad,
        mixer_gain_grad,
        proj_mixer_grad,
        norm_attn_grad,
        attn_input_grad,
        attn_output_grad,
        norm_ffn_grad,
        expand_grad,
        shrink_grad,
    )


def solution(mesh):
    seq, tps = mesh.shape["seq"], mesh.shape["tp"]
    fine = Mesh(mesh.devices.reshape(seq // GROUP, 2, 2, 2, tps), SEQ + ("tp",))
    rows_cols = P(SEQ, "tp")
    last = P(None, "tp")
    lead = P("tp", None)
    return jax.shard_map(
        shards,
        mesh=fine,
        in_specs=(
            rows_cols,
            rows_cols,
            P(),
            P(),
            last,
            last,
            P(),
            last,
            P("tp"),
            P("tp"),
            last,
            P(),
            P("tp"),
            P("tp"),
            lead,
            P(),
            P(None, None, "tp"),
            lead,
            P(),
            P(None, None, "tp"),
            lead,
            rows_cols,
        ),
        out_specs=(
            rows_cols,
            rows_cols,
            rows_cols,
            P(),
            last,
            last,
            P(),
            last,
            P("tp"),
            P("tp"),
            last,
            P(),
            P("tp"),
            P("tp"),
            lead,
            P(),
            P(None, None, "tp"),
            lead,
            P(),
            P(None, None, "tp"),
            lead,
        ),
        check_vma=False,
    )
```

```python
import functools

import jax
import jax.numpy as jnp
from jax import lax
from jax.experimental import pallas as pl
from jax.experimental.pallas import tpu as pltpu
from jax.sharding import Mesh, PartitionSpec as P

D = 1024
HEAD_DIM = 64
STATE = 128
HEADS_A = 16
CONV = 4
PATCH = 8
DI = 2048
GROUP = 8
TILE = 128
PIECES = 2

epsilon = 1e-05
highest = lax.Precision.HIGHEST
F32 = jnp.float32
BF16 = jnp.bfloat16
SEQ = ("g", "a", "b", "c")
INNER = ("a", "b", "c")


def mm(left, right):
    return lax.dot_general(left, right, (((1,), (0,)), ((), ())), preferred_element_type=F32)


def mm_nt(left, right):
    return lax.dot_general(left, right, (((1,), (1,)), ((), ())), preferred_element_type=F32)


def mm_tn(left, right):
    return lax.dot_general(left, right, (((0,), (0,)), ((), ())), preferred_element_type=F32)


def inverse_rms(values):
    return lax.rsqrt(jnp.mean(values * values, axis=-1, keepdims=True) + epsilon)


def params(limit=60):
    return pltpu.CompilerParams(
        dimension_semantics=("arbitrary",), vmem_limit_bytes=limit * 1024 * 1024
    )


def whole(shape):
    return pl.BlockSpec(shape, lambda j: (0,) * len(shape))


def scalar_spec():
    return pl.BlockSpec(memory_space=pltpu.SMEM)


def halves_shape(tps, depth, wide):
    return jax.ShapeDtypeStruct((2, 2, tps, depth, wide), BF16)


def halves_spec(depth, wide):
    return pl.BlockSpec((2, 2, 1, depth, wide), lambda j: (0, 0, j, 0, 0))


def anywhere():
    return pl.BlockSpec(memory_space=pl.ANY)


def weight_specs(weights, first):
    parts, _, _, wide = weights.shape
    block = (parts, 1, D // GROUP, wide)
    return [
        pl.BlockSpec(block, functools.partial(lambda k, j: (0, j, k, 0), first + k))
        for k in range(3)
    ]


def attention_spec(weights):
    parts, _, _, wide = weights.shape
    return pl.BlockSpec((parts, 1, 2 * D // GROUP, wide), lambda j: (0, j, 0, 0))


def attention_view(weight_ref, k, width):
    deep = D // weight_ref.shape[0]
    rows = slice((k % 2) * deep, (k % 2 + 1) * deep)
    return weight_ref.at[:, 0, rows, (k // 2) * width : (k // 2 + 1) * width]


def head_mask(width):
    lane = lax.broadcasted_iota(jnp.int32, (1, width), 1) // (D // HEADS_A)
    return [lane == h for h in range(width // (D // HEADS_A))]


def split_heads(tile, masks):
    zero = jnp.zeros_like(tile)
    return jnp.concatenate([jnp.where(m, tile, zero) for m in masks], axis=0)


def tile_mask(heads):
    row = lax.broadcasted_iota(jnp.int32, (heads * TILE, TILE), 0) % TILE
    col = lax.broadcasted_iota(jnp.int32, (heads * TILE, TILE), 1)
    return (row // PATCH == col // PATCH) & (col <= row)


def tile_probs(query_split, keys, keep):
    scores = mm_nt(query_split, keys) * ((D // HEADS_A) ** -0.5)
    scores = jnp.where(keep, scores, -1e30)
    expo = jnp.exp(scores - jnp.max(scores, axis=-1, keepdims=True))
    return expo / jnp.sum(expo, axis=-1, keepdims=True)


def beside(stacked, heads):
    return jnp.concatenate([stacked[h * TILE : (h + 1) * TILE] for h in range(heads)], axis=1)


def attention_forward_kernel(
    embed_ref, global_ref, gain_ref, weight_ref, *refs
):
    hidden_ref, input_ref, normed_ref, qkv_ref, context_ref = refs[-5:]
    step = pl.program_id(0)
    blocks, rows, width = embed_ref.shape
    parts = weight_ref.shape[0]

    @pl.when(step == 0)
    def _():
        embed = jnp.concatenate([embed_ref[i] for i in range(blocks)], axis=1).astype(F32)
        spread = jnp.broadcast_to(global_ref[...], (rows // PATCH, PATCH, D)).reshape(rows, D)
        total = embed + spread
        hidden_ref[...] = total
        low = total.astype(BF16)
        input_ref[...] = low
        values = low.astype(F32)
        normed_ref[...] = (values * inverse_rms(values) * gain_ref[...]).astype(BF16)

    normed = normed_ref[...]
    for k in range(3):
        weight = attention_view(weight_ref, k, width)[...].reshape(D, width)
        qkv_ref[0, k] = mm(normed, weight).astype(BF16)
    masks = head_mask(width)
    heads = len(masks)
    keep = tile_mask(heads)
    for r in range(rows // TILE):
        at = slice(r * TILE, (r + 1) * TILE)
        query = split_heads(qkv_ref[0, 0, at], masks)
        probs = tile_probs(query, qkv_ref[0, 1, at], keep).astype(BF16)
        values = split_heads(qkv_ref[0, 2, at], masks)
        context_ref[0, at] = mm(beside(probs, heads), values).astype(BF16)
    context = context_ref[0]
    piece = width // parts
    outward = attention_view(weight_ref, 3, width)
    for c in range(D // width):
        weight = outward[:, c * piece : (c + 1) * piece].reshape(width, width)
        cols = slice(c * width, (c + 1) * width)
        hidden_ref[:, cols] += mm(context, weight)


def attention_forward(embed, global_rows, gain, weights, tokens):
    blocks, rows, width = embed.shape
    tps = weights.shape[1]
    return pl.pallas_call(
        attention_forward_kernel,
        grid=(tps,),
        in_specs=[
            whole((blocks, rows, width)),
            whole((rows // PATCH, 1, D)),
            whole((1, D)),
            attention_spec(weights),
            *(anywhere() for _ in tokens),
        ],
        out_specs=[
            whole((rows, D)),
            whole((rows, D)),
            whole((rows, D)),
            pl.BlockSpec((1, 3, rows, width), lambda j: (j, 0, 0, 0)),
            pl.BlockSpec((1, rows, width), lambda j: (j, 0, 0)),
        ],
        out_shape=[
            jax.ShapeDtypeStruct((rows, D), F32),
            jax.ShapeDtypeStruct((rows, D), BF16),
            jax.ShapeDtypeStruct((rows, D), BF16),
            jax.ShapeDtypeStruct((tps, 3, rows, width), BF16),
            jax.ShapeDtypeStruct((tps, rows, width), BF16),
        ],
        compiler_params=params(),
        name="attention_forward",
        cost_estimate=pl.CostEstimate(
            flops=2 * rows * D * D * 4, bytes_accessed=14 << 20, transcendentals=rows * 2048
        ),
    )(embed, global_rows, gain, weights, *tokens)


def core_halves(core, grad):
    parts = grad.reshape((2, 2, 2, grad.shape[0] // GROUP) + grad.shape[1:])
    mine = jnp.where(core == 0, parts[:, :, 0], parts[:, :, 1])
    other = jnp.where(core == 0, parts[:, :, 1], parts[:, :, 0])
    return mine, other


def put_halves(core, grad, own_ref, other_ref, low, high, cols=slice(None)):
    own, other = core_halves(core, grad.astype(BF16))
    own_ref[:, :, 0, low:high, cols] = own
    other_ref[:, :, 0, low:high, cols] = other


def put_whole(core, grad, grad_ref, low, high):
    parts = grad_ref.shape[0]
    grad_ref[:, 0, low:high] = grad.astype(BF16).reshape((parts, -1) + grad.shape[1:])


def feed_forward_step(
    core_ref, weight_refs, cot, normed_ref, turned_ref, out_acc, normed_acc, put
):
    parts, _, _, wide = weight_refs[0].shape
    deep = D // parts
    core = core_ref[0]
    normed = normed_ref[...]
    gate_weight = weight_refs[0][:, 0].reshape(D, wide)
    up_weight = weight_refs[1][:, 0].reshape(D, wide)
    piece = wide // parts
    folds = D // wide
    down_weight = jnp.concatenate(
        [
            weight_refs[2][:, 0, i * piece : (i + 1) * piece].reshape(wide, wide)
            for i in range(folds)
        ],
        axis=1,
    )
    gate = mm(normed, gate_weight)
    up = mm(normed, up_weight)
    sigma = 1.0 / (1.0 + jnp.exp(-gate))
    swish = gate * sigma
    activ = (swish * up).astype(BF16)
    out_acc[...] += mm(activ, down_weight)
    shrink = mm_tn(activ, cot)
    for i in range(folds):
        low = 2 * deep + i * piece
        put(core, shrink[:, i * wide : (i + 1) * wide], low, low + piece)
    dactiv = mm_nt(cot, down_weight)
    dgate = (dactiv * up * sigma * (1.0 + gate * (1.0 - sigma))).astype(BF16)
    dup = (dactiv * swish).astype(BF16)
    normed_acc[...] += mm_nt(dgate, gate_weight) + mm_nt(dup, up_weight)
    turned = turned_ref[...]
    put(core, mm(turned, dgate), 0, deep)
    put(core, mm(turned, dup), deep, 2 * deep)


def feed_forward_first_kernel(
    core_ref,
    hidden_ref,
    cot_ref,
    gain_ref,
    gate_ref,
    up_ref,
    down_ref,
    normed_ref,
    turned_ref,
    cot_out,
    out_acc,
    normed_acc,
    own_ref,
    other_ref,
):
    blocks, _, width = cot_ref.shape

    @pl.when(pl.program_id(0) == 0)
    def _():
        values = hidden_ref[...].astype(BF16).astype(F32)
        normed = (values * inverse_rms(values) * gain_ref[...]).astype(BF16)
        normed_ref[...] = normed
        turned_ref[...] = normed.astype(F32).T.astype(BF16)
        for i in range(blocks):
            cot_out[:, i * width : (i + 1) * width] = cot_ref[i]
        out_acc[...] = hidden_ref[...]
        normed_acc[...] = jnp.zeros_like(normed_acc)

    def put(core, grad, low, high):
        put_halves(core, grad, own_ref, other_ref, low, high)

    feed_forward_step(
        core_ref,
        (gate_ref, up_ref, down_ref),
        cot_out[...],
        normed_ref,
        turned_ref,
        out_acc,
        normed_acc,
        put,
    )


def feed_forward_last_kernel(
    core_ref,
    hidden_ref,
    cot_ref,
    gain_ref,
    gate_ref,
    up_ref,
    down_ref,
    normed_ref,
    turned_ref,
    out_in,
    normed_in,
    token_ref,
    layer_ref,
    grad_ref,
    gain_grad_ref,
    weight_grad_ref,
    out_acc,
    normed_acc,
):
    step = pl.program_id(0)
    blocks, _, width = layer_ref.shape

    @pl.when(step == 0)
    def _():
        out_acc[...] = out_in[...]
        normed_acc[...] = normed_in[...]

    def put(core, grad, low, high):
        put_whole(core, grad, weight_grad_ref, low, high)

    feed_forward_step(
        core_ref,
        (gate_ref, up_ref, down_ref),
        cot_ref[...],
        normed_ref,
        turned_ref,
        out_acc,
        normed_acc,
        put,
    )

    @pl.when(step == pl.num_programs(0) - 1)
    def _():
        layer = out_acc[...].astype(BF16)
        for i in range(blocks):
            layer_ref[i] = layer[:, i * width : (i + 1) * width]
        values = hidden_ref[...].astype(BF16).astype(F32)
        scale = inverse_rms(values)
        normal = values * scale
        grad = normed_acc[...]
        gain_grad_ref[...] = jnp.sum(grad * normal, axis=0, keepdims=True)
        scaled = grad * gain_ref[...]
        back = scale * (scaled - normal * jnp.mean(scaled * normal, axis=-1, keepdims=True))
        grad_ref[...] = cot_ref[...].astype(F32) + back


def feed_forward_cost(rows, weights):
    _, tps, _, wide = weights.shape
    return pl.CostEstimate(
        flops=18 * rows * D * wide * tps,
        bytes_accessed=12 * D * wide * tps + 16 * rows * D,
        transcendentals=rows * wide * tps,
    )


def feed_forward_first(core, hidden, cot, gain, weights):
    rows = hidden.shape[0]
    _, tps, _, wide = weights.shape
    depth = 3 * D // GROUP
    return pl.pallas_call(
        feed_forward_first_kernel,
        grid=(tps,),
        in_specs=[
            scalar_spec(),
            whole((rows, D)),
            whole(cot.shape),
            whole((1, D)),
            *weight_specs(weights, 2),
        ],
        out_specs=[
            whole((rows, D)),
            whole((D, rows)),
            whole((rows, D)),
            whole((rows, D)),
            whole((rows, D)),
            halves_spec(depth, wide),
            halves_spec(depth, wide),
        ],
        out_shape=[
            jax.ShapeDtypeStruct((rows, D), BF16),
            jax.ShapeDtypeStruct((D, rows), BF16),
            jax.ShapeDtypeStruct((rows, D), BF16),
            jax.ShapeDtypeStruct((rows, D), F32),
            jax.ShapeDtypeStruct((rows, D), F32),
            halves_shape(tps, depth, wide),
            halves_shape(tps, depth, wide),
        ],
        compiler_params=params(),
        name="feed_forward_first",
        cost_estimate=feed_forward_cost(rows, weights),
    )(core, hidden, cot, gain, weights, weights, weights)


def feed_forward_last(
    core, hidden, cot, gain, weights, normed, turned, out_in, normed_in, token
):
    rows = hidden.shape[0]
    _, tps, _, wide = weights.shape
    depth = 3 * D // GROUP
    width = D // tps
    return pl.pallas_call(
        feed_forward_last_kernel,
        grid=(tps,),
        in_specs=[
            scalar_spec(),
            whole((rows, D)),
            whole((rows, D)),
            whole((1, D)),
            *weight_specs(weights, 0),
            whole((rows, D)),
            whole((D, rows)),
            whole((rows, D)),
            whole((rows, D)),
            anywhere(),
        ],
        out_specs=[
            whole((tps, rows, width)),
            whole((rows, D)),
            whole((1, D)),
            pl.BlockSpec((GROUP, 1, depth, wide), lambda j: (0, j, 0, 0)),
        ],
        out_shape=[
            jax.ShapeDtypeStruct((tps, rows, width), BF16),
            jax.ShapeDtypeStruct((rows, D), F32),
            jax.ShapeDtypeStruct((1, D), F32),
            jax.ShapeDtypeStruct((GROUP, tps, depth, wide), BF16),
        ],
        scratch_shapes=[pltpu.VMEM((rows, D), F32), pltpu.VMEM((rows, D), F32)],
        compiler_params=params(),
        name="feed_forward_last",
        cost_estimate=feed_forward_cost(rows, weights),
    )(core, hidden, cot, gain, weights, weights, weights, normed, turned, out_in, normed_in, token)


def attention_backward_kernel(
    core_ref,
    grad_ref,
    mixer_ref,
    input_ref,
    normed_ref,
    gain_ref,
    weight_ref,
    qkv_ref,
    context_ref,
    squares_ref,
    token_ref,
    embed_ref,
    global_ref,
    payload_ref,
    gain_grad_ref,
    own_ref,
    other_ref,
    turned_ref,
    low_ref,
    normed_acc,
    context_grad_ref,
    qkv_grad_ref,
):
    step = pl.program_id(0)
    rows = grad_ref.shape[0]
    blocks, _, width = embed_ref.shape
    parts = weight_ref.shape[0]
    deep = D // parts
    scaling = (D // HEADS_A) ** -0.5
    core = core_ref[0]

    @pl.when(step == 0)
    def _():
        turned_ref[...] = normed_ref[...].astype(F32).T.astype(BF16)
        low_ref[...] = grad_ref[...].astype(BF16)
        normed_acc[...] = jnp.zeros_like(normed_acc)

    low = low_ref[...]
    context = context_ref[0]
    piece = width // parts
    total = jnp.zeros((rows, width), F32)
    outward = attention_view(weight_ref, 3, width)
    for c in range(D // width):
        first = deep + c * piece
        weight = outward[:, c * piece : (c + 1) * piece].reshape(width, width)
        columns = low[:, c * width : (c + 1) * width]
        total = total + mm_nt(columns, weight)
        put_halves(
            core,
            mm_tn(context, columns),
            own_ref,
            other_ref,
            first,
            first + piece,
            slice(width, 2 * width),
        )
    context_grad_ref[...] = total.astype(BF16)
    masks = head_mask(width)
    heads = len(masks)
    keep = tile_mask(heads)
    for r in range(rows // TILE):
        at = slice(r * TILE, (r + 1) * TILE)
        query = split_heads(qkv_ref[0, 0, at], masks)
        keys = qkv_ref[0, 1, at]
        probs = tile_probs(query, keys, keep)
        dcontext = split_heads(context_grad_ref[at], masks)
        dprobs = mm_nt(dcontext, qkv_ref[0, 2, at])
        dvalues = mm_tn(probs.astype(BF16), dcontext)
        inner = jnp.sum(dprobs * probs, axis=-1, keepdims=True)
        dscores = (probs * (dprobs - inner)).astype(BF16)
        dquery = mm(beside(dscores, heads), split_heads(keys, masks)) * scaling
        dkeys = mm_tn(dscores, query) * scaling
        qkv_grad_ref[at, :width] = dquery.astype(BF16)
        qkv_grad_ref[at, width : 2 * width] = dkeys.astype(BF16)
        qkv_grad_ref[at, 2 * width :] = dvalues.astype(BF16)
    turned = turned_ref[...]
    for k in range(3):
        part = qkv_grad_ref[:, k * width : (k + 1) * width]
        weight = attention_view(weight_ref, k, width)[...].reshape(D, width)
        normed_acc[...] += mm_nt(part, weight)
        first = (k % 2) * deep
        put_halves(
            core,
            mm(turned, part),
            own_ref,
            other_ref,
            first,
            first + deep,
            slice((k // 2) * width, (k // 2 + 1) * width),
        )

    @pl.when(step == pl.num_programs(0) - 1)
    def _():
        values = input_ref[...].astype(F32)
        scale = inverse_rms(values)
        normal = values * scale
        grad = normed_acc[...]
        gain_grad_ref[...] = jnp.sum(grad * normal, axis=0, keepdims=True)
        scaled = grad * gain_ref[...]
        back = scale * (scaled - normal * jnp.mean(scaled * normal, axis=-1, keepdims=True))
        result = grad_ref[...] + back
        for i in range(blocks):
            embed_ref[i] = result[:, i * width : (i + 1) * width].astype(BF16)
        patch = jnp.sum(result.reshape(rows // PATCH, PATCH, D), axis=1)
        global_ref[...] = patch
        dots = jnp.sum(patch * mixer_ref[...], axis=1, keepdims=True)
        payload_ref[:, :D] = patch.astype(BF16)
        lane = lax.broadcasted_iota(jnp.int32, (patch.shape[0], 128), 1)
        values = jnp.where(lane % 64 < 32, squares_ref[...], dots)
        high = values.astype(BF16).astype(F32)
        payload_ref[:, D:] = jnp.where(lane < 64, high, values - high).astype(BF16)


def attention_backward(core, grad, mixer_rows, inputs, normed, gain, weights, qkv, context, squares, token):
    rows = grad.shape[0]
    tps, _, width = context.shape
    depth = 2 * D // GROUP
    return pl.pallas_call(
        attention_backward_kernel,
        grid=(tps,),
        in_specs=[
            scalar_spec(),
            whole((rows, D)),
            whole((rows // PATCH, D)),
            whole((rows, D)),
            whole((rows, D)),
            whole((1, D)),
            attention_spec(weights),
            pl.BlockSpec((1, 3, rows, width), lambda j: (j, 0, 0, 0)),
            pl.BlockSpec((1, rows, width), lambda j: (j, 0, 0)),
            whole(squares.shape),
            anywhere(),
        ],
        out_specs=[
            whole((tps, rows, width)),
            whole((rows // PATCH, D)),
            whole((rows // PATCH, D + 128)),
            whole((1, D)),
            halves_spec(depth, 2 * width),
            halves_spec(depth, 2 * width),
        ],
        out_shape=[
            jax.ShapeDtypeStruct((tps, rows, width), BF16),
            jax.ShapeDtypeStruct((rows // PATCH, D), F32),
            jax.ShapeDtypeStruct((rows // PATCH, D + 128), BF16),
            jax.ShapeDtypeStruct((1, D), F32),
            halves_shape(tps, depth, 2 * width),
            halves_shape(tps, depth, 2 * width),
        ],
        scratch_shapes=[
            pltpu.VMEM((D, rows), BF16),
            pltpu.VMEM((rows, D), BF16),
            pltpu.VMEM((rows, D), F32),
            pltpu.VMEM((rows, width), BF16),
            pltpu.VMEM((rows, 3 * width), BF16),
        ],
        compiler_params=params(),
        name="attention_backward",
        cost_estimate=pl.CostEstimate(
            flops=4 * rows * D * D * 4, bytes_accessed=26 << 20, transcendentals=rows * 2048
        ),
    )(core, grad, mixer_rows, inputs, normed, gain, weights, qkv, context, squares, token)


def shifted(block, distance):
    devices = range(lax.axis_size(SEQ))
    route = [(i - distance, i) for i in devices if i - distance in devices]
    return lax.ppermute(block, SEQ, route)


def rms_scale(values):
    return values * inverse_rms(values)


def sequence_first(positions, lengths):
    offsets = jnp.cumsum(lengths) - lengths
    chosen = jnp.where(offsets[None, :] <= positions[:, None], offsets[None, :], 0)
    return jnp.max(chosen, axis=1)


def causal_conv(padded, weight, positions, first):
    count = positions.shape[0]
    total = jnp.zeros((count, padded.shape[1]), jnp.float32)
    for offset in range(CONV):
        lag = CONV - 1 - offset
        keep = (positions - lag >= first).astype(jnp.float32)[:, None]
        total = total + weight[offset][None, :] * padded[offset : offset + count] * keep
    return total


def front_part(padded, step_raw, conv_weight, step_bias, decay_log, positions, first):
    activated = jax.nn.silu(causal_conv(padded, conv_weight, positions, first))
    inner = activated.shape[1] - 2 * STATE
    count = positions.shape[0]
    inner_vals = activated[:, :inner].reshape(count, inner // HEAD_DIM, HEAD_DIM)
    bmatrix = activated[:, inner : inner + STATE]
    cmatrix = activated[:, inner + STATE :]
    steps = jax.nn.softplus(step_raw + step_bias[None, :])
    rates = -jnp.exp(decay_log)
    return (inner_vals, bmatrix, cmatrix, steps, rates)


def block_summary(inner_vals, bmatrix, steps, rates, positions, first):
    logs = jnp.cumsum(steps * rates[None, :], axis=0)
    final = logs[-1]
    in_last = (first == first[-1]).astype(jnp.float32)[:, None]
    weights = jnp.exp(final[None, :] - logs) * in_last * steps
    carried = jnp.exp(final) * (first[-1] < positions[0]).astype(jnp.float32)
    states = jnp.einsum("sh,shp,sn->hpn", weights, inner_vals, bmatrix, precision=highest)
    return (carried, states)


def block_output(inner_vals, bmatrix, cmatrix, steps, rates, skip_gain, incoming, positions, first):
    logs = jnp.cumsum(steps * rates[None, :], axis=0)
    count = positions.shape[0]
    same = (first[:, None] == first[None, :]) & (positions[None, :] <= positions[:, None])
    diff = logs.T[:, :, None] - logs.T[:, None, :]
    decay = jnp.where(same[None], jnp.exp(jnp.where(same[None], diff, 0.0)), 0.0)
    inner_prod = jnp.dot(cmatrix, bmatrix.T, precision=highest, preferred_element_type=jnp.float32)
    mixing = decay * inner_prod[None] * steps.T[:, None, :]
    within = jnp.einsum("hts,shp->thp", mixing, inner_vals, precision=highest)
    carry = jnp.exp(logs) * (first < positions[0]).astype(jnp.float32)[:, None]
    remote = jnp.einsum("tn,hpn->thp", cmatrix, incoming, precision=highest) * carry[:, :, None]
    result = within + remote + skip_gain[None, :, None] * inner_vals
    return result.reshape(count, -1)


def product(left, right, form):
    return jnp.einsum(form, left, right, preferred_element_type=jnp.float32)


def norm_backward(grad, values, gain):
    scale = inverse_rms(values)
    normed = values * scale
    scaled = grad * gain[None, :]
    result = scale * (scaled - normed * jnp.mean(scaled * normed, axis=-1, keepdims=True))
    return (result, jnp.sum(grad * normed, axis=0))


def high_low(values):
    high = values.astype(BF16)
    low = (values - high.astype(F32)).astype(BF16)
    return high, low


def reached(factors, states, distance):
    heads = factors.shape[0]
    columns = jnp.broadcast_to(factors[:, None], (heads, STATE))
    high, low = high_low(columns)
    packed = jnp.concatenate([states.reshape(-1, STATE).astype(BF16), high, low], axis=0)
    return reached_from(packed, distance).reshape(states.shape)


def reached_from(packed, distance):
    count = lax.axis_size(SEQ)
    heads = packed.shape[0] // (HEAD_DIM + 2)
    total = jnp.zeros((heads, HEAD_DIM, STATE), F32)
    chain = jnp.ones((heads, 1, 1), F32)
    for hop in range(1, count // 2 + 1):
        step = hop * distance
        route = [(i, i + step) for i in range(count) if 0 <= i + step < count]
        got = lax.ppermute(packed, SEQ, route).astype(F32)
        total = total + chain * got[: -2 * heads].reshape(total.shape)
        factor = (got[-2 * heads : -heads] + got[-heads:])[:, :1]
        chain = chain * factor[:, :, None]
    return total.reshape(-1, STATE)


def tied(array, *tokens):
    zero = sum(t[(0,) * t.ndim].astype(F32) * 0.0 for t in tokens)
    return (array.astype(F32) + zero).astype(array.dtype)


def swap(array, axis):
    return lax.ppermute(array, axis, [(0, 1), (1, 0)])


def picked(array, axis, index):
    return lax.dynamic_index_in_dim(array, index, axis, False)


def parallel_params(axes):
    return pltpu.CompilerParams(
        dimension_semantics=("arbitrary",) * axes, vmem_limit_bytes=32 * 1024 * 1024
    )


def first_sum_kernel(place_ref, *refs):
    ins, outs = refs[:8], refs[-4:]
    for k in range(4):
        total = ins[2 * k][...].astype(F32) + ins[2 * k + 1][...].astype(F32)
        outs[k][...] = total.reshape(outs[k].shape).astype(BF16)


def first_sum(place, own, got, tokens=()):
    _, _, tps, rows, cols = own.shape
    half = rows // 2
    block = (1, 1, 1, half, cols)
    maps = [
        lambda t, i, p: (i, 1 - p[1], t, 0, 0),
        lambda t, i, p: (i, p[1], t, 0, 0),
        lambda t, i, p: (1 - p[0], i, t, 1, 0),
        lambda t, i, p: (p[0], i, t, 1, 0),
    ]
    specs = [pl.BlockSpec(block, m) for m in maps for _ in range(2)]
    return pl.pallas_call(
        first_sum_kernel,
        grid_spec=pltpu.PrefetchScalarGridSpec(
            num_scalar_prefetch=1,
            grid=(tps, 2),
            in_specs=specs + [anywhere() for _ in tokens],
            out_specs=[
                pl.BlockSpec((1, 1, half, cols), lambda t, i, p: (i, t, 0, 0)) for _ in range(4)
            ],
        ),
        out_shape=[jax.ShapeDtypeStruct((2, tps, half, cols), BF16) for _ in range(4)],
        compiler_params=parallel_params(2),
        name="first_sum",
        cost_estimate=pl.CostEstimate(
            flops=own.size, bytes_accessed=6 * own.size, transcendentals=0
        ),
    )(place, *([own, got] * 4), *tokens)


def second_sum_kernel(place_ref, *refs):
    ins, outs = refs[:8], refs[-4:]
    for k in range(4):
        total = ins[2 * k][...].astype(F32) + ins[2 * k + 1][...].astype(F32)
        outs[k][...] = total.reshape(outs[k].shape).astype(BF16)


def second_sum(place, kept_one, got_one, kept_two, got_two, tokens=()):
    _, tps, half, cols = kept_one.shape
    block = (1, 1, half, cols)
    maps = [
        lambda t, p: (1 - p[0], t, 0, 0),
        lambda t, p: (p[0], t, 0, 0),
        lambda t, p: (1 - p[1], t, 0, 0),
        lambda t, p: (p[1], t, 0, 0),
    ]
    return pl.pallas_call(
        second_sum_kernel,
        grid_spec=pltpu.PrefetchScalarGridSpec(
            num_scalar_prefetch=1,
            grid=(tps,),
            in_specs=[pl.BlockSpec(block, m) for m in maps for _ in range(2)]
            + [anywhere() for _ in tokens],
            out_specs=[pl.BlockSpec((1, half, cols), lambda t, p: (t, 0, 0)) for _ in range(4)],
        ),
        out_shape=[jax.ShapeDtypeStruct((tps, half, cols), BF16) for _ in range(4)],
        compiler_params=parallel_params(1),
        name="second_sum",
        cost_estimate=pl.CostEstimate(
            flops=2 * kept_one.size, bytes_accessed=12 * kept_one.size, transcendentals=0
        ),
    )(place, *([kept_one, got_one] * 2), *([kept_two, got_two] * 2), *tokens)


def third_sum_kernel(one_ref, two_ref, three_ref, four_ref, *refs):
    out_ref = refs[-2]
    half = one_ref.shape[1]
    out_ref[0, :half] = (one_ref[0].astype(F32) + two_ref[0].astype(F32)).astype(BF16)
    out_ref[0, half:] = (three_ref[0].astype(F32) + four_ref[0].astype(F32)).astype(BF16)


def third_sum(kept_one, got_one, kept_two, got_two, carried):
    tps, half, cols = kept_one.shape
    return pl.pallas_call(
        third_sum_kernel,
        grid=(tps,),
        in_specs=[pl.BlockSpec((1, half, cols), lambda t: (t, 0, 0)) for _ in range(4)]
        + [anywhere()],
        out_specs=[pl.BlockSpec((1, 2 * half, cols), lambda t: (t, 0, 0)), anywhere()],
        out_shape=[
            jax.ShapeDtypeStruct((tps, 2 * half, cols), BF16),
            jax.ShapeDtypeStruct(carried.shape, carried.dtype),
        ],
        input_output_aliases={4: 1},
        compiler_params=parallel_params(1),
        name="third_sum",
        cost_estimate=pl.CostEstimate(
            flops=2 * kept_one.size, bytes_accessed=12 * kept_one.size, transcendentals=0
        ),
    )(kept_one, got_one, kept_two, got_two, carried)


def reduce_first(place, own, other, tokens=()):
    return first_sum(place, own, swap(other, "c"), tokens)


def reduce_second(place, sums, tokens=()):
    send_one, keep_one, send_two, keep_two = sums
    return second_sum(
        place, keep_one, swap(send_one, "b"), keep_two, swap(send_two, "a"), tokens
    )


def reduce_third(sums, carried):
    send_one, keep_one, send_two, keep_two = sums
    return third_sum(keep_one, swap(send_one, "a"), keep_two, swap(send_two, "b"), carried)


def over_groups(part):
    return lax.psum(part, "g") if lax.axis_size("g") > 1 else part


def reduce_last(summed):
    return over_groups(lax.psum_scatter(summed, "tp", scatter_dimension=0))


def exchange_last(summed):
    pieces = lax.all_to_all(summed, "tp", 0, 0)
    return over_groups(jnp.sum(pieces.astype(F32), axis=0).astype(BF16))


def unpack_kernel(
    grads_ref,
    expand_ref,
    shrink_ref,
    input_ref,
    output_ref,
    gate_ref,
    inner_ref,
    mixer_ref,
    state_ref,
):
    wide = grads_ref.shape[2]
    deep = D // GROUP
    width = input_ref.shape[2]

    def rows(low, count):
        return grads_ref[0, low : low + count].astype(F32)

    down = wide // GROUP
    for p in range(PIECES):
        base = 3 * deep * p
        for i in range(2):
            expand_ref[i, :, p * wide : (p + 1) * wide] = rows(base + i * deep, deep)
        for i in range(D // wide):
            shrink_ref[p, 0, :, i * wide : (i + 1) * wide] = rows(base + 2 * deep + i * down, down)
    base = 3 * deep * PIECES
    for k in range(3):
        part = rows(base + (k % 2) * deep, deep)
        input_ref[k] = part[:, (k // 2) * width : (k // 2 + 1) * width]
    part = rows(base + deep, deep)[:, width:]
    out_rows = width // GROUP
    for i in range(D // width):
        output_ref[:, i * width : (i + 1) * width] = part[i * out_rows : (i + 1) * out_rows]
    base = base + 2 * deep
    gate_ref[...] = rows(base, deep)
    inner_ref[...] = rows(base + deep, deep)
    for i in range(D // wide):
        mixer_ref[:, i * wide : (i + 1) * wide] = rows(base + 2 * deep + i * down, down)
    state = rows(base + 3 * deep, deep // 2)
    half = wide // 2
    for i in range(2):
        state_ref[i * deep // 2 : (i + 1) * deep // 2] = state[:, i * half : (i + 1) * half]


def unpack(grads, tps):
    _, total, wide = grads.shape
    deep, width, down = D // GROUP, D // tps, wide // GROUP
    shapes = [
        (2, D, PIECES * wide),
        (PIECES, GROUP, down, D),
        (3, D, width),
        (width, D),
        (D, wide),
        (D, wide),
        (wide, D),
        (D, wide // 2),
    ]
    specs = [
        pl.BlockSpec((2, deep, PIECES * wide), lambda j: (0, j, 0)),
        pl.BlockSpec((PIECES, 1, down, D), lambda j: (0, j, 0, 0)),
        pl.BlockSpec((3, deep, width), lambda j: (0, j, 0)),
        pl.BlockSpec((width // GROUP, D), lambda j: (j, 0)),
        pl.BlockSpec((deep, wide), lambda j: (j, 0)),
        pl.BlockSpec((deep, wide), lambda j: (j, 0)),
        pl.BlockSpec((down, D), lambda j: (j, 0)),
        pl.BlockSpec((deep, wide // 2), lambda j: (j, 0)),
    ]
    outs = pl.pallas_call(
        unpack_kernel,
        grid=(GROUP,),
        in_specs=[pl.BlockSpec((1, total, wide), lambda j: (j, 0, 0))],
        out_specs=specs,
        out_shape=[jax.ShapeDtypeStruct(shape, F32) for shape in shapes],
        compiler_params=parallel_params(1),
        name="unpack",
        cost_estimate=pl.CostEstimate(
            flops=grads.size, bytes_accessed=6 * grads.size, transcendentals=0
        ),
    )(grads)
    outs = list(outs)
    outs[1] = outs[1].reshape(PIECES * wide, D)
    return outs


def exact(left, right, dims):
    return lax.dot_general(
        left, right, (dims, ((), ())), precision=highest, preferred_element_type=F32
    )


NN, NT, TN = ((1,), (0,)), ((1,), (1,)), ((0,), (0,))


def column(array, index):
    lane = lax.broadcasted_iota(jnp.int32, array.shape, 1)
    return jnp.sum(jnp.where(lane == index, array, 0.0), axis=1, keepdims=True)


def by_head(pair, one, two):
    lane = lax.broadcasted_iota(jnp.int32, pair, 1)
    return jnp.where(lane < HEAD_DIM, one, two)


def only_head(array, j):
    lane = lax.broadcasted_iota(jnp.int32, array.shape, 1)
    return jnp.where((lane // HEAD_DIM) == j, array, 0.0)


def pair_of(ref, q):
    return ref[:, pl.ds(pl.multiple_of(q * 128, 128), 128)]


def gate_backward_kernel(
    returned_ref,
    weight_ref,
    gain_ref,
    gate_ref,
    mixed_ref,
    cmat_ref,
    reach_ref,
    factor_ref,
    token_ref,
    mix_ref,
    gate_back_ref,
    gain_grad_ref,
    out_grad_ref,
    packed_ref,
):
    back = returned_ref[:, :D]
    extra = returned_ref[:, D:].astype(F32)
    lane = lax.broadcasted_iota(jnp.int32, extra.shape, 1)
    squares = jnp.sum(jnp.where(lane % 64 == 0, extra, 0.0), axis=1, keepdims=True)
    dots = jnp.sum(jnp.where(lane % 64 == 32, extra, 0.0), axis=1, keepdims=True)
    scale = lax.rsqrt(squares / DI + epsilon)
    grad = mm_nt(back, weight_ref[...])
    gate = gate_ref[...]
    mixed = mixed_ref[...]
    gain = gain_ref[...]
    sigma = 1.0 / (1.0 + jnp.exp(-gate))
    act = gate * sigma
    normal = mixed * act * scale
    mix_ref[...] = (normal * gain).astype(BF16)
    gain_grad_ref[...] = jnp.sum(grad * normal, axis=0, keepdims=True)
    gated_grad = scale * (grad * gain - normal * (dots / DI))
    out_grad_ref[...] = gated_grad * act
    gate_back_ref[...] = (gated_grad * mixed * sigma * (1.0 + gate * (1.0 - sigma))).astype(BF16)
    reach = reach_ref[...]
    cmat = cmat_ref[...]
    width = gate.shape[1]
    for q in range(width // 128):
        part = out_grad_ref[:, q * 128 : (q + 1) * 128]
        part = part * by_head(part.shape, column(reach, 2 * q), column(reach, 2 * q + 1))
        packed_ref[q * 128 : (q + 1) * 128] = exact(part, cmat, TN).astype(BF16)
    packed_ref[width:] = factor_ref[...]


def gate_backward(returned, weight, gain, gate, mixed, cmat, reach, factors, token):
    count, width = gate.shape
    args = (returned, weight, gain, gate, mixed, cmat, reach, factors)
    shapes = [
        jax.ShapeDtypeStruct((count, width), BF16),
        jax.ShapeDtypeStruct((count, width), BF16),
        jax.ShapeDtypeStruct((1, width), F32),
        jax.ShapeDtypeStruct((count, width), F32),
        jax.ShapeDtypeStruct((width + factors.shape[0], STATE), BF16),
    ]
    return pl.pallas_call(
        gate_backward_kernel,
        grid=(1,),
        in_specs=[whole(a.shape) for a in args] + [anywhere()],
        out_specs=[whole(o.shape) for o in shapes],
        out_shape=shapes,
        compiler_params=params(),
        name="gate_backward",
        cost_estimate=pl.CostEstimate(
            flops=2 * count * D * width, bytes_accessed=6 << 20, transcendentals=count * width
        ),
    )(*args, token)


def chunk_backward_kernel(
    grad_ref,
    inner_ref,
    bmat_ref,
    cmat_ref,
    logs_ref,
    logs_row_ref,
    steps_row_ref,
    first_ref,
    first_row_ref,
    reach_ref,
    skip_ref,
    incoming_ref,
    token_ref,
    other_token_ref,
    inner_grad_ref,
    bmat_grad_ref,
    cmat_grad_ref,
    logs_grad_ref,
    logs_row_grad_ref,
    steps_row_grad_ref,
    skip_grad_ref,
    product_ref,
    product_grad_ref,
):
    count = grad_ref.shape[0]
    bmat, cmat = bmat_ref[...], cmat_ref[...]
    product_ref[...] = exact(cmat, bmat, NT)
    product_grad_ref[...] = jnp.zeros_like(product_grad_ref)
    cmat_grad_ref[...] = jnp.zeros_like(cmat_grad_ref)
    logs_grad_ref[...] = jnp.zeros_like(logs_grad_ref)
    skip_grad_ref[...] = jnp.zeros_like(skip_grad_ref)

    def one_pair(q, carry):
        inner = pair_of(inner_ref, q)
        grad = pair_of(grad_ref, q)
        incoming = incoming_ref[pl.ds(pl.multiple_of(q * 128, 128), 128), :]
        reading = exact(cmat, incoming, NT)
        row = lax.broadcasted_iota(jnp.int32, (count, count), 0)
        col = lax.broadcasted_iota(jnp.int32, (count, count), 1)
        same = (first_ref[...] == first_row_ref[...]) & (col <= row)
        logs = logs_ref[...]
        reach = reach_ref[...]
        skip = skip_ref[...]
        total = jnp.zeros_like(inner)
        reaches = []
        for j in range(2):
            h = 2 * q + j
            own_grad = only_head(grad, j)
            steps = steps_row_ref[pl.ds(h, 1), :]
            diff = column(logs, h) - logs_row_ref[pl.ds(h, 1), :]
            decay = jnp.where(same, jnp.exp(jnp.where(same, diff, 0.0)), 0.0)
            both = exact(own_grad, inner, NT) * decay
            mixing = decay * product_ref[...]
            product_grad_ref[...] += both * steps
            used = both * product_ref[...]
            total = total + exact(mixing * steps, own_grad, TN)
            over_rows = jnp.sum(used, axis=0, keepdims=True)
            reached_here = column(reach, h)
            reaches.append(reached_here)
            logs_grad = jnp.sum(used * steps, axis=1, keepdims=True)
            logs_grad = logs_grad + reached_here * jnp.sum(
                own_grad * reading, axis=1, keepdims=True
            )
            lane = lax.broadcasted_iota(jnp.int32, logs.shape, 1)
            logs_grad_ref[...] += jnp.where(lane == h, logs_grad, 0.0)
            logs_row_grad_ref[pl.ds(h, 1), :] = -steps * over_rows
            steps_row_grad_ref[pl.ds(h, 1), :] = over_rows
            lane = lax.broadcasted_iota(jnp.int32, skip.shape, 1)
            gained = jnp.sum(jnp.sum(own_grad * inner, axis=1, keepdims=True), axis=0, keepdims=True)
            skip_grad_ref[...] += jnp.where(lane == h, gained, 0.0)
        gains = by_head((1, 128), column(skip, 2 * q), column(skip, 2 * q + 1))
        inner_grad_ref[:, pl.ds(pl.multiple_of(q * 128, 128), 128)] = total + gains * grad
        weighted = grad * by_head(grad.shape, reaches[0], reaches[1])
        cmat_grad_ref[...] += exact(weighted, incoming, NN)
        return carry

    lax.fori_loop(0, grad_ref.shape[1] // 128, one_pair, 0)
    cmat_grad_ref[...] += exact(product_grad_ref[...], bmat, NN)
    bmat_grad_ref[...] = exact(product_grad_ref[...], cmat, TN)


def chunk_backward(args, *tokens):
    count, width = args[0].shape
    heads = args[5].shape[0]
    shapes = [
        jax.ShapeDtypeStruct((count, width), F32),
        jax.ShapeDtypeStruct((count, STATE), F32),
        jax.ShapeDtypeStruct((count, STATE), F32),
        jax.ShapeDtypeStruct((count, heads), F32),
        jax.ShapeDtypeStruct((heads, count), F32),
        jax.ShapeDtypeStruct((heads, count), F32),
        jax.ShapeDtypeStruct((1, heads), F32),
    ]
    return pl.pallas_call(
        chunk_backward_kernel,
        grid=(1,),
        in_specs=[whole(a.shape) for a in args] + [anywhere() for _ in tokens],
        out_specs=[whole(o.shape) for o in shapes],
        out_shape=shapes,
        scratch_shapes=[pltpu.VMEM((count, count), F32), pltpu.VMEM((count, count), F32)],
        compiler_params=params(),
        name="chunk_backward",
        cost_estimate=pl.CostEstimate(
            flops=24 * count * count * width, bytes_accessed=4 << 20, transcendentals=count * count * heads
        ),
    )(*args, *tokens)


def front_backward_kernel(
    later_ref,
    incoming_ref,
    inner_ref,
    bmat_ref,
    logs_ref,
    steps_ref,
    steps_row_ref,
    raw_row_ref,
    last_ref,
    factor_ref,
    rate_ref,
    bias_ref,
    inner_grad_ref,
    bmat_grad_ref,
    cmat_grad_ref,
    logs_grad_ref,
    logs_row_grad_ref,
    steps_row_grad_ref,
    padded_ref,
    conv_ref,
    keep_ref,
    token_ref,
    raw_grad_ref,
    head_grad_ref,
    conv_grad_ref,
    step_back_ref,
    bias_grad_ref,
    decay_grad_ref,
    act_grad_ref,
    logs_total_ref,
    steps_total_ref,
    padded_grad_ref,
):
    count, width = inner_ref.shape
    bmat = bmat_ref[...]
    logs, steps, last = logs_ref[...], steps_ref[...], last_ref[...]
    final = logs[count - 1 : count, :]
    fading = jnp.exp(final - logs) * last
    weights = fading * steps
    logs_total_ref[...] = logs_grad_ref[...]
    steps_total_ref[...] = jnp.zeros_like(steps_total_ref)
    bmat_total = bmat_grad_ref[...]
    lane = lax.broadcasted_iota(jnp.int32, logs.shape, 1)
    row = lax.broadcasted_iota(jnp.int32, logs.shape, 0)
    for q in range(width // 128):
        cols = slice(q * 128, (q + 1) * 128)
        later = later_ref[cols, :]
        inner = inner_ref[:, cols]
        reading = exact(bmat, later, NT)
        spread = by_head(inner.shape, column(weights, 2 * q), column(weights, 2 * q + 1))
        act_grad_ref[:, cols] = inner_grad_ref[:, cols] + spread * reading
        bmat_total = bmat_total + exact(inner * spread, later, NN)
        crossing = jnp.sum(later * incoming_ref[cols, :], axis=1, keepdims=True)
        for j in range(2):
            h = 2 * q + j
            gained = jnp.sum(only_head(inner * reading, j), axis=1, keepdims=True)
            part = lax.broadcasted_iota(jnp.int32, crossing.shape, 0) // HEAD_DIM == j
            crossed = jnp.sum(jnp.where(part, crossing, 0.0), axis=0, keepdims=True)
            crossed = crossed * column(factor_ref[...], h)
            steps_total_ref[...] += jnp.where(lane == h, fading * gained, 0.0)
            moved = column(weights, h) * gained
            ending = jnp.sum(moved, axis=0, keepdims=True) + crossed
            change = jnp.where(row == count - 1, ending - moved, -moved)
            logs_total_ref[...] += jnp.where(lane == h, change, 0.0)
    act_grad_ref[:, width : width + STATE] = bmat_total
    act_grad_ref[:, width + STATE :] = cmat_grad_ref[...]
    t = lax.broadcasted_iota(jnp.int32, (count, count), 0)
    u = lax.broadcasted_iota(jnp.int32, (count, count), 1)
    after = (t >= u).astype(F32)
    here = (t == u).astype(F32)
    reverse = exact(logs_total_ref[...], after, TN) + exact(logs_row_grad_ref[...], after, NN)
    rate = rate_ref[...]
    steps_grad = steps_row_grad_ref[...] + exact(steps_total_ref[...], here, TN) + rate * reverse
    decay_grad_ref[...] = rate * jnp.sum(steps_row_ref[...] * reverse, axis=1, keepdims=True)
    raw = raw_row_ref[...] + bias_ref[...]
    step_grad = steps_grad / (1.0 + jnp.exp(-raw))
    bias_grad_ref[...] = jnp.sum(step_grad, axis=1, keepdims=True)
    step_back_ref[...] = step_grad.astype(BF16)
    top = 8 - (CONV - 1)
    pre = jnp.zeros(act_grad_ref.shape, F32)
    keep = keep_ref[...]
    for k in range(CONV):
        kept = column(keep, k)
        pre = pre + conv_ref[k : k + 1, :] * padded_ref[top + k : top + k + count, :] * kept
    sigma = 1.0 / (1.0 + jnp.exp(-pre))
    act_grad_ref[...] = act_grad_ref[...] * sigma * (1.0 + pre * (1.0 - sigma))
    padded_grad_ref[...] = jnp.zeros_like(padded_grad_ref)
    for k in range(CONV):
        kept = act_grad_ref[...] * column(keep, k)
        conv_grad_ref[k : k + 1, :] = jnp.sum(
            kept * padded_ref[top + k : top + k + count, :], axis=0, keepdims=True
        )
        padded_grad_ref[top + k : top + k + count, :] += conv_ref[k : k + 1, :] * kept
    raw_grad_ref[...] = padded_grad_ref[8:, :]
    head_grad_ref[...] = padded_grad_ref[:8, :]


def front_backward(args, token):
    count, heads = args[4].shape
    wide = args[18].shape[1]
    shapes = [
        jax.ShapeDtypeStruct((count, wide), F32),
        jax.ShapeDtypeStruct((8, wide), F32),
        jax.ShapeDtypeStruct((CONV, wide), F32),
        jax.ShapeDtypeStruct((heads, count), BF16),
        jax.ShapeDtypeStruct((heads, 1), F32),
        jax.ShapeDtypeStruct((heads, 1), F32),
    ]
    return pl.pallas_call(
        front_backward_kernel,
        grid=(1,),
        in_specs=[whole(a.shape) for a in args] + [anywhere()],
        out_specs=[whole(o.shape) for o in shapes],
        out_shape=shapes,
        scratch_shapes=[
            pltpu.VMEM((count, wide), F32),
            pltpu.VMEM((count, heads), F32),
            pltpu.VMEM((count, heads), F32),
            pltpu.VMEM((count + 8, wide), F32),
        ],
        compiler_params=params(),
        name="front_backward",
        cost_estimate=pl.CostEstimate(
            flops=24 * count * STATE * wide, bytes_accessed=8 << 20, transcendentals=2 * count * wide
        ),
    )(*args, token)


def project_backward_kernel(
    mine_ref,
    gate_back_ref,
    inner_back_ref,
    state_back_ref,
    step_back_ref,
    gate_ref,
    inner_ref,
    state_ref,
    step_ref,
    rows_ref,
    normed_ref,
    gain_ref,
    own_ref,
    token_ref,
    blocks_ref,
    gain_grad_ref,
    step_grad_ref,
    total_ref,
):
    grad = mm_nt(gate_back_ref[...], gate_ref[...])
    grad = grad + mm_nt(inner_back_ref[...], inner_ref[...])
    grad = grad + mm_nt(state_back_ref[...], state_ref[...])
    grad = grad + mm_tn(step_back_ref[...], step_ref[...])
    step_grad_ref[...] = mm(step_back_ref[...], normed_ref[...])
    values = rows_ref[...].astype(F32)
    scale = inverse_rms(values)
    normal = values * scale
    gain_grad_ref[...] = jnp.sum(grad * normal, axis=0, keepdims=True)
    scaled = grad * gain_ref[...]
    total_ref[...] = scale * (scaled - normal * jnp.mean(scaled * normal, axis=-1, keepdims=True))
    share = own_ref.shape[0]
    at = pl.ds(pl.multiple_of(mine_ref[0] * share, share), share)
    total_ref[at, :] += own_ref[...]
    width = blocks_ref.shape[2]
    for i in range(blocks_ref.shape[0]):
        blocks_ref[i] = total_ref[:, i * width : (i + 1) * width].astype(BF16)


def project_backward(mine, args, tps, token):
    count = args[0].shape[0]
    heads = args[3].shape[0]
    shapes = [
        jax.ShapeDtypeStruct((tps, count, D // tps), BF16),
        jax.ShapeDtypeStruct((1, D), F32),
        jax.ShapeDtypeStruct((heads, D), F32),
    ]
    return pl.pallas_call(
        project_backward_kernel,
        grid=(1,),
        in_specs=[scalar_spec()] + [whole(a.shape) for a in args] + [anywhere()],
        out_specs=[whole(o.shape) for o in shapes],
        out_shape=shapes,
        scratch_shapes=[pltpu.VMEM((count, D), F32)],
        compiler_params=params(),
        name="project_backward",
        cost_estimate=pl.CostEstimate(
            flops=2 * count * D * 1288, bytes_accessed=6 << 20, transcendentals=count
        ),
    )(mine, *args, token)


def mixer_weight_grads_kernel(
    core_ref,
    normed_ref,
    gate_ref,
    inner_ref,
    state_ref,
    mix_ref,
    back_ref,
    token_ref,
    own_ref,
    other_ref,
):
    core = core_ref[0]
    normed = normed_ref[...]
    deep = D // GROUP
    wide = gate_ref.shape[1]
    put_halves(core, mm_tn(normed, gate_ref[...]), own_ref, other_ref, 0, deep)
    put_halves(core, mm_tn(normed, inner_ref[...]), own_ref, other_ref, deep, 2 * deep)
    rows = wide // GROUP
    mix = mix_ref[...]
    for i in range(D // wide):
        low = 2 * deep + i * rows
        grad = mm_tn(mix, back_ref[:, i * wide : (i + 1) * wide])
        put_halves(core, grad, own_ref, other_ref, low, low + rows)
    low = own_ref.shape[3] - deep // 2
    own, other = core_halves(core, mm_tn(normed, state_ref[...]).astype(BF16))
    for i in range(2):
        cols = slice(i * wide // 2, (i + 1) * wide // 2)
        rows_in = slice(i * deep // 2, (i + 1) * deep // 2)
        own_ref[:, :, 0, low:, cols] = own[:, :, rows_in]
        other_ref[:, :, 0, low:, cols] = other[:, :, rows_in]


def mixer_weight_grads(core, normed, gate, inner, state, mix, back, token):
    wide = gate.shape[1]
    deep = D // GROUP
    depth = 2 * deep + D // GROUP + deep // 2
    args = (normed, gate, inner, state, mix, back)
    return pl.pallas_call(
        mixer_weight_grads_kernel,
        grid=(1,),
        in_specs=[scalar_spec()] + [whole(a.shape) for a in args] + [anywhere()],
        out_specs=[halves_spec(depth, wide)] * 2,
        out_shape=[halves_shape(1, depth, wide)] * 2,
        compiler_params=params(),
        name="mixer_weight_grads",
        cost_estimate=pl.CostEstimate(
            flops=8 * normed.shape[0] * D * wide, bytes_accessed=8 << 20, transcendentals=0
        ),
    )(core, *args, token)


def shards(
    patches,
    byte_embed,
    seq_lengths,
    norm_global,
    proj_gate,
    proj_inner,
    proj_state,
    proj_step,
    step_bias,
    decay_log,
    conv_inner,
    conv_state,
    skip_gain,
    mixer_gain,
    proj_mixer,
    norm_attn,
    attn_input,
    attn_output,
    norm_ffn,
    expand_weight,
    shrink_weight,
    grad_output,
):
    count, quarter = patches.shape
    tps = lax.axis_size("tp")
    mine = lax.axis_index("tp")
    here = lax.axis_index(SEQ)
    core = lax.axis_index("c").reshape(1)
    tail = CONV - 1
    inner_width = proj_inner.shape[1]
    share = count // tps
    total_rows = byte_embed.shape[0]
    rows = total_rows // tps

    narrow = D // GROUP
    slot = lax.axis_index(INNER)

    def gather_weights(part):
        return lax.all_gather(part, INNER + ("tp",)).reshape((GROUP, tps) + part.shape)

    def folded(array, width):
        rows_in = array.shape[0]
        return array.reshape(rows_in, -1, width).transpose(1, 0, 2).reshape(-1, width)

    attn_in_part = lax.dynamic_slice_in_dim(attn_input, slot * narrow, narrow, 1)
    out_rows = attn_output.shape[0] // GROUP
    attn_out_part = lax.dynamic_slice_in_dim(attn_output, slot * out_rows, out_rows, 0)
    attn_out_part = folded(attn_out_part, quarter)
    hidden_width = expand_weight.shape[2]
    wide = hidden_width // PIECES
    down_rows = wide // GROUP
    ffn_parts = []
    for p in range(PIECES):
        up_part = lax.dynamic_slice(
            expand_weight, (0, slot * narrow, p * wide), (2, narrow, wide)
        )
        down_part = lax.dynamic_slice_in_dim(
            shrink_weight, p * wide + slot * down_rows, down_rows, 0
        )
        ffn_parts.append([up_part.reshape(-1, wide), folded(down_part, wide)])
    attn_parts = [
        jnp.concatenate([attn_in_part[0], attn_in_part[2]], axis=1),
        jnp.concatenate([attn_in_part[1], attn_out_part], axis=1),
    ]
    weights = gather_weights(jnp.concatenate(attn_parts + ffn_parts[0], axis=0))
    last_weights = gather_weights(jnp.concatenate(ffn_parts[1], axis=0))
    place = jnp.stack([lax.axis_index("a"), lax.axis_index("b")]).astype(jnp.int32)

    def to_rows(array):
        return lax.all_to_all(array.reshape(tps, rows, quarter), "tp", 0, 0)

    def to_columns(blocks):
        return lax.all_to_all(blocks, "tp", 0, 0).reshape(total_rows, quarter)

    positions = here * count + jnp.arange(count, dtype=jnp.int32)
    first = sequence_first(positions, seq_lengths)
    patch_rows = lax.all_gather(patches, "tp", axis=1, tiled=True)
    embed_rows = to_rows(byte_embed)
    cot_rows = to_rows(grad_output)
    global_in = patch_rows.astype(jnp.float32)
    normed = (rms_scale(global_in) * norm_global[None, :]).astype(jnp.bfloat16)
    gate_vals = product(normed, proj_gate, "rd,dc->rc")
    inner_raw = product(normed, proj_inner, "rd,dc->rc")
    state_raw = product(normed, proj_state, "rd,dc->rc")
    step_raw = product(normed, proj_step, "rd,dc->rc")
    raw = jnp.concatenate([inner_raw, state_raw], axis=1)
    before = shifted(raw[count - tail :], 1)
    padded = jnp.concatenate([before, raw], axis=0)
    conv_weight = jnp.concatenate([conv_inner, conv_state], axis=1)

    inner_vals, bmatrix, cmatrix, steps, rates = front_part(
        padded, step_raw, conv_weight, step_bias, decay_log, positions, first
    )
    carried, states = block_summary(inner_vals, bmatrix, steps, rates, positions, first)
    incoming = reached(carried, states, 1)
    mixed = block_output(
        inner_vals, bmatrix, cmatrix, steps, rates, skip_gain, incoming, positions, first
    )
    gate_act = jax.nn.silu(gate_vals)
    gated = mixed * gate_act
    squares = jnp.sum(gated * gated, axis=1, keepdims=True)
    partial = product((gated * mixer_gain[None, :]).astype(BF16), proj_mixer, "rc,cd->rd")
    square_high, square_low = high_low(jnp.broadcast_to(squares, (count, 64)))
    partial = partial + embed_rows[0, 0, 0].astype(F32) * 0.0
    sent = jnp.concatenate([partial.astype(BF16), square_high, square_low], axis=1)
    summed = jnp.sum(
        lax.all_to_all(sent.reshape(tps, share, -1), "tp", 0, 0).astype(F32), axis=0
    )
    own_squares = summed[:, D : D + 1] + summed[:, D + 64 : D + 65]
    mixer_rows = summed[:, :D] * lax.rsqrt(own_squares / DI + epsilon)
    own_patches = lax.dynamic_slice_in_dim(patch_rows, mine * share, share, 0)
    global_out = own_patches.astype(F32) + mixer_rows

    logs = jnp.cumsum(steps * rates[None, :], axis=0)
    from_before = (first < positions[0]).astype(F32)[:, None]
    reach = jnp.exp(logs) * from_before
    factor_high, factor_low = high_low(jnp.broadcast_to(carried[:, None], (carried.size, STATE)))
    factors = jnp.concatenate([factor_high, factor_low], axis=0)
    flat_inner = inner_vals.reshape(count, -1)
    flat_incoming = incoming.reshape(-1, STATE)
    keep = jnp.stack(
        [(positions - (CONV - 1 - k) >= first).astype(F32) for k in range(CONV)], axis=1
    )
    logs_row, steps_row, raw_row = logs.T, steps.T, step_raw.T
    last = (first == first[-1]).astype(F32)[:, None]
    rate_column, bias_column = rates[:, None], step_bias[:, None]
    wide_padded = jnp.pad(padded, ((8 - tail, 0), (0, 0)))
    step_weight = proj_step.T
    prepared = (
        reach, factors, keep, logs_row, steps_row, raw_row, last, rate_column, bias_column,
        wide_padded, step_weight, flat_inner, flat_incoming,
    )

    hidden, attn_in, attn_normed, qkv, context = attention_forward(
        embed_rows, global_out[:, None, :], norm_attn[None, :], weights, prepared
    )
    ffn_normed, ffn_turned, cot_whole, out_acc, normed_acc, own_first, other_first = (
        feed_forward_first(core, hidden, cot_rows, norm_ffn[None, :], weights)
    )
    first_one = reduce_first(place, own_first, other_first)
    first_two = reduce_second(place, first_one)
    layer_blocks, hidden_grad, norm_ffn_part, last_grad = feed_forward_last(
        core,
        hidden,
        cot_whole,
        norm_ffn[None, :],
        last_weights,
        ffn_normed,
        ffn_turned,
        out_acc,
        normed_acc,
        first_two[0],
    )
    layer_output = to_columns(layer_blocks)
    first_three, hidden_grad = reduce_third(first_two, hidden_grad)
    embed_blocks, own_grad, payload, norm_attn_part, own_attn, other_attn = attention_backward(
        core,
        hidden_grad,
        mixer_rows,
        attn_in,
        attn_normed,
        norm_attn[None, :],
        weights,
        qkv,
        context,
        own_squares,
        layer_output,
    )
    last_three = lax.psum_scatter(last_grad, INNER, scatter_dimension=0)
    embed_columns = to_columns(embed_blocks)
    embed_grad = embed_columns.astype(F32)

    attn_one = reduce_first(place, own_attn, other_attn)
    returned = lax.all_gather(payload, "tp", axis=0, tiled=True)
    mix_back_in = returned[:, :D]
    mix_low, gate_back, mixer_gain_grad, mixed_grad, packed = gate_backward(
        returned,
        proj_mixer,
        mixer_gain[None, :],
        gate_vals,
        mixed,
        cmatrix,
        reach,
        factors,
        attn_one[0],
    )
    attn_two = reduce_second(place, attn_one, (packed,))
    ffn_sums = tied(jnp.concatenate([first_three, last_three], axis=1), packed)
    ffn_part = reduce_last(ffn_sums)
    chunk_grads = chunk_backward(
        (
            mixed_grad,
            flat_inner,
            bmatrix,
            cmatrix,
            logs,
            logs_row,
            steps_row,
            first[:, None],
            first[None, :],
            reach,
            skip_gain[None, :],
            flat_incoming,
        ),
        attn_two[0],
        ffn_sums,
    )
    skip_gain_grad = chunk_grads[6][0]
    later_grad = reached_from(packed, -1)
    raw_grad, head_grad, conv_grad, step_back, step_bias_grad, decay_log_grad = front_backward(
        (
            later_grad,
            flat_incoming,
            flat_inner,
            bmatrix,
            logs,
            steps,
            steps_row,
            raw_row,
            last,
            carried[None, :],
            rate_column,
            bias_column,
        )
        + tuple(chunk_grads[:6])
        + (
            wide_padded,
            conv_weight,
            keep,
        ),
        attn_two[1],
    )
    step_bias_grad, decay_log_grad = step_bias_grad[:, 0], decay_log_grad[:, 0]
    tail_grad = shifted(head_grad, -1)
    raw_grad = jnp.concatenate(
        [raw_grad[: count - 8], raw_grad[count - 8 :] + tail_grad], axis=0
    ).astype(BF16)
    inner_back, state_back = raw_grad[:, :inner_width], raw_grad[:, inner_width:]
    own_mixer, other_mixer = mixer_weight_grads(
        core, normed, gate_back, inner_back, state_back, mix_low, mix_back_in, attn_two[1]
    )
    mixer_one = reduce_first(place, own_mixer, other_mixer)
    attn_three, mixer_kept = reduce_third(attn_two, mixer_one[1])
    attn_part = reduce_last(tied(attn_three, ffn_part))
    mixer_two = reduce_second(place, (mixer_one[0], mixer_kept) + tuple(mixer_one[2:]))
    mixer_three, step_back = reduce_third(mixer_two, step_back)
    mixer_three = mixer_three[0]
    mixer_part = over_groups(mixer_three)
    state_rows = lax.all_gather(mixer_part[3 * narrow :], "tp")
    state_rows = jnp.sum(state_rows.astype(F32), axis=0).astype(BF16)
    columns, norm_global_part, step_grad = project_backward(
        mine.reshape(1),
        (
            gate_back,
            inner_back,
            state_back,
            step_back,
            proj_gate,
            proj_inner,
            proj_state,
            step_weight,
            patch_rows,
            normed,
            norm_global[None, :],
            own_grad,
        ),
        tps,
        state_rows,
    )
    norm_global_part = norm_global_part[0]
    shared = jnp.concatenate(
        [
            conv_grad[:, inner_width:].reshape(-1),
            norm_attn_part[0],
            norm_ffn_part[0],
            norm_global_part,
        ]
    ).reshape(-1, quarter)
    shared_high, shared_low = high_low(shared)
    shared_rows = jnp.concatenate([shared_high, shared_low], axis=0)
    returned = lax.all_to_all(
        jnp.concatenate(
            [columns, jnp.broadcast_to(shared_rows[None], (tps,) + shared_rows.shape)], axis=1
        ),
        "tp",
        0,
        0,
    )
    returned = jnp.sum(returned.astype(F32), axis=0)
    patch_grad = returned[:count]
    shared = returned[count : count + shared.shape[0]] + returned[count + shared.shape[0] :]
    shared = shared.reshape(-1)
    held = conv_state.size
    shared = (
        shared[:held].reshape(conv_state.shape),
        shared[held : held + D],
        shared[held + D : held + 2 * D],
        shared[held + 2 * D :],
    )
    (
        conv_state_grad,
        norm_attn_grad,
        norm_ffn_grad,
        norm_global_grad,
        proj_step_grad,
        step_bias_grad,
        decay_log_grad,
        conv_inner_grad,
        skip_gain_grad,
        mixer_gain_grad,
    ) = lax.psum(
        shared
        + (
            step_grad.T,
            step_bias_grad,
            decay_log_grad,
            conv_grad[:, :inner_width],
            skip_gain_grad,
            mixer_gain_grad[0],
        ),
        SEQ,
    )
    ffn_depth, attn_depth = 3 * narrow, 2 * narrow
    all_grads = lax.all_gather(
        jnp.concatenate([ffn_part, attn_part, mixer_part[: 3 * narrow], state_rows]), INNER
    )
    (
        expand_grad,
        shrink_grad,
        attn_input_grad,
        attn_output_grad,
        proj_gate_grad,
        proj_inner_grad,
        proj_mixer_grad,
        proj_state_grad,
    ) = unpack(all_grads, tps)
    return (
        layer_output,
        embed_grad,
        patch_grad,
        norm_global_grad,
        proj_gate_grad,
        proj_inner_grad,
        proj_state_grad,
        proj_step_grad,
        step_bias_grad,
        decay_log_grad,
        conv_inner_grad,
        conv_state_grad,
        skip_gain_grad,
        mixer_gain_grad,
        proj_mixer_grad,
        norm_attn_grad,
        attn_input_grad,
        attn_output_grad,
        norm_ffn_grad,
        expand_grad,
        shrink_grad,
    )


def solution(mesh):
    seq, tps = mesh.shape["seq"], mesh.shape["tp"]
    fine = Mesh(mesh.devices.reshape(seq // GROUP, 2, 2, 2, tps), SEQ + ("tp",))
    rows_cols = P(SEQ, "tp")
    last = P(None, "tp")
    lead = P("tp", None)
    return jax.shard_map(
        shards,
        mesh=fine,
        in_specs=(
            rows_cols,
            rows_cols,
            P(),
            P(),
            last,
            last,
            P(),
            last,
            P("tp"),
            P("tp"),
            last,
            P(),
            P("tp"),
            P("tp"),
            lead,
            P(),
            P(None, None, "tp"),
            lead,
            P(),
            P(None, None, "tp"),
            lead,
            rows_cols,
        ),
        out_specs=(
            rows_cols,
            rows_cols,
            rows_cols,
            P(),
            last,
            last,
            P(),
            last,
            P("tp"),
            P("tp"),
            last,
            P(),
            P("tp"),
            P("tp"),
            lead,
            P(),
            P(None, None, "tp"),
            lead,
            P(),
            P(None, None, "tp"),
            lead,
        ),
        check_vma=False,
    )
```

```python
import functools

import jax
import jax.numpy as jnp
from jax import lax
from jax.experimental import pallas as pl
from jax.experimental.pallas import tpu as pltpu
from jax.sharding import Mesh, PartitionSpec as P

D = 1024
HEAD_DIM = 64
STATE = 128
HEADS_A = 16
CONV = 4
PATCH = 8
DI = 2048
GROUP = 8
TILE = 128
PIECES = 2

epsilon = 1e-05
highest = lax.Precision.HIGHEST
F32 = jnp.float32
BF16 = jnp.bfloat16
SEQ = ("g", "a", "b", "c")
INNER = ("a", "b", "c")


def mm(left, right):
    return lax.dot_general(left, right, (((1,), (0,)), ((), ())), preferred_element_type=F32)


def mm_nt(left, right):
    return lax.dot_general(left, right, (((1,), (1,)), ((), ())), preferred_element_type=F32)


def mm_tn(left, right):
    return lax.dot_general(left, right, (((0,), (0,)), ((), ())), preferred_element_type=F32)


def inverse_rms(values):
    return lax.rsqrt(jnp.mean(values * values, axis=-1, keepdims=True) + epsilon)


def params(limit=60):
    return pltpu.CompilerParams(
        dimension_semantics=("arbitrary",), vmem_limit_bytes=limit * 1024 * 1024
    )


def whole(shape):
    return pl.BlockSpec(shape, lambda j: (0,) * len(shape))


def scalar_spec():
    return pl.BlockSpec(memory_space=pltpu.SMEM)


def halves_shape(tps, depth, wide):
    return jax.ShapeDtypeStruct((2, 2, tps, depth, wide), BF16)


def halves_spec(depth, wide):
    return pl.BlockSpec((2, 2, 1, depth, wide), lambda j: (0, 0, j, 0, 0))


def anywhere():
    return pl.BlockSpec(memory_space=pl.ANY)


def weight_specs(weights, first):
    parts, _, _, wide = weights.shape
    block = (parts, 1, D // GROUP, wide)
    return [
        pl.BlockSpec(block, functools.partial(lambda k, j: (0, j, k, 0), first + k))
        for k in range(3)
    ]


def attention_spec(weights):
    parts, _, _, wide = weights.shape
    return pl.BlockSpec((parts, 1, 2 * D // GROUP, wide), lambda j: (0, j, 0, 0))


def attention_view(weight_ref, k, width):
    deep = D // weight_ref.shape[0]
    rows = slice((k % 2) * deep, (k % 2 + 1) * deep)
    return weight_ref.at[:, 0, rows, (k // 2) * width : (k // 2 + 1) * width]


def head_mask(width):
    lane = lax.broadcasted_iota(jnp.int32, (1, width), 1) // (D // HEADS_A)
    return [lane == h for h in range(width // (D // HEADS_A))]


def split_heads(tile, masks):
    zero = jnp.zeros_like(tile)
    return jnp.concatenate([jnp.where(m, tile, zero) for m in masks], axis=0)


def tile_mask(heads):
    row = lax.broadcasted_iota(jnp.int32, (heads * TILE, TILE), 0) % TILE
    col = lax.broadcasted_iota(jnp.int32, (heads * TILE, TILE), 1)
    return (row // PATCH == col // PATCH) & (col <= row)


def tile_probs(query_split, keys, keep):
    scores = mm_nt(query_split, keys) * ((D // HEADS_A) ** -0.5)
    scores = jnp.where(keep, scores, -1e30)
    expo = jnp.exp(scores - jnp.max(scores, axis=-1, keepdims=True))
    return expo / jnp.sum(expo, axis=-1, keepdims=True)


def beside(stacked, heads):
    return jnp.concatenate([stacked[h * TILE : (h + 1) * TILE] for h in range(heads)], axis=1)


def attention_forward_kernel(
    embed_ref, global_ref, gain_ref, weight_ref, *refs
):
    hidden_ref, input_ref, normed_ref, qkv_ref, context_ref = refs[-5:]
    step = pl.program_id(0)
    blocks, rows, width = embed_ref.shape
    parts = weight_ref.shape[0]

    @pl.when(step == 0)
    def _():
        embed = jnp.concatenate([embed_ref[i] for i in range(blocks)], axis=1).astype(F32)
        spread = jnp.broadcast_to(global_ref[...], (rows // PATCH, PATCH, D)).reshape(rows, D)
        total = embed + spread
        hidden_ref[...] = total
        low = total.astype(BF16)
        input_ref[...] = low
        values = low.astype(F32)
        normed_ref[...] = (values * inverse_rms(values) * gain_ref[...]).astype(BF16)

    normed = normed_ref[...]
    for k in range(3):
        weight = attention_view(weight_ref, k, width)[...].reshape(D, width)
        qkv_ref[0, k] = mm(normed, weight).astype(BF16)
    masks = head_mask(width)
    heads = len(masks)
    keep = tile_mask(heads)
    for r in range(rows // TILE):
        at = slice(r * TILE, (r + 1) * TILE)
        query = split_heads(qkv_ref[0, 0, at], masks)
        probs = tile_probs(query, qkv_ref[0, 1, at], keep).astype(BF16)
        values = split_heads(qkv_ref[0, 2, at], masks)
        context_ref[0, at] = mm(beside(probs, heads), values).astype(BF16)
    context = context_ref[0]
    piece = width // parts
    outward = attention_view(weight_ref, 3, width)
    for c in range(D // width):
        weight = outward[:, c * piece : (c + 1) * piece].reshape(width, width)
        cols = slice(c * width, (c + 1) * width)
        hidden_ref[:, cols] += mm(context, weight)


def attention_forward(embed, global_rows, gain, weights, tokens):
    blocks, rows, width = embed.shape
    tps = weights.shape[1]
    return pl.pallas_call(
        attention_forward_kernel,
        grid=(tps,),
        in_specs=[
            whole((blocks, rows, width)),
            whole((rows // PATCH, 1, D)),
            whole((1, D)),
            attention_spec(weights),
            *(anywhere() for _ in tokens),
        ],
        out_specs=[
            whole((rows, D)),
            whole((rows, D)),
            whole((rows, D)),
            pl.BlockSpec((1, 3, rows, width), lambda j: (j, 0, 0, 0)),
            pl.BlockSpec((1, rows, width), lambda j: (j, 0, 0)),
        ],
        out_shape=[
            jax.ShapeDtypeStruct((rows, D), F32),
            jax.ShapeDtypeStruct((rows, D), BF16),
            jax.ShapeDtypeStruct((rows, D), BF16),
            jax.ShapeDtypeStruct((tps, 3, rows, width), BF16),
            jax.ShapeDtypeStruct((tps, rows, width), BF16),
        ],
        compiler_params=params(),
        name="attention_forward",
        cost_estimate=pl.CostEstimate(
            flops=2 * rows * D * D * 4, bytes_accessed=14 << 20, transcendentals=rows * 2048
        ),
    )(embed, global_rows, gain, weights, *tokens)


def core_halves(core, grad):
    parts = grad.reshape((2, 2, 2, grad.shape[0] // GROUP) + grad.shape[1:])
    mine = jnp.where(core == 0, parts[:, :, 0], parts[:, :, 1])
    other = jnp.where(core == 0, parts[:, :, 1], parts[:, :, 0])
    return mine, other


def put_halves(core, grad, own_ref, other_ref, low, high, cols=slice(None)):
    own, other = core_halves(core, grad.astype(BF16))
    own_ref[:, :, 0, low:high, cols] = own
    other_ref[:, :, 0, low:high, cols] = other


def put_whole(core, grad, grad_ref, low, high):
    parts = grad_ref.shape[0]
    grad_ref[:, 0, low:high] = grad.astype(BF16).reshape((parts, -1) + grad.shape[1:])


def feed_forward_step(
    core_ref, weight_refs, cot, normed_ref, turned_ref, out_acc, normed_acc, put
):
    parts, _, _, wide = weight_refs[0].shape
    deep = D // parts
    core = core_ref[0]
    normed = normed_ref[...]
    gate_weight = weight_refs[0][:, 0].reshape(D, wide)
    up_weight = weight_refs[1][:, 0].reshape(D, wide)
    piece = wide // parts
    folds = D // wide
    down_weight = jnp.concatenate(
        [
            weight_refs[2][:, 0, i * piece : (i + 1) * piece].reshape(wide, wide)
            for i in range(folds)
        ],
        axis=1,
    )
    gate = mm(normed, gate_weight)
    up = mm(normed, up_weight)
    sigma = 1.0 / (1.0 + jnp.exp(-gate))
    swish = gate * sigma
    activ = (swish * up).astype(BF16)
    out_acc[...] += mm(activ, down_weight)
    shrink = mm_tn(activ, cot)
    for i in range(folds):
        low = 2 * deep + i * piece
        put(core, shrink[:, i * wide : (i + 1) * wide], low, low + piece)
    dactiv = mm_nt(cot, down_weight)
    dgate = (dactiv * up * sigma * (1.0 + gate * (1.0 - sigma))).astype(BF16)
    dup = (dactiv * swish).astype(BF16)
    normed_acc[...] += mm_nt(dgate, gate_weight) + mm_nt(dup, up_weight)
    turned = turned_ref[...]
    put(core, mm(turned, dgate), 0, deep)
    put(core, mm(turned, dup), deep, 2 * deep)


def feed_forward_first_kernel(
    core_ref,
    hidden_ref,
    cot_ref,
    gain_ref,
    gate_ref,
    up_ref,
    down_ref,
    normed_ref,
    turned_ref,
    cot_out,
    out_acc,
    normed_acc,
    own_ref,
    other_ref,
):
    blocks, _, width = cot_ref.shape

    @pl.when(pl.program_id(0) == 0)
    def _():
        values = hidden_ref[...].astype(BF16).astype(F32)
        normed = (values * inverse_rms(values) * gain_ref[...]).astype(BF16)
        normed_ref[...] = normed
        turned_ref[...] = normed.astype(F32).T.astype(BF16)
        for i in range(blocks):
            cot_out[:, i * width : (i + 1) * width] = cot_ref[i]
        out_acc[...] = hidden_ref[...]
        normed_acc[...] = jnp.zeros_like(normed_acc)

    def put(core, grad, low, high):
        put_halves(core, grad, own_ref, other_ref, low, high)

    feed_forward_step(
        core_ref,
        (gate_ref, up_ref, down_ref),
        cot_out[...],
        normed_ref,
        turned_ref,
        out_acc,
        normed_acc,
        put,
    )


def feed_forward_last_kernel(
    core_ref,
    hidden_ref,
    cot_ref,
    gain_ref,
    gate_ref,
    up_ref,
    down_ref,
    normed_ref,
    turned_ref,
    out_in,
    normed_in,
    token_ref,
    layer_ref,
    grad_ref,
    gain_grad_ref,
    weight_grad_ref,
    out_acc,
    normed_acc,
):
    step = pl.program_id(0)
    blocks, _, width = layer_ref.shape

    @pl.when(step == 0)
    def _():
        out_acc[...] = out_in[...]
        normed_acc[...] = normed_in[...]

    def put(core, grad, low, high):
        put_whole(core, grad, weight_grad_ref, low, high)

    feed_forward_step(
        core_ref,
        (gate_ref, up_ref, down_ref),
        cot_ref[...],
        normed_ref,
        turned_ref,
        out_acc,
        normed_acc,
        put,
    )

    @pl.when(step == pl.num_programs(0) - 1)
    def _():
        layer = out_acc[...].astype(BF16)
        for i in range(blocks):
            layer_ref[i] = layer[:, i * width : (i + 1) * width]
        values = hidden_ref[...].astype(BF16).astype(F32)
        scale = inverse_rms(values)
        normal = values * scale
        grad = normed_acc[...]
        gain_grad_ref[...] = jnp.sum(grad * normal, axis=0, keepdims=True)
        scaled = grad * gain_ref[...]
        back = scale * (scaled - normal * jnp.mean(scaled * normal, axis=-1, keepdims=True))
        grad_ref[...] = cot_ref[...].astype(F32) + back


def feed_forward_cost(rows, weights):
    _, tps, _, wide = weights.shape
    return pl.CostEstimate(
        flops=18 * rows * D * wide * tps,
        bytes_accessed=12 * D * wide * tps + 16 * rows * D,
        transcendentals=rows * wide * tps,
    )


def feed_forward_first(core, hidden, cot, gain, weights):
    rows = hidden.shape[0]
    _, tps, _, wide = weights.shape
    depth = 3 * D // GROUP
    return pl.pallas_call(
        feed_forward_first_kernel,
        grid=(tps,),
        in_specs=[
            scalar_spec(),
            whole((rows, D)),
            whole(cot.shape),
            whole((1, D)),
            *weight_specs(weights, 2),
        ],
        out_specs=[
            whole((rows, D)),
            whole((D, rows)),
            whole((rows, D)),
            whole((rows, D)),
            whole((rows, D)),
            halves_spec(depth, wide),
            halves_spec(depth, wide),
        ],
        out_shape=[
            jax.ShapeDtypeStruct((rows, D), BF16),
            jax.ShapeDtypeStruct((D, rows), BF16),
            jax.ShapeDtypeStruct((rows, D), BF16),
            jax.ShapeDtypeStruct((rows, D), F32),
            jax.ShapeDtypeStruct((rows, D), F32),
            halves_shape(tps, depth, wide),
            halves_shape(tps, depth, wide),
        ],
        compiler_params=params(),
        name="feed_forward_first",
        cost_estimate=feed_forward_cost(rows, weights),
    )(core, hidden, cot, gain, weights, weights, weights)


def feed_forward_last(
    core, hidden, cot, gain, weights, normed, turned, out_in, normed_in, token
):
    rows = hidden.shape[0]
    _, tps, _, wide = weights.shape
    depth = 3 * D // GROUP
    width = D // tps
    return pl.pallas_call(
        feed_forward_last_kernel,
        grid=(tps,),
        in_specs=[
            scalar_spec(),
            whole((rows, D)),
            whole((rows, D)),
            whole((1, D)),
            *weight_specs(weights, 0),
            whole((rows, D)),
            whole((D, rows)),
            whole((rows, D)),
            whole((rows, D)),
            anywhere(),
        ],
        out_specs=[
            whole((tps, rows, width)),
            whole((rows, D)),
            whole((1, D)),
            pl.BlockSpec((GROUP, 1, depth, wide), lambda j: (0, j, 0, 0)),
        ],
        out_shape=[
            jax.ShapeDtypeStruct((tps, rows, width), BF16),
            jax.ShapeDtypeStruct((rows, D), F32),
            jax.ShapeDtypeStruct((1, D), F32),
            jax.ShapeDtypeStruct((GROUP, tps, depth, wide), BF16),
        ],
        scratch_shapes=[pltpu.VMEM((rows, D), F32), pltpu.VMEM((rows, D), F32)],
        compiler_params=params(),
        name="feed_forward_last",
        cost_estimate=feed_forward_cost(rows, weights),
    )(core, hidden, cot, gain, weights, weights, weights, normed, turned, out_in, normed_in, token)


def attention_backward_kernel(
    core_ref,
    grad_ref,
    mixer_ref,
    input_ref,
    normed_ref,
    gain_ref,
    weight_ref,
    qkv_ref,
    context_ref,
    squares_ref,
    token_ref,
    embed_ref,
    global_ref,
    payload_ref,
    gain_grad_ref,
    own_ref,
    other_ref,
    turned_ref,
    low_ref,
    normed_acc,
    context_grad_ref,
    qkv_grad_ref,
):
    step = pl.program_id(0)
    rows = grad_ref.shape[0]
    blocks, _, width = embed_ref.shape
    parts = weight_ref.shape[0]
    deep = D // parts
    scaling = (D // HEADS_A) ** -0.5
    core = core_ref[0]

    @pl.when(step == 0)
    def _():
        turned_ref[...] = normed_ref[...].astype(F32).T.astype(BF16)
        low_ref[...] = grad_ref[...].astype(BF16)
        normed_acc[...] = jnp.zeros_like(normed_acc)

    low = low_ref[...]
    context = context_ref[0]
    piece = width // parts
    total = jnp.zeros((rows, width), F32)
    outward = attention_view(weight_ref, 3, width)
    for c in range(D // width):
        first = deep + c * piece
        weight = outward[:, c * piece : (c + 1) * piece].reshape(width, width)
        columns = low[:, c * width : (c + 1) * width]
        total = total + mm_nt(columns, weight)
        put_halves(
            core,
            mm_tn(context, columns),
            own_ref,
            other_ref,
            first,
            first + piece,
            slice(width, 2 * width),
        )
    context_grad_ref[...] = total.astype(BF16)
    masks = head_mask(width)
    heads = len(masks)
    keep = tile_mask(heads)
    for r in range(rows // TILE):
        at = slice(r * TILE, (r + 1) * TILE)
        query = split_heads(qkv_ref[0, 0, at], masks)
        keys = qkv_ref[0, 1, at]
        probs = tile_probs(query, keys, keep)
        dcontext = split_heads(context_grad_ref[at], masks)
        dprobs = mm_nt(dcontext, qkv_ref[0, 2, at])
        dvalues = mm_tn(probs.astype(BF16), dcontext)
        inner = jnp.sum(dprobs * probs, axis=-1, keepdims=True)
        dscores = (probs * (dprobs - inner)).astype(BF16)
        dquery = mm(beside(dscores, heads), split_heads(keys, masks)) * scaling
        dkeys = mm_tn(dscores, query) * scaling
        qkv_grad_ref[at, :width] = dquery.astype(BF16)
        qkv_grad_ref[at, width : 2 * width] = dkeys.astype(BF16)
        qkv_grad_ref[at, 2 * width :] = dvalues.astype(BF16)
    turned = turned_ref[...]
    for k in range(3):
        part = qkv_grad_ref[:, k * width : (k + 1) * width]
        weight = attention_view(weight_ref, k, width)[...].reshape(D, width)
        normed_acc[...] += mm_nt(part, weight)
        first = (k % 2) * deep
        put_halves(
            core,
            mm(turned, part),
            own_ref,
            other_ref,
            first,
            first + deep,
            slice((k // 2) * width, (k // 2 + 1) * width),
        )

    @pl.when(step == pl.num_programs(0) - 1)
    def _():
        values = input_ref[...].astype(F32)
        scale = inverse_rms(values)
        normal = values * scale
        grad = normed_acc[...]
        gain_grad_ref[...] = jnp.sum(grad * normal, axis=0, keepdims=True)
        scaled = grad * gain_ref[...]
        back = scale * (scaled - normal * jnp.mean(scaled * normal, axis=-1, keepdims=True))
        result = grad_ref[...] + back
        for i in range(blocks):
            embed_ref[i] = result[:, i * width : (i + 1) * width].astype(BF16)
        patch = jnp.sum(result.reshape(rows // PATCH, PATCH, D), axis=1)
        global_ref[...] = patch
        dots = jnp.sum(patch * mixer_ref[...], axis=1, keepdims=True)
        payload_ref[:, :D] = patch.astype(BF16)
        lane = lax.broadcasted_iota(jnp.int32, (patch.shape[0], 128), 1)
        values = jnp.where(lane % 64 < 32, squares_ref[...], dots)
        high = values.astype(BF16).astype(F32)
        payload_ref[:, D:] = jnp.where(lane < 64, high, values - high).astype(BF16)


def attention_backward(core, grad, mixer_rows, inputs, normed, gain, weights, qkv, context, squares, token):
    rows = grad.shape[0]
    tps, _, width = context.shape
    depth = 2 * D // GROUP
    return pl.pallas_call(
        attention_backward_kernel,
        grid=(tps,),
        in_specs=[
            scalar_spec(),
            whole((rows, D)),
            whole((rows // PATCH, D)),
            whole((rows, D)),
            whole((rows, D)),
            whole((1, D)),
            attention_spec(weights),
            pl.BlockSpec((1, 3, rows, width), lambda j: (j, 0, 0, 0)),
            pl.BlockSpec((1, rows, width), lambda j: (j, 0, 0)),
            whole(squares.shape),
            anywhere(),
        ],
        out_specs=[
            whole((tps, rows, width)),
            whole((rows // PATCH, D)),
            whole((rows // PATCH, D + 128)),
            whole((1, D)),
            halves_spec(depth, 2 * width),
            halves_spec(depth, 2 * width),
        ],
        out_shape=[
            jax.ShapeDtypeStruct((tps, rows, width), BF16),
            jax.ShapeDtypeStruct((rows // PATCH, D), F32),
            jax.ShapeDtypeStruct((rows // PATCH, D + 128), BF16),
            jax.ShapeDtypeStruct((1, D), F32),
            halves_shape(tps, depth, 2 * width),
            halves_shape(tps, depth, 2 * width),
        ],
        scratch_shapes=[
            pltpu.VMEM((D, rows), BF16),
            pltpu.VMEM((rows, D), BF16),
            pltpu.VMEM((rows, D), F32),
            pltpu.VMEM((rows, width), BF16),
            pltpu.VMEM((rows, 3 * width), BF16),
        ],
        compiler_params=params(),
        name="attention_backward",
        cost_estimate=pl.CostEstimate(
            flops=4 * rows * D * D * 4, bytes_accessed=26 << 20, transcendentals=rows * 2048
        ),
    )(core, grad, mixer_rows, inputs, normed, gain, weights, qkv, context, squares, token)


def shifted(block, distance):
    devices = range(lax.axis_size(SEQ))
    route = [(i - distance, i) for i in devices if i - distance in devices]
    return lax.ppermute(block, SEQ, route)


def rms_scale(values):
    return values * inverse_rms(values)


def sequence_first(positions, lengths):
    offsets = jnp.cumsum(lengths) - lengths
    chosen = jnp.where(offsets[None, :] <= positions[:, None], offsets[None, :], 0)
    return jnp.max(chosen, axis=1)


def causal_conv(padded, weight, positions, first):
    count = positions.shape[0]
    total = jnp.zeros((count, padded.shape[1]), jnp.float32)
    for offset in range(CONV):
        lag = CONV - 1 - offset
        keep = (positions - lag >= first).astype(jnp.float32)[:, None]
        total = total + weight[offset][None, :] * padded[offset : offset + count] * keep
    return total


def front_part(padded, step_raw, conv_weight, step_bias, decay_log, positions, first):
    activated = jax.nn.silu(causal_conv(padded, conv_weight, positions, first))
    inner = activated.shape[1] - 2 * STATE
    count = positions.shape[0]
    inner_vals = activated[:, :inner].reshape(count, inner // HEAD_DIM, HEAD_DIM)
    bmatrix = activated[:, inner : inner + STATE]
    cmatrix = activated[:, inner + STATE :]
    steps = jax.nn.softplus(step_raw + step_bias[None, :])
    rates = -jnp.exp(decay_log)
    return (inner_vals, bmatrix, cmatrix, steps, rates)


def block_summary(inner_vals, bmatrix, steps, rates, positions, first):
    logs = jnp.cumsum(steps * rates[None, :], axis=0)
    final = logs[-1]
    in_last = (first == first[-1]).astype(jnp.float32)[:, None]
    weights = jnp.exp(final[None, :] - logs) * in_last * steps
    carried = jnp.exp(final) * (first[-1] < positions[0]).astype(jnp.float32)
    states = jnp.einsum("sh,shp,sn->hpn", weights, inner_vals, bmatrix, precision=highest)
    return (carried, states)


def block_output(inner_vals, bmatrix, cmatrix, steps, rates, skip_gain, incoming, positions, first):
    logs = jnp.cumsum(steps * rates[None, :], axis=0)
    count = positions.shape[0]
    same = (first[:, None] == first[None, :]) & (positions[None, :] <= positions[:, None])
    diff = logs.T[:, :, None] - logs.T[:, None, :]
    decay = jnp.where(same[None], jnp.exp(jnp.where(same[None], diff, 0.0)), 0.0)
    inner_prod = jnp.dot(cmatrix, bmatrix.T, precision=highest, preferred_element_type=jnp.float32)
    mixing = decay * inner_prod[None] * steps.T[:, None, :]
    within = jnp.einsum("hts,shp->thp", mixing, inner_vals, precision=highest)
    carry = jnp.exp(logs) * (first < positions[0]).astype(jnp.float32)[:, None]
    remote = jnp.einsum("tn,hpn->thp", cmatrix, incoming, precision=highest) * carry[:, :, None]
    result = within + remote + skip_gain[None, :, None] * inner_vals
    return result.reshape(count, -1)


def product(left, right, form):
    return jnp.einsum(form, left, right, preferred_element_type=jnp.float32)


def norm_backward(grad, values, gain):
    scale = inverse_rms(values)
    normed = values * scale
    scaled = grad * gain[None, :]
    result = scale * (scaled - normed * jnp.mean(scaled * normed, axis=-1, keepdims=True))
    return (result, jnp.sum(grad * normed, axis=0))


def high_low(values):
    high = values.astype(BF16)
    low = (values - high.astype(F32)).astype(BF16)
    return high, low


def reached(factors, states, distance):
    heads = factors.shape[0]
    columns = jnp.broadcast_to(factors[:, None], (heads, STATE))
    high, low = high_low(columns)
    packed = jnp.concatenate([states.reshape(-1, STATE).astype(BF16), high, low], axis=0)
    return reached_from(packed, distance).reshape(states.shape)


def reached_from(packed, distance):
    count = lax.axis_size(SEQ)
    heads = packed.shape[0] // (HEAD_DIM + 2)
    total = jnp.zeros((heads, HEAD_DIM, STATE), F32)
    chain = jnp.ones((heads, 1, 1), F32)
    for hop in range(1, count // 2 + 1):
        step = hop * distance
        route = [(i, i + step) for i in range(count) if 0 <= i + step < count]
        got = lax.ppermute(packed, SEQ, route).astype(F32)
        total = total + chain * got[: -2 * heads].reshape(total.shape)
        factor = (got[-2 * heads : -heads] + got[-heads:])[:, :1]
        chain = chain * factor[:, :, None]
    return total.reshape(-1, STATE)


def tied(array, *tokens):
    zero = sum(t[(0,) * t.ndim].astype(F32) * 0.0 for t in tokens)
    return (array.astype(F32) + zero).astype(array.dtype)


def swap(array, axis):
    return lax.ppermute(array, axis, [(0, 1), (1, 0)])


def picked(array, axis, index):
    return lax.dynamic_index_in_dim(array, index, axis, False)


def parallel_params(axes):
    return pltpu.CompilerParams(
        dimension_semantics=("arbitrary",) * axes, vmem_limit_bytes=32 * 1024 * 1024
    )


def first_sum_kernel(place_ref, *refs):
    ins, outs = refs[:8], refs[-4:]
    for k in range(4):
        total = ins[2 * k][...].astype(F32) + ins[2 * k + 1][...].astype(F32)
        outs[k][...] = total.reshape(outs[k].shape).astype(BF16)


def first_sum(place, own, got, tokens=()):
    _, _, tps, rows, cols = own.shape
    half = rows // 2
    block = (1, 1, 1, half, cols)
    maps = [
        lambda t, i, p: (i, 1 - p[1], t, 0, 0),
        lambda t, i, p: (i, p[1], t, 0, 0),
        lambda t, i, p: (1 - p[0], i, t, 1, 0),
        lambda t, i, p: (p[0], i, t, 1, 0),
    ]
    specs = [pl.BlockSpec(block, m) for m in maps for _ in range(2)]
    return pl.pallas_call(
        first_sum_kernel,
        grid_spec=pltpu.PrefetchScalarGridSpec(
            num_scalar_prefetch=1,
            grid=(tps, 2),
            in_specs=specs + [anywhere() for _ in tokens],
            out_specs=[
                pl.BlockSpec((1, 1, half, cols), lambda t, i, p: (i, t, 0, 0)) for _ in range(4)
            ],
        ),
        out_shape=[jax.ShapeDtypeStruct((2, tps, half, cols), BF16) for _ in range(4)],
        compiler_params=parallel_params(2),
        name="first_sum",
        cost_estimate=pl.CostEstimate(
            flops=own.size, bytes_accessed=6 * own.size, transcendentals=0
        ),
    )(place, *([own, got] * 4), *tokens)


def second_sum_kernel(place_ref, *refs):
    ins, outs = refs[:8], refs[-4:]
    for k in range(4):
        total = ins[2 * k][...].astype(F32) + ins[2 * k + 1][...].astype(F32)
        outs[k][...] = total.reshape(outs[k].shape).astype(BF16)


def second_sum(place, kept_one, got_one, kept_two, got_two, tokens=()):
    _, tps, half, cols = kept_one.shape
    block = (1, 1, half, cols)
    maps = [
        lambda t, p: (1 - p[0], t, 0, 0),
        lambda t, p: (p[0], t, 0, 0),
        lambda t, p: (1 - p[1], t, 0, 0),
        lambda t, p: (p[1], t, 0, 0),
    ]
    return pl.pallas_call(
        second_sum_kernel,
        grid_spec=pltpu.PrefetchScalarGridSpec(
            num_scalar_prefetch=1,
            grid=(tps,),
            in_specs=[pl.BlockSpec(block, m) for m in maps for _ in range(2)]
            + [anywhere() for _ in tokens],
            out_specs=[pl.BlockSpec((1, half, cols), lambda t, p: (t, 0, 0)) for _ in range(4)],
        ),
        out_shape=[jax.ShapeDtypeStruct((tps, half, cols), BF16) for _ in range(4)],
        compiler_params=parallel_params(1),
        name="second_sum",
        cost_estimate=pl.CostEstimate(
            flops=2 * kept_one.size, bytes_accessed=12 * kept_one.size, transcendentals=0
        ),
    )(place, *([kept_one, got_one] * 2), *([kept_two, got_two] * 2), *tokens)


def third_sum_kernel(one_ref, two_ref, three_ref, four_ref, *refs):
    out_ref = refs[-2]
    half = one_ref.shape[1]
    out_ref[0, :half] = (one_ref[0].astype(F32) + two_ref[0].astype(F32)).astype(BF16)
    out_ref[0, half:] = (three_ref[0].astype(F32) + four_ref[0].astype(F32)).astype(BF16)


def third_sum(kept_one, got_one, kept_two, got_two, carried):
    tps, half, cols = kept_one.shape
    return pl.pallas_call(
        third_sum_kernel,
        grid=(tps,),
        in_specs=[pl.BlockSpec((1, half, cols), lambda t: (t, 0, 0)) for _ in range(4)]
        + [anywhere()],
        out_specs=[pl.BlockSpec((1, 2 * half, cols), lambda t: (t, 0, 0)), anywhere()],
        out_shape=[
            jax.ShapeDtypeStruct((tps, 2 * half, cols), BF16),
            jax.ShapeDtypeStruct(carried.shape, carried.dtype),
        ],
        input_output_aliases={4: 1},
        compiler_params=parallel_params(1),
        name="third_sum",
        cost_estimate=pl.CostEstimate(
            flops=2 * kept_one.size, bytes_accessed=12 * kept_one.size, transcendentals=0
        ),
    )(kept_one, got_one, kept_two, got_two, carried)


def reduce_first(place, own, other, tokens=()):
    return first_sum(place, own, swap(other, "c"), tokens)


def reduce_second(place, sums, tokens=()):
    send_one, keep_one, send_two, keep_two = sums
    return second_sum(
        place, keep_one, swap(send_one, "b"), keep_two, swap(send_two, "a"), tokens
    )


def reduce_third(sums, carried):
    send_one, keep_one, send_two, keep_two = sums
    return third_sum(keep_one, swap(send_one, "a"), keep_two, swap(send_two, "b"), carried)


def over_groups(part):
    return lax.psum(part, "g") if lax.axis_size("g") > 1 else part


def reduce_last(summed):
    return over_groups(lax.psum_scatter(summed, "tp", scatter_dimension=0))


def exchange_last(summed):
    pieces = lax.all_to_all(summed, "tp", 0, 0)
    return over_groups(jnp.sum(pieces.astype(F32), axis=0).astype(BF16))


def unpack_kernel(
    grads_ref,
    expand_ref,
    shrink_ref,
    input_ref,
    output_ref,
    gate_ref,
    inner_ref,
    mixer_ref,
    state_ref,
):
    wide = grads_ref.shape[2]
    deep = D // GROUP
    width = input_ref.shape[2]

    def rows(low, count):
        return grads_ref[0, low : low + count].astype(F32)

    down = wide // GROUP
    for p in range(PIECES):
        base = 3 * deep * p
        for i in range(2):
            expand_ref[i, :, p * wide : (p + 1) * wide] = rows(base + i * deep, deep)
        for i in range(D // wide):
            shrink_ref[p, 0, :, i * wide : (i + 1) * wide] = rows(base + 2 * deep + i * down, down)
    base = 3 * deep * PIECES
    for k in range(3):
        part = rows(base + (k % 2) * deep, deep)
        input_ref[k] = part[:, (k // 2) * width : (k // 2 + 1) * width]
    part = rows(base + deep, deep)[:, width:]
    out_rows = width // GROUP
    for i in range(D // width):
        output_ref[:, i * width : (i + 1) * width] = part[i * out_rows : (i + 1) * out_rows]
    base = base + 2 * deep
    gate_ref[...] = rows(base, deep)
    inner_ref[...] = rows(base + deep, deep)
    for i in range(D // wide):
        mixer_ref[:, i * wide : (i + 1) * wide] = rows(base + 2 * deep + i * down, down)
    state = rows(base + 3 * deep, deep // 2)
    half = wide // 2
    for i in range(2):
        state_ref[i * deep // 2 : (i + 1) * deep // 2] = state[:, i * half : (i + 1) * half]


def unpack(grads, tps):
    _, total, wide = grads.shape
    deep, width, down = D // GROUP, D // tps, wide // GROUP
    shapes = [
        (2, D, PIECES * wide),
        (PIECES, GROUP, down, D),
        (3, D, width),
        (width, D),
        (D, wide),
        (D, wide),
        (wide, D),
        (D, wide // 2),
    ]
    specs = [
        pl.BlockSpec((2, deep, PIECES * wide), lambda j: (0, j, 0)),
        pl.BlockSpec((PIECES, 1, down, D), lambda j: (0, j, 0, 0)),
        pl.BlockSpec((3, deep, width), lambda j: (0, j, 0)),
        pl.BlockSpec((width // GROUP, D), lambda j: (j, 0)),
        pl.BlockSpec((deep, wide), lambda j: (j, 0)),
        pl.BlockSpec((deep, wide), lambda j: (j, 0)),
        pl.BlockSpec((down, D), lambda j: (j, 0)),
        pl.BlockSpec((deep, wide // 2), lambda j: (j, 0)),
    ]
    outs = pl.pallas_call(
        unpack_kernel,
        grid=(GROUP,),
        in_specs=[pl.BlockSpec((1, total, wide), lambda j: (j, 0, 0))],
        out_specs=specs,
        out_shape=[jax.ShapeDtypeStruct(shape, F32) for shape in shapes],
        compiler_params=parallel_params(1),
        name="unpack",
        cost_estimate=pl.CostEstimate(
            flops=grads.size, bytes_accessed=6 * grads.size, transcendentals=0
        ),
    )(grads)
    outs = list(outs)
    outs[1] = outs[1].reshape(PIECES * wide, D)
    return outs


def exact(left, right, dims):
    return lax.dot_general(
        left, right, (dims, ((), ())), precision=highest, preferred_element_type=F32
    )


NN, NT, TN = ((1,), (0,)), ((1,), (1,)), ((0,), (0,))


def column(array, index):
    lane = lax.broadcasted_iota(jnp.int32, array.shape, 1)
    return jnp.sum(jnp.where(lane == index, array, 0.0), axis=1, keepdims=True)


def by_head(pair, one, two):
    lane = lax.broadcasted_iota(jnp.int32, pair, 1)
    return jnp.where(lane < HEAD_DIM, one, two)


def only_head(array, j):
    lane = lax.broadcasted_iota(jnp.int32, array.shape, 1)
    return jnp.where((lane // HEAD_DIM) == j, array, 0.0)


def pair_of(ref, q):
    return ref[:, pl.ds(pl.multiple_of(q * 128, 128), 128)]


def gate_backward_kernel(
    returned_ref,
    weight_ref,
    gain_ref,
    gate_ref,
    mixed_ref,
    cmat_ref,
    reach_ref,
    factor_ref,
    token_ref,
    mix_ref,
    gate_back_ref,
    gain_grad_ref,
    out_grad_ref,
    packed_ref,
):
    back = returned_ref[:, :D]
    extra = returned_ref[:, D:].astype(F32)
    lane = lax.broadcasted_iota(jnp.int32, extra.shape, 1)
    squares = jnp.sum(jnp.where(lane % 64 == 0, extra, 0.0), axis=1, keepdims=True)
    dots = jnp.sum(jnp.where(lane % 64 == 32, extra, 0.0), axis=1, keepdims=True)
    scale = lax.rsqrt(squares / DI + epsilon)
    grad = mm_nt(back, weight_ref[...])
    gate = gate_ref[...]
    mixed = mixed_ref[...]
    gain = gain_ref[...]
    sigma = 1.0 / (1.0 + jnp.exp(-gate))
    act = gate * sigma
    normal = mixed * act * scale
    mix_ref[...] = (normal * gain).astype(BF16)
    gain_grad_ref[...] = jnp.sum(grad * normal, axis=0, keepdims=True)
    gated_grad = scale * (grad * gain - normal * (dots / DI))
    out_grad_ref[...] = gated_grad * act
    gate_back_ref[...] = (gated_grad * mixed * sigma * (1.0 + gate * (1.0 - sigma))).astype(BF16)
    reach = reach_ref[...]
    cmat = cmat_ref[...]
    width = gate.shape[1]
    for q in range(width // 128):
        part = out_grad_ref[:, q * 128 : (q + 1) * 128]
        part = part * by_head(part.shape, column(reach, 2 * q), column(reach, 2 * q + 1))
        packed_ref[q * 128 : (q + 1) * 128] = exact(part, cmat, TN).astype(BF16)
    packed_ref[width:] = factor_ref[...]


def gate_backward(returned, weight, gain, gate, mixed, cmat, reach, factors, token):
    count, width = gate.shape
    args = (returned, weight, gain, gate, mixed, cmat, reach, factors)
    shapes = [
        jax.ShapeDtypeStruct((count, width), BF16),
        jax.ShapeDtypeStruct((count, width), BF16),
        jax.ShapeDtypeStruct((1, width), F32),
        jax.ShapeDtypeStruct((count, width), F32),
        jax.ShapeDtypeStruct((width + factors.shape[0], STATE), BF16),
    ]
    return pl.pallas_call(
        gate_backward_kernel,
        grid=(1,),
        in_specs=[whole(a.shape) for a in args] + [anywhere()],
        out_specs=[whole(o.shape) for o in shapes],
        out_shape=shapes,
        compiler_params=params(),
        name="gate_backward",
        cost_estimate=pl.CostEstimate(
            flops=2 * count * D * width, bytes_accessed=6 << 20, transcendentals=count * width
        ),
    )(*args, token)


def chunk_backward_kernel(
    grad_ref,
    inner_ref,
    bmat_ref,
    cmat_ref,
    logs_ref,
    logs_row_ref,
    steps_row_ref,
    first_ref,
    first_row_ref,
    reach_ref,
    skip_ref,
    incoming_ref,
    token_ref,
    other_token_ref,
    inner_grad_ref,
    bmat_grad_ref,
    cmat_grad_ref,
    logs_grad_ref,
    logs_row_grad_ref,
    steps_row_grad_ref,
    skip_grad_ref,
    product_ref,
    product_grad_ref,
):
    count = grad_ref.shape[0]
    bmat, cmat = bmat_ref[...], cmat_ref[...]
    product_ref[...] = exact(cmat, bmat, NT)
    product_grad_ref[...] = jnp.zeros_like(product_grad_ref)
    cmat_grad_ref[...] = jnp.zeros_like(cmat_grad_ref)
    logs_grad_ref[...] = jnp.zeros_like(logs_grad_ref)
    skip_grad_ref[...] = jnp.zeros_like(skip_grad_ref)

    def one_pair(q, carry):
        inner = pair_of(inner_ref, q)
        grad = pair_of(grad_ref, q)
        incoming = incoming_ref[pl.ds(pl.multiple_of(q * 128, 128), 128), :]
        reading = exact(cmat, incoming, NT)
        row = lax.broadcasted_iota(jnp.int32, (count, count), 0)
        col = lax.broadcasted_iota(jnp.int32, (count, count), 1)
        same = (first_ref[...] == first_row_ref[...]) & (col <= row)
        logs = logs_ref[...]
        reach = reach_ref[...]
        skip = skip_ref[...]
        total = jnp.zeros_like(inner)
        reaches = []
        for j in range(2):
            h = 2 * q + j
            own_grad = only_head(grad, j)
            steps = steps_row_ref[pl.ds(h, 1), :]
            diff = column(logs, h) - logs_row_ref[pl.ds(h, 1), :]
            decay = jnp.where(same, jnp.exp(jnp.where(same, diff, 0.0)), 0.0)
            both = exact(own_grad, inner, NT) * decay
            mixing = decay * product_ref[...]
            product_grad_ref[...] += both * steps
            used = both * product_ref[...]
            total = total + exact(mixing * steps, own_grad, TN)
            over_rows = jnp.sum(used, axis=0, keepdims=True)
            reached_here = column(reach, h)
            reaches.append(reached_here)
            logs_grad = jnp.sum(used * steps, axis=1, keepdims=True)
            logs_grad = logs_grad + reached_here * jnp.sum(
                own_grad * reading, axis=1, keepdims=True
            )
            lane = lax.broadcasted_iota(jnp.int32, logs.shape, 1)
            logs_grad_ref[...] += jnp.where(lane == h, logs_grad, 0.0)
            logs_row_grad_ref[pl.ds(h, 1), :] = -steps * over_rows
            steps_row_grad_ref[pl.ds(h, 1), :] = over_rows
            lane = lax.broadcasted_iota(jnp.int32, skip.shape, 1)
            gained = jnp.sum(jnp.sum(own_grad * inner, axis=1, keepdims=True), axis=0, keepdims=True)
            skip_grad_ref[...] += jnp.where(lane == h, gained, 0.0)
        gains = by_head((1, 128), column(skip, 2 * q), column(skip, 2 * q + 1))
        inner_grad_ref[:, pl.ds(pl.multiple_of(q * 128, 128), 128)] = total + gains * grad
        weighted = grad * by_head(grad.shape, reaches[0], reaches[1])
        cmat_grad_ref[...] += exact(weighted, incoming, NN)
        return carry

    lax.fori_loop(0, grad_ref.shape[1] // 128, one_pair, 0)
    cmat_grad_ref[...] += exact(product_grad_ref[...], bmat, NN)
    bmat_grad_ref[...] = exact(product_grad_ref[...], cmat, TN)


def chunk_backward(args, *tokens):
    count, width = args[0].shape
    heads = args[5].shape[0]
    shapes = [
        jax.ShapeDtypeStruct((count, width), F32),
        jax.ShapeDtypeStruct((count, STATE), F32),
        jax.ShapeDtypeStruct((count, STATE), F32),
        jax.ShapeDtypeStruct((count, heads), F32),
        jax.ShapeDtypeStruct((heads, count), F32),
        jax.ShapeDtypeStruct((heads, count), F32),
        jax.ShapeDtypeStruct((1, heads), F32),
    ]
    return pl.pallas_call(
        chunk_backward_kernel,
        grid=(1,),
        in_specs=[whole(a.shape) for a in args] + [anywhere() for _ in tokens],
        out_specs=[whole(o.shape) for o in shapes],
        out_shape=shapes,
        scratch_shapes=[pltpu.VMEM((count, count), F32), pltpu.VMEM((count, count), F32)],
        compiler_params=params(),
        name="chunk_backward",
        cost_estimate=pl.CostEstimate(
            flops=24 * count * count * width, bytes_accessed=4 << 20, transcendentals=count * count * heads
        ),
    )(*args, *tokens)


def front_backward_kernel(hops, *refs):
    front_backward_body(refs[:hops], *refs[hops:])


def front_backward_body(
    got_refs,
    incoming_ref,
    inner_ref,
    bmat_ref,
    logs_ref,
    steps_ref,
    steps_row_ref,
    raw_row_ref,
    last_ref,
    factor_ref,
    rate_ref,
    bias_ref,
    inner_grad_ref,
    bmat_grad_ref,
    cmat_grad_ref,
    logs_grad_ref,
    logs_row_grad_ref,
    steps_row_grad_ref,
    padded_ref,
    conv_ref,
    keep_ref,
    token_ref,
    raw_grad_ref,
    head_grad_ref,
    conv_grad_ref,
    step_back_ref,
    bias_grad_ref,
    decay_grad_ref,
    act_grad_ref,
    logs_total_ref,
    steps_total_ref,
    padded_grad_ref,
    later_ref,
):
    count, width = inner_ref.shape
    heads = width // HEAD_DIM
    chain = jnp.ones((heads, STATE), F32)
    for k, got_ref in enumerate(got_refs):
        for h in range(heads):
            at = slice(h * HEAD_DIM, (h + 1) * HEAD_DIM)
            part = chain[h : h + 1] * got_ref[at, :].astype(F32)
            later_ref[at, :] = part if k == 0 else later_ref[at, :] + part
        factors = got_ref[width : width + 2 * heads, :].astype(F32)
        chain = chain * (factors[:heads] + factors[heads:])
    bmat = bmat_ref[...]
    logs, steps, last = logs_ref[...], steps_ref[...], last_ref[...]
    final = logs[count - 1 : count, :]
    fading = jnp.exp(final - logs) * last
    weights = fading * steps
    logs_total_ref[...] = logs_grad_ref[...]
    steps_total_ref[...] = jnp.zeros_like(steps_total_ref)
    bmat_total = bmat_grad_ref[...]
    lane = lax.broadcasted_iota(jnp.int32, logs.shape, 1)
    row = lax.broadcasted_iota(jnp.int32, logs.shape, 0)
    for q in range(width // 128):
        cols = slice(q * 128, (q + 1) * 128)
        later = later_ref[cols, :]
        inner = inner_ref[:, cols]
        reading = exact(bmat, later, NT)
        spread = by_head(inner.shape, column(weights, 2 * q), column(weights, 2 * q + 1))
        act_grad_ref[:, cols] = inner_grad_ref[:, cols] + spread * reading
        bmat_total = bmat_total + exact(inner * spread, later, NN)
        crossing = jnp.sum(later * incoming_ref[cols, :], axis=1, keepdims=True)
        for j in range(2):
            h = 2 * q + j
            gained = jnp.sum(only_head(inner * reading, j), axis=1, keepdims=True)
            part = lax.broadcasted_iota(jnp.int32, crossing.shape, 0) // HEAD_DIM == j
            crossed = jnp.sum(jnp.where(part, crossing, 0.0), axis=0, keepdims=True)
            crossed = crossed * column(factor_ref[...], h)
            steps_total_ref[...] += jnp.where(lane == h, fading * gained, 0.0)
            moved = column(weights, h) * gained
            ending = jnp.sum(moved, axis=0, keepdims=True) + crossed
            change = jnp.where(row == count - 1, ending - moved, -moved)
            logs_total_ref[...] += jnp.where(lane == h, change, 0.0)
    act_grad_ref[:, width : width + STATE] = bmat_total
    act_grad_ref[:, width + STATE :] = cmat_grad_ref[...]
    t = lax.broadcasted_iota(jnp.int32, (count, count), 0)
    u = lax.broadcasted_iota(jnp.int32, (count, count), 1)
    after = (t >= u).astype(F32)
    here = (t == u).astype(F32)
    reverse = exact(logs_total_ref[...], after, TN) + exact(logs_row_grad_ref[...], after, NN)
    rate = rate_ref[...]
    steps_grad = steps_row_grad_ref[...] + exact(steps_total_ref[...], here, TN) + rate * reverse
    decay_grad_ref[...] = rate * jnp.sum(steps_row_ref[...] * reverse, axis=1, keepdims=True)
    raw = raw_row_ref[...] + bias_ref[...]
    step_grad = steps_grad / (1.0 + jnp.exp(-raw))
    bias_grad_ref[...] = jnp.sum(step_grad, axis=1, keepdims=True)
    step_back_ref[...] = step_grad.astype(BF16)
    top = 8 - (CONV - 1)
    pre = jnp.zeros(act_grad_ref.shape, F32)
    keep = keep_ref[...]
    for k in range(CONV):
        kept = column(keep, k)
        pre = pre + conv_ref[k : k + 1, :] * padded_ref[top + k : top + k + count, :] * kept
    sigma = 1.0 / (1.0 + jnp.exp(-pre))
    act_grad_ref[...] = act_grad_ref[...] * sigma * (1.0 + pre * (1.0 - sigma))
    padded_grad_ref[...] = jnp.zeros_like(padded_grad_ref)
    for k in range(CONV):
        kept = act_grad_ref[...] * column(keep, k)
        conv_grad_ref[k : k + 1, :] = jnp.sum(
            kept * padded_ref[top + k : top + k + count, :], axis=0, keepdims=True
        )
        padded_grad_ref[top + k : top + k + count, :] += conv_ref[k : k + 1, :] * kept
    raw_grad_ref[...] = padded_grad_ref[8:, :]
    head_grad_ref[...] = padded_grad_ref[:8, :]


def front_backward(gots, args, token):
    count, heads = args[3].shape
    wide = args[17].shape[1]
    shapes = [
        jax.ShapeDtypeStruct((count, wide), F32),
        jax.ShapeDtypeStruct((8, wide), F32),
        jax.ShapeDtypeStruct((CONV, wide), F32),
        jax.ShapeDtypeStruct((heads, count), BF16),
        jax.ShapeDtypeStruct((heads, 1), F32),
        jax.ShapeDtypeStruct((heads, 1), F32),
    ]
    return pl.pallas_call(
        functools.partial(front_backward_kernel, len(gots)),
        grid=(1,),
        in_specs=[whole(a.shape) for a in gots + args] + [anywhere()],
        out_specs=[whole(o.shape) for o in shapes],
        out_shape=shapes,
        scratch_shapes=[
            pltpu.VMEM((count, wide), F32),
            pltpu.VMEM((count, heads), F32),
            pltpu.VMEM((count, heads), F32),
            pltpu.VMEM((count + 8, wide), F32),
            pltpu.VMEM(args[0].shape, F32),
        ],
        compiler_params=params(),
        name="front_backward",
        cost_estimate=pl.CostEstimate(
            flops=24 * count * STATE * wide, bytes_accessed=8 << 20, transcendentals=2 * count * wide
        ),
    )(*gots, *args, token)


def project_backward_kernel(
    mine_ref,
    gate_back_ref,
    inner_back_ref,
    state_back_ref,
    step_back_ref,
    gate_ref,
    inner_ref,
    state_ref,
    step_ref,
    rows_ref,
    normed_ref,
    gain_ref,
    own_ref,
    token_ref,
    blocks_ref,
    gain_grad_ref,
    step_grad_ref,
    total_ref,
):
    grad = mm_nt(gate_back_ref[...], gate_ref[...])
    grad = grad + mm_nt(inner_back_ref[...], inner_ref[...])
    grad = grad + mm_nt(state_back_ref[...], state_ref[...])
    grad = grad + mm_tn(step_back_ref[...], step_ref[...])
    step_grad_ref[...] = mm(step_back_ref[...], normed_ref[...])
    values = rows_ref[...].astype(F32)
    scale = inverse_rms(values)
    normal = values * scale
    gain_grad_ref[...] = jnp.sum(grad * normal, axis=0, keepdims=True)
    scaled = grad * gain_ref[...]
    total_ref[...] = scale * (scaled - normal * jnp.mean(scaled * normal, axis=-1, keepdims=True))
    share = own_ref.shape[0]
    at = pl.ds(pl.multiple_of(mine_ref[0] * share, share), share)
    total_ref[at, :] += own_ref[...]
    width = blocks_ref.shape[2]
    for i in range(blocks_ref.shape[0]):
        blocks_ref[i] = total_ref[:, i * width : (i + 1) * width].astype(BF16)


def project_backward(mine, args, tps, token):
    count = args[0].shape[0]
    heads = args[3].shape[0]
    shapes = [
        jax.ShapeDtypeStruct((tps, count, D // tps), BF16),
        jax.ShapeDtypeStruct((1, D), F32),
        jax.ShapeDtypeStruct((heads, D), F32),
    ]
    return pl.pallas_call(
        project_backward_kernel,
        grid=(1,),
        in_specs=[scalar_spec()] + [whole(a.shape) for a in args] + [anywhere()],
        out_specs=[whole(o.shape) for o in shapes],
        out_shape=shapes,
        scratch_shapes=[pltpu.VMEM((count, D), F32)],
        compiler_params=params(),
        name="project_backward",
        cost_estimate=pl.CostEstimate(
            flops=2 * count * D * 1288, bytes_accessed=6 << 20, transcendentals=count
        ),
    )(mine, *args, token)


def mixer_weight_grads_kernel(
    core_ref,
    normed_ref,
    gate_ref,
    inner_ref,
    state_ref,
    mix_ref,
    back_ref,
    token_ref,
    own_ref,
    other_ref,
):
    core = core_ref[0]
    normed = normed_ref[...]
    deep = D // GROUP
    wide = gate_ref.shape[1]
    put_halves(core, mm_tn(normed, gate_ref[...]), own_ref, other_ref, 0, deep)
    put_halves(core, mm_tn(normed, inner_ref[...]), own_ref, other_ref, deep, 2 * deep)
    rows = wide // GROUP
    mix = mix_ref[...]
    for i in range(D // wide):
        low = 2 * deep + i * rows
        grad = mm_tn(mix, back_ref[:, i * wide : (i + 1) * wide])
        put_halves(core, grad, own_ref, other_ref, low, low + rows)
    low = own_ref.shape[3] - deep // 2
    own, other = core_halves(core, mm_tn(normed, state_ref[...]).astype(BF16))
    for i in range(2):
        cols = slice(i * wide // 2, (i + 1) * wide // 2)
        rows_in = slice(i * deep // 2, (i + 1) * deep // 2)
        own_ref[:, :, 0, low:, cols] = own[:, :, rows_in]
        other_ref[:, :, 0, low:, cols] = other[:, :, rows_in]


def mixer_weight_grads(core, normed, gate, inner, state, mix, back, token):
    wide = gate.shape[1]
    deep = D // GROUP
    depth = 2 * deep + D // GROUP + deep // 2
    args = (normed, gate, inner, state, mix, back)
    return pl.pallas_call(
        mixer_weight_grads_kernel,
        grid=(1,),
        in_specs=[scalar_spec()] + [whole(a.shape) for a in args] + [anywhere()],
        out_specs=[halves_spec(depth, wide)] * 2,
        out_shape=[halves_shape(1, depth, wide)] * 2,
        compiler_params=params(),
        name="mixer_weight_grads",
        cost_estimate=pl.CostEstimate(
            flops=8 * normed.shape[0] * D * wide, bytes_accessed=8 << 20, transcendentals=0
        ),
    )(core, *args, token)


def shards(
    patches,
    byte_embed,
    seq_lengths,
    norm_global,
    proj_gate,
    proj_inner,
    proj_state,
    proj_step,
    step_bias,
    decay_log,
    conv_inner,
    conv_state,
    skip_gain,
    mixer_gain,
    proj_mixer,
    norm_attn,
    attn_input,
    attn_output,
    norm_ffn,
    expand_weight,
    shrink_weight,
    grad_output,
):
    count, quarter = patches.shape
    tps = lax.axis_size("tp")
    mine = lax.axis_index("tp")
    here = lax.axis_index(SEQ)
    core = lax.axis_index("c").reshape(1)
    tail = CONV - 1
    inner_width = proj_inner.shape[1]
    share = count // tps
    total_rows = byte_embed.shape[0]
    rows = total_rows // tps

    narrow = D // GROUP
    slot = lax.axis_index(INNER)

    def folded(array, width):
        rows_in = array.shape[0]
        return array.reshape(rows_in, -1, width).transpose(1, 0, 2).reshape(-1, width)

    attn_in_part = lax.dynamic_slice_in_dim(attn_input, slot * narrow, narrow, 1)
    out_rows = attn_output.shape[0] // GROUP
    attn_out_part = lax.dynamic_slice_in_dim(attn_output, slot * out_rows, out_rows, 0)
    attn_out_part = folded(attn_out_part, quarter)
    hidden_width = expand_weight.shape[2]
    wide = hidden_width // PIECES
    down_rows = wide // GROUP
    ffn_parts = []
    for p in range(PIECES):
        up_part = lax.dynamic_slice(
            expand_weight, (0, slot * narrow, p * wide), (2, narrow, wide)
        )
        down_part = lax.dynamic_slice_in_dim(
            shrink_weight, p * wide + slot * down_rows, down_rows, 0
        )
        ffn_parts.append([up_part.reshape(-1, wide), folded(down_part, wide)])
    attn_parts = [
        jnp.concatenate([attn_in_part[0], attn_in_part[2]], axis=1),
        jnp.concatenate([attn_in_part[1], attn_out_part], axis=1),
    ]
    weights_line = lax.all_gather(jnp.concatenate(attn_parts + ffn_parts[0], axis=0), "tp")
    last_part = jnp.concatenate(ffn_parts[1], axis=0)
    place = jnp.stack([lax.axis_index("a"), lax.axis_index("b")]).astype(jnp.int32)

    def to_rows(array):
        return lax.all_to_all(array.reshape(tps, rows, quarter), "tp", 0, 0)

    def to_columns(blocks):
        return lax.all_to_all(blocks, "tp", 0, 0).reshape(total_rows, quarter)

    positions = here * count + jnp.arange(count, dtype=jnp.int32)
    first = sequence_first(positions, seq_lengths)
    patch_rows = lax.all_gather(patches, "tp", axis=1, tiled=True)
    embed_rows = to_rows(byte_embed)
    cot_rows = to_rows(grad_output)
    global_in = patch_rows.astype(jnp.float32)
    normed = (rms_scale(global_in) * norm_global[None, :]).astype(jnp.bfloat16)
    gate_vals = product(normed, proj_gate, "rd,dc->rc")
    inner_raw = product(normed, proj_inner, "rd,dc->rc")
    state_raw = product(normed, proj_state, "rd,dc->rc")
    step_raw = product(normed, proj_step, "rd,dc->rc")
    raw = jnp.concatenate([inner_raw, state_raw], axis=1)
    before = shifted(raw[count - tail :], 1)
    padded = jnp.concatenate([before, raw], axis=0)
    conv_weight = jnp.concatenate([conv_inner, conv_state], axis=1)

    inner_vals, bmatrix, cmatrix, steps, rates = front_part(
        padded, step_raw, conv_weight, step_bias, decay_log, positions, first
    )
    carried, states = block_summary(inner_vals, bmatrix, steps, rates, positions, first)
    weights = lax.all_gather(tied(weights_line, states), INNER)
    incoming = reached(carried, states, 1)
    mixed = block_output(
        inner_vals, bmatrix, cmatrix, steps, rates, skip_gain, incoming, positions, first
    )
    gate_act = jax.nn.silu(gate_vals)
    gated = mixed * gate_act
    squares = jnp.sum(gated * gated, axis=1, keepdims=True)
    partial = product((gated * mixer_gain[None, :]).astype(BF16), proj_mixer, "rc,cd->rd")
    square_high, square_low = high_low(jnp.broadcast_to(squares, (count, 64)))
    partial = partial + embed_rows[0, 0, 0].astype(F32) * 0.0
    sent = jnp.concatenate([partial.astype(BF16), square_high, square_low], axis=1)
    summed = jnp.sum(
        lax.all_to_all(sent.reshape(tps, share, -1), "tp", 0, 0).astype(F32), axis=0
    )
    own_squares = summed[:, D : D + 1] + summed[:, D + 64 : D + 65]
    last_part = tied(last_part, own_squares)
    last_line = lax.all_to_all(
        jnp.broadcast_to(last_part[None], (tps,) + last_part.shape), "tp", 0, 0
    )
    last_weights = lax.all_gather(last_line, INNER)
    mixer_rows = summed[:, :D] * lax.rsqrt(own_squares / DI + epsilon)
    own_patches = lax.dynamic_slice_in_dim(patch_rows, mine * share, share, 0)
    global_out = own_patches.astype(F32) + mixer_rows

    logs = jnp.cumsum(steps * rates[None, :], axis=0)
    from_before = (first < positions[0]).astype(F32)[:, None]
    reach = jnp.exp(logs) * from_before
    factor_high, factor_low = high_low(jnp.broadcast_to(carried[:, None], (carried.size, STATE)))
    factors = jnp.concatenate([factor_high, factor_low], axis=0)
    flat_inner = inner_vals.reshape(count, -1)
    flat_incoming = incoming.reshape(-1, STATE)
    keep = jnp.stack(
        [(positions - (CONV - 1 - k) >= first).astype(F32) for k in range(CONV)], axis=1
    )
    logs_row, steps_row, raw_row = logs.T, steps.T, step_raw.T
    last = (first == first[-1]).astype(F32)[:, None]
    rate_column, bias_column = rates[:, None], step_bias[:, None]
    wide_padded = jnp.pad(padded, ((8 - tail, 0), (0, 0)))
    step_weight = proj_step.T
    prepared = (
        reach, factors, keep, logs_row, steps_row, raw_row, last, rate_column, bias_column,
        wide_padded, step_weight, flat_inner, flat_incoming,
    )

    hidden, attn_in, attn_normed, qkv, context = attention_forward(
        embed_rows, global_out[:, None, :], norm_attn[None, :], weights, prepared
    )
    ffn_normed, ffn_turned, cot_whole, out_acc, normed_acc, own_first, other_first = (
        feed_forward_first(core, hidden, cot_rows, norm_ffn[None, :], weights)
    )
    first_one = reduce_first(place, own_first, other_first)
    first_two = reduce_second(place, first_one)
    layer_blocks, hidden_grad, norm_ffn_part, last_grad = feed_forward_last(
        core,
        hidden,
        cot_whole,
        norm_ffn[None, :],
        last_weights,
        ffn_normed,
        ffn_turned,
        out_acc,
        normed_acc,
        first_two[0],
    )
    layer_output = to_columns(layer_blocks)
    first_three, hidden_grad = reduce_third(first_two, hidden_grad)
    embed_blocks, own_grad, payload, norm_attn_part, own_attn, other_attn = attention_backward(
        core,
        hidden_grad,
        mixer_rows,
        attn_in,
        attn_normed,
        norm_attn[None, :],
        weights,
        qkv,
        context,
        own_squares,
        layer_output,
    )
    last_three = lax.psum_scatter(last_grad, INNER, scatter_dimension=0)
    embed_columns = to_columns(embed_blocks)
    embed_grad = embed_columns.astype(F32)

    attn_one = reduce_first(place, own_attn, other_attn)
    returned = lax.all_gather(payload, "tp", axis=0, tiled=True)
    mix_back_in = returned[:, :D]
    mix_low, gate_back, mixer_gain_grad, mixed_grad, packed = gate_backward(
        returned,
        proj_mixer,
        mixer_gain[None, :],
        gate_vals,
        mixed,
        cmatrix,
        reach,
        factors,
        attn_one[0],
    )
    ffn_sums = tied(jnp.concatenate([first_three, last_three], axis=1), packed)
    ffn_part = reduce_last(ffn_sums)
    chunk_grads = chunk_backward(
        (
            mixed_grad,
            flat_inner,
            bmatrix,
            cmatrix,
            logs,
            logs_row,
            steps_row,
            first[:, None],
            first[None, :],
            reach,
            skip_gain[None, :],
            flat_incoming,
        ),
        attn_one[0],
        ffn_sums,
    )
    attn_two = reduce_second(place, attn_one, (chunk_grads[0],))
    skip_gain_grad = chunk_grads[6][0]
    devices = lax.axis_size(SEQ)
    gots = tuple(
        lax.ppermute(packed, SEQ, [(i + hop, i) for i in range(devices - hop)])
        for hop in range(1, devices // 2 + 1)
    )
    raw_grad, head_grad, conv_grad, step_back, step_bias_grad, decay_log_grad = front_backward(
        gots,
        (
            flat_incoming,
            flat_inner,
            bmatrix,
            logs,
            steps,
            steps_row,
            raw_row,
            last,
            carried[None, :],
            rate_column,
            bias_column,
        )
        + tuple(chunk_grads[:6])
        + (
            wide_padded,
            conv_weight,
            keep,
        ),
        attn_two[1],
    )
    step_bias_grad, decay_log_grad = step_bias_grad[:, 0], decay_log_grad[:, 0]
    tail_grad = shifted(head_grad, -1)
    raw_grad = jnp.concatenate(
        [raw_grad[: count - 8], raw_grad[count - 8 :] + tail_grad], axis=0
    ).astype(BF16)
    inner_back, state_back = raw_grad[:, :inner_width], raw_grad[:, inner_width:]
    own_mixer, other_mixer = mixer_weight_grads(
        core, normed, gate_back, inner_back, state_back, mix_low, mix_back_in, attn_two[1]
    )
    mixer_one = reduce_first(place, own_mixer, other_mixer)
    attn_three, mixer_kept = reduce_third(attn_two, mixer_one[1])
    attn_part = reduce_last(tied(attn_three, ffn_part))
    mixer_two = reduce_second(place, (mixer_one[0], mixer_kept) + tuple(mixer_one[2:]))
    mixer_three, step_back = reduce_third(mixer_two, step_back)
    mixer_three = mixer_three[0]
    mixer_part = over_groups(mixer_three)
    state_rows = lax.all_gather(mixer_part[3 * narrow :], "tp")
    state_rows = jnp.sum(state_rows.astype(F32), axis=0).astype(BF16)
    columns, norm_global_part, step_grad = project_backward(
        mine.reshape(1),
        (
            gate_back,
            inner_back,
            state_back,
            step_back,
            proj_gate,
            proj_inner,
            proj_state,
            step_weight,
            patch_rows,
            normed,
            norm_global[None, :],
            own_grad,
        ),
        tps,
        state_rows,
    )
    norm_global_part = norm_global_part[0]
    shared = jnp.concatenate(
        [
            conv_grad[:, inner_width:].reshape(-1),
            norm_attn_part[0],
            norm_ffn_part[0],
            norm_global_part,
        ]
    ).reshape(-1, quarter)
    shared_high, shared_low = high_low(shared)
    shared_rows = jnp.concatenate([shared_high, shared_low], axis=0)
    returned = lax.all_to_all(
        jnp.concatenate(
            [columns, jnp.broadcast_to(shared_rows[None], (tps,) + shared_rows.shape)], axis=1
        ),
        "tp",
        0,
        0,
    )
    returned = jnp.sum(returned.astype(F32), axis=0)
    patch_grad = returned[:count]
    shared = returned[count : count + shared.shape[0]] + returned[count + shared.shape[0] :]
    shared = shared.reshape(-1)
    held = conv_state.size
    shared = (
        shared[:held].reshape(conv_state.shape),
        shared[held : held + D],
        shared[held + D : held + 2 * D],
        shared[held + 2 * D :],
    )
    (
        conv_state_grad,
        norm_attn_grad,
        norm_ffn_grad,
        norm_global_grad,
        proj_step_grad,
        step_bias_grad,
        decay_log_grad,
        conv_inner_grad,
        skip_gain_grad,
        mixer_gain_grad,
    ) = lax.psum(
        shared
        + (
            step_grad.T,
            step_bias_grad,
            decay_log_grad,
            conv_grad[:, :inner_width],
            skip_gain_grad,
            mixer_gain_grad[0],
        ),
        SEQ,
    )
    ffn_depth, attn_depth = 3 * narrow, 2 * narrow
    all_grads = lax.all_gather(
        jnp.concatenate([ffn_part, attn_part, mixer_part[: 3 * narrow], state_rows]), INNER
    )
    (
        expand_grad,
        shrink_grad,
        attn_input_grad,
        attn_output_grad,
        proj_gate_grad,
        proj_inner_grad,
        proj_mixer_grad,
        proj_state_grad,
    ) = unpack(all_grads, tps)
    return (
        layer_output,
        embed_grad,
        patch_grad,
        norm_global_grad,
        proj_gate_grad,
        proj_inner_grad,
        proj_state_grad,
        proj_step_grad,
        step_bias_grad,
        decay_log_grad,
        conv_inner_grad,
        conv_state_grad,
        skip_gain_grad,
        mixer_gain_grad,
        proj_mixer_grad,
        norm_attn_grad,
        attn_input_grad,
        attn_output_grad,
        norm_ffn_grad,
        expand_grad,
        shrink_grad,
    )


def solution(mesh):
    seq, tps = mesh.shape["seq"], mesh.shape["tp"]
    fine = Mesh(mesh.devices.reshape(seq // GROUP, 2, 2, 2, tps), SEQ + ("tp",))
    rows_cols = P(SEQ, "tp")
    last = P(None, "tp")
    lead = P("tp", None)
    return jax.shard_map(
        shards,
        mesh=fine,
        in_specs=(
            rows_cols,
            rows_cols,
            P(),
            P(),
            last,
            last,
            P(),
            last,
            P("tp"),
            P("tp"),
            last,
            P(),
            P("tp"),
            P("tp"),
            lead,
            P(),
            P(None, None, "tp"),
            lead,
            P(),
            P(None, None, "tp"),
            lead,
            rows_cols,
        ),
        out_specs=(
            rows_cols,
            rows_cols,
            rows_cols,
            P(),
            last,
            last,
            P(),
            last,
            P("tp"),
            P("tp"),
            last,
            P(),
            P("tp"),
            P("tp"),
            lead,
            P(),
            P(None, None, "tp"),
            lead,
            P(),
            P(None, None, "tp"),
            lead,
        ),
        check_vma=False,
    )
```

```python
import functools

import jax
import jax.numpy as jnp
from jax import lax
from jax.experimental import pallas as pl
from jax.experimental.pallas import tpu as pltpu
from jax.sharding import Mesh, PartitionSpec as P

D = 1024
HEAD_DIM = 64
STATE = 128
HEADS_A = 16
CONV = 4
PATCH = 8
DI = 2048
GROUP = 8
TILE = 128
PIECES = 2

epsilon = 1e-05
highest = lax.Precision.HIGHEST
F32 = jnp.float32
BF16 = jnp.bfloat16
SEQ = ("g", "a", "b", "c")
INNER = ("a", "b", "c")


def mm(left, right):
    return lax.dot_general(left, right, (((1,), (0,)), ((), ())), preferred_element_type=F32)


def mm_nt(left, right):
    return lax.dot_general(left, right, (((1,), (1,)), ((), ())), preferred_element_type=F32)


def mm_tn(left, right):
    return lax.dot_general(left, right, (((0,), (0,)), ((), ())), preferred_element_type=F32)


def inverse_rms(values):
    return lax.rsqrt(jnp.mean(values * values, axis=-1, keepdims=True) + epsilon)


def params(limit=60):
    return pltpu.CompilerParams(
        dimension_semantics=("arbitrary",), vmem_limit_bytes=limit * 1024 * 1024
    )


def whole(shape):
    return pl.BlockSpec(shape, lambda j: (0,) * len(shape))


def scalar_spec():
    return pl.BlockSpec(memory_space=pltpu.SMEM)


def halves_shape(tps, depth, wide):
    return jax.ShapeDtypeStruct((2, 2, tps, depth, wide), BF16)


def halves_spec(depth, wide):
    return pl.BlockSpec((2, 2, 1, depth, wide), lambda j: (0, 0, j, 0, 0))


def anywhere():
    return pl.BlockSpec(memory_space=pl.ANY)


def weight_specs(weights, first):
    parts, _, _, wide = weights.shape
    block = (parts, 1, D // GROUP, wide)
    return [
        pl.BlockSpec(block, functools.partial(lambda k, j: (0, j, k, 0), first + k))
        for k in range(3)
    ]


def attention_spec(weights):
    parts, _, _, wide = weights.shape
    return pl.BlockSpec((parts, 1, 2 * D // GROUP, wide), lambda j: (0, j, 0, 0))


def attention_view(weight_ref, k, width):
    deep = D // weight_ref.shape[0]
    rows = slice((k % 2) * deep, (k % 2 + 1) * deep)
    return weight_ref.at[:, 0, rows, (k // 2) * width : (k // 2 + 1) * width]


def head_mask(width):
    lane = lax.broadcasted_iota(jnp.int32, (1, width), 1) // (D // HEADS_A)
    return [lane == h for h in range(width // (D // HEADS_A))]


def split_heads(tile, masks):
    zero = jnp.zeros_like(tile)
    return jnp.concatenate([jnp.where(m, tile, zero) for m in masks], axis=0)


def tile_mask(heads):
    row = lax.broadcasted_iota(jnp.int32, (heads * TILE, TILE), 0) % TILE
    col = lax.broadcasted_iota(jnp.int32, (heads * TILE, TILE), 1)
    return (row // PATCH == col // PATCH) & (col <= row)


def tile_probs(query_split, keys, keep):
    scores = mm_nt(query_split, keys) * ((D // HEADS_A) ** -0.5)
    scores = jnp.where(keep, scores, -1e30)
    expo = jnp.exp(scores - jnp.max(scores, axis=-1, keepdims=True))
    return expo * (1.0 / jnp.sum(expo, axis=-1, keepdims=True))


def beside(stacked, heads):
    return jnp.concatenate([stacked[h * TILE : (h + 1) * TILE] for h in range(heads)], axis=1)


def attention_forward_kernel(
    embed_ref, global_ref, gain_ref, weight_ref, *refs
):
    hidden_ref, input_ref, normed_ref, qkv_ref, context_ref = refs[-5:]
    step = pl.program_id(0)
    blocks, rows, width = embed_ref.shape
    parts = weight_ref.shape[0]

    @pl.when(step == 0)
    def _():
        embed = jnp.concatenate([embed_ref[i] for i in range(blocks)], axis=1).astype(F32)
        spread = jnp.broadcast_to(global_ref[...], (rows // PATCH, PATCH, D)).reshape(rows, D)
        total = embed + spread
        hidden_ref[...] = total
        low = total.astype(BF16)
        input_ref[...] = low
        values = low.astype(F32)
        normed_ref[...] = (values * inverse_rms(values) * gain_ref[...]).astype(BF16)

    normed = normed_ref[...]
    for k in range(3):
        weight = attention_view(weight_ref, k, width)[...].reshape(D, width)
        qkv_ref[0, k] = mm(normed, weight).astype(BF16)
    masks = head_mask(width)
    heads = len(masks)
    keep = tile_mask(heads)
    for r in range(rows // TILE):
        at = slice(r * TILE, (r + 1) * TILE)
        query = split_heads(qkv_ref[0, 0, at], masks)
        probs = tile_probs(query, qkv_ref[0, 1, at], keep).astype(BF16)
        values = split_heads(qkv_ref[0, 2, at], masks)
        context_ref[0, at] = mm(beside(probs, heads), values).astype(BF16)
    context = context_ref[0]
    piece = width // parts
    outward = attention_view(weight_ref, 3, width)
    for c in range(D // width):
        weight = outward[:, c * piece : (c + 1) * piece].reshape(width, width)
        cols = slice(c * width, (c + 1) * width)
        hidden_ref[:, cols] += mm(context, weight)


def attention_forward(embed, global_rows, gain, weights, tokens):
    blocks, rows, width = embed.shape
    tps = weights.shape[1]
    return pl.pallas_call(
        attention_forward_kernel,
        grid=(tps,),
        in_specs=[
            whole((blocks, rows, width)),
            whole((rows // PATCH, 1, D)),
            whole((1, D)),
            attention_spec(weights),
            *(anywhere() for _ in tokens),
        ],
        out_specs=[
            whole((rows, D)),
            whole((rows, D)),
            whole((rows, D)),
            pl.BlockSpec((1, 3, rows, width), lambda j: (j, 0, 0, 0)),
            pl.BlockSpec((1, rows, width), lambda j: (j, 0, 0)),
        ],
        out_shape=[
            jax.ShapeDtypeStruct((rows, D), F32),
            jax.ShapeDtypeStruct((rows, D), BF16),
            jax.ShapeDtypeStruct((rows, D), BF16),
            jax.ShapeDtypeStruct((tps, 3, rows, width), BF16),
            jax.ShapeDtypeStruct((tps, rows, width), BF16),
        ],
        compiler_params=params(),
        name="attention_forward",
        cost_estimate=pl.CostEstimate(
            flops=2 * rows * D * D * 4, bytes_accessed=14 << 20, transcendentals=rows * 2048
        ),
    )(embed, global_rows, gain, weights, *tokens)


def core_halves(core, grad):
    parts = grad.reshape((2, 2, 2, grad.shape[0] // GROUP) + grad.shape[1:])
    mine = jnp.where(core == 0, parts[:, :, 0], parts[:, :, 1])
    other = jnp.where(core == 0, parts[:, :, 1], parts[:, :, 0])
    return mine, other


def put_halves(core, grad, own_ref, other_ref, low, high, cols=slice(None)):
    own, other = core_halves(core, grad.astype(BF16))
    own_ref[:, :, 0, low:high, cols] = own
    other_ref[:, :, 0, low:high, cols] = other


def put_whole(core, grad, grad_ref, low, high):
    parts = grad_ref.shape[0]
    grad_ref[:, 0, low:high] = grad.astype(BF16).reshape((parts, -1) + grad.shape[1:])


def feed_forward_step(
    core_ref, weight_refs, cot, normed_ref, turned_ref, out_acc, normed_acc, put
):
    parts, _, _, wide = weight_refs[0].shape
    deep = D // parts
    core = core_ref[0]
    normed = normed_ref[...]
    gate_weight = weight_refs[0][:, 0].reshape(D, wide)
    up_weight = weight_refs[1][:, 0].reshape(D, wide)
    piece = wide // parts
    folds = D // wide
    down_weight = jnp.concatenate(
        [
            weight_refs[2][:, 0, i * piece : (i + 1) * piece].reshape(wide, wide)
            for i in range(folds)
        ],
        axis=1,
    )
    gate = mm(normed, gate_weight)
    up = mm(normed, up_weight)
    sigma = 1.0 / (1.0 + jnp.exp(-gate))
    swish = gate * sigma
    activ = (swish * up).astype(BF16)
    out_acc[...] += mm(activ, down_weight)
    shrink = mm_tn(activ, cot)
    for i in range(folds):
        low = 2 * deep + i * piece
        put(core, shrink[:, i * wide : (i + 1) * wide], low, low + piece)
    dactiv = mm_nt(cot, down_weight)
    dgate = (dactiv * up * sigma * (1.0 + gate * (1.0 - sigma))).astype(BF16)
    dup = (dactiv * swish).astype(BF16)
    normed_acc[...] += mm_nt(dgate, gate_weight) + mm_nt(dup, up_weight)
    turned = turned_ref[...]
    put(core, mm(turned, dgate), 0, deep)
    put(core, mm(turned, dup), deep, 2 * deep)


def feed_forward_first_kernel(
    core_ref,
    hidden_ref,
    cot_ref,
    gain_ref,
    gate_ref,
    up_ref,
    down_ref,
    normed_ref,
    turned_ref,
    cot_out,
    out_acc,
    normed_acc,
    own_ref,
    other_ref,
):
    blocks, _, width = cot_ref.shape

    @pl.when(pl.program_id(0) == 0)
    def _():
        values = hidden_ref[...].astype(BF16).astype(F32)
        normed = (values * inverse_rms(values) * gain_ref[...]).astype(BF16)
        normed_ref[...] = normed
        turned_ref[...] = normed.astype(F32).T.astype(BF16)
        for i in range(blocks):
            cot_out[:, i * width : (i + 1) * width] = cot_ref[i]
        out_acc[...] = hidden_ref[...]
        normed_acc[...] = jnp.zeros_like(normed_acc)

    def put(core, grad, low, high):
        put_halves(core, grad, own_ref, other_ref, low, high)

    feed_forward_step(
        core_ref,
        (gate_ref, up_ref, down_ref),
        cot_out[...],
        normed_ref,
        turned_ref,
        out_acc,
        normed_acc,
        put,
    )


def feed_forward_last_kernel(
    core_ref,
    hidden_ref,
    cot_ref,
    gain_ref,
    gate_ref,
    up_ref,
    down_ref,
    normed_ref,
    turned_ref,
    out_in,
    normed_in,
    token_ref,
    layer_ref,
    grad_ref,
    gain_grad_ref,
    weight_grad_ref,
    out_acc,
    normed_acc,
):
    step = pl.program_id(0)
    blocks, _, width = layer_ref.shape

    @pl.when(step == 0)
    def _():
        out_acc[...] = out_in[...]
        normed_acc[...] = normed_in[...]

    def put(core, grad, low, high):
        put_whole(core, grad, weight_grad_ref, low, high)

    feed_forward_step(
        core_ref,
        (gate_ref, up_ref, down_ref),
        cot_ref[...],
        normed_ref,
        turned_ref,
        out_acc,
        normed_acc,
        put,
    )

    @pl.when(step == pl.num_programs(0) - 1)
    def _():
        layer = out_acc[...].astype(BF16)
        for i in range(blocks):
            layer_ref[i] = layer[:, i * width : (i + 1) * width]
        values = hidden_ref[...].astype(BF16).astype(F32)
        scale = inverse_rms(values)
        normal = values * scale
        grad = normed_acc[...]
        gain_grad_ref[...] = jnp.sum(grad * normal, axis=0, keepdims=True)
        scaled = grad * gain_ref[...]
        back = scale * (scaled - normal * jnp.mean(scaled * normal, axis=-1, keepdims=True))
        grad_ref[...] = cot_ref[...].astype(F32) + back


def feed_forward_cost(rows, weights):
    _, tps, _, wide = weights.shape
    return pl.CostEstimate(
        flops=18 * rows * D * wide * tps,
        bytes_accessed=12 * D * wide * tps + 16 * rows * D,
        transcendentals=rows * wide * tps,
    )


def feed_forward_first(core, hidden, cot, gain, weights):
    rows = hidden.shape[0]
    _, tps, _, wide = weights.shape
    depth = 3 * D // GROUP
    return pl.pallas_call(
        feed_forward_first_kernel,
        grid=(tps,),
        in_specs=[
            scalar_spec(),
            whole((rows, D)),
            whole(cot.shape),
            whole((1, D)),
            *weight_specs(weights, 2),
        ],
        out_specs=[
            whole((rows, D)),
            whole((D, rows)),
            whole((rows, D)),
            whole((rows, D)),
            whole((rows, D)),
            halves_spec(depth, wide),
            halves_spec(depth, wide),
        ],
        out_shape=[
            jax.ShapeDtypeStruct((rows, D), BF16),
            jax.ShapeDtypeStruct((D, rows), BF16),
            jax.ShapeDtypeStruct((rows, D), BF16),
            jax.ShapeDtypeStruct((rows, D), F32),
            jax.ShapeDtypeStruct((rows, D), F32),
            halves_shape(tps, depth, wide),
            halves_shape(tps, depth, wide),
        ],
        compiler_params=params(),
        name="feed_forward_first",
        cost_estimate=feed_forward_cost(rows, weights),
    )(core, hidden, cot, gain, weights, weights, weights)


def feed_forward_last(
    core, hidden, cot, gain, weights, normed, turned, out_in, normed_in, token
):
    rows = hidden.shape[0]
    _, tps, _, wide = weights.shape
    depth = 3 * D // GROUP
    width = D // tps
    return pl.pallas_call(
        feed_forward_last_kernel,
        grid=(tps,),
        in_specs=[
            scalar_spec(),
            whole((rows, D)),
            whole((rows, D)),
            whole((1, D)),
            *weight_specs(weights, 0),
            whole((rows, D)),
            whole((D, rows)),
            whole((rows, D)),
            whole((rows, D)),
            anywhere(),
        ],
        out_specs=[
            whole((tps, rows, width)),
            whole((rows, D)),
            whole((1, D)),
            pl.BlockSpec((GROUP, 1, depth, wide), lambda j: (0, j, 0, 0)),
        ],
        out_shape=[
            jax.ShapeDtypeStruct((tps, rows, width), BF16),
            jax.ShapeDtypeStruct((rows, D), F32),
            jax.ShapeDtypeStruct((1, D), F32),
            jax.ShapeDtypeStruct((GROUP, tps, depth, wide), BF16),
        ],
        scratch_shapes=[pltpu.VMEM((rows, D), F32), pltpu.VMEM((rows, D), F32)],
        compiler_params=params(),
        name="feed_forward_last",
        cost_estimate=feed_forward_cost(rows, weights),
    )(core, hidden, cot, gain, weights, weights, weights, normed, turned, out_in, normed_in, token)


def attention_backward_kernel(
    core_ref,
    grad_ref,
    mixer_ref,
    input_ref,
    normed_ref,
    gain_ref,
    weight_ref,
    qkv_ref,
    context_ref,
    squares_ref,
    token_ref,
    embed_ref,
    global_ref,
    payload_ref,
    gain_grad_ref,
    own_ref,
    other_ref,
    turned_ref,
    low_ref,
    normed_acc,
    context_grad_ref,
    qkv_grad_ref,
):
    step = pl.program_id(0)
    rows = grad_ref.shape[0]
    blocks, _, width = embed_ref.shape
    parts = weight_ref.shape[0]
    deep = D // parts
    scaling = (D // HEADS_A) ** -0.5
    core = core_ref[0]

    @pl.when(step == 0)
    def _():
        turned_ref[...] = normed_ref[...].astype(F32).T.astype(BF16)
        low_ref[...] = grad_ref[...].astype(BF16)
        normed_acc[...] = jnp.zeros_like(normed_acc)

    low = low_ref[...]
    context = context_ref[0]
    piece = width // parts
    total = jnp.zeros((rows, width), F32)
    outward = attention_view(weight_ref, 3, width)
    for c in range(D // width):
        first = deep + c * piece
        weight = outward[:, c * piece : (c + 1) * piece].reshape(width, width)
        columns = low[:, c * width : (c + 1) * width]
        total = total + mm_nt(columns, weight)
        put_halves(
            core,
            mm_tn(context, columns),
            own_ref,
            other_ref,
            first,
            first + piece,
            slice(width, 2 * width),
        )
    context_grad_ref[...] = total.astype(BF16)
    masks = head_mask(width)
    heads = len(masks)
    keep = tile_mask(heads)
    for r in range(rows // TILE):
        at = slice(r * TILE, (r + 1) * TILE)
        query = split_heads(qkv_ref[0, 0, at], masks)
        keys = qkv_ref[0, 1, at]
        probs = tile_probs(query, keys, keep)
        dcontext = split_heads(context_grad_ref[at], masks)
        dprobs = mm_nt(dcontext, qkv_ref[0, 2, at])
        dvalues = mm_tn(probs.astype(BF16), dcontext)
        inner = jnp.sum(dprobs * probs, axis=-1, keepdims=True)
        dscores = (probs * (dprobs - inner)).astype(BF16)
        dquery = mm(beside(dscores, heads), split_heads(keys, masks)) * scaling
        dkeys = mm_tn(dscores, query) * scaling
        qkv_grad_ref[at, :width] = dquery.astype(BF16)
        qkv_grad_ref[at, width : 2 * width] = dkeys.astype(BF16)
        qkv_grad_ref[at, 2 * width :] = dvalues.astype(BF16)
    turned = turned_ref[...]
    for k in range(3):
        part = qkv_grad_ref[:, k * width : (k + 1) * width]
        weight = attention_view(weight_ref, k, width)[...].reshape(D, width)
        normed_acc[...] += mm_nt(part, weight)
        first = (k % 2) * deep
        put_halves(
            core,
            mm(turned, part),
            own_ref,
            other_ref,
            first,
            first + deep,
            slice((k // 2) * width, (k // 2 + 1) * width),
        )

    @pl.when(step == pl.num_programs(0) - 1)
    def _():
        values = input_ref[...].astype(F32)
        scale = inverse_rms(values)
        normal = values * scale
        grad = normed_acc[...]
        gain_grad_ref[...] = jnp.sum(grad * normal, axis=0, keepdims=True)
        scaled = grad * gain_ref[...]
        back = scale * (scaled - normal * jnp.mean(scaled * normal, axis=-1, keepdims=True))
        result = grad_ref[...] + back
        for i in range(blocks):
            embed_ref[i] = result[:, i * width : (i + 1) * width].astype(BF16)
        patch = jnp.sum(result.reshape(rows // PATCH, PATCH, D), axis=1)
        global_ref[...] = patch
        dots = jnp.sum(patch * mixer_ref[...], axis=1, keepdims=True)
        payload_ref[:, :D] = patch.astype(BF16)
        lane = lax.broadcasted_iota(jnp.int32, (patch.shape[0], 128), 1)
        values = jnp.where(lane % 64 < 32, squares_ref[...], dots)
        high = values.astype(BF16).astype(F32)
        payload_ref[:, D:] = jnp.where(lane < 64, high, values - high).astype(BF16)


def attention_backward(core, grad, mixer_rows, inputs, normed, gain, weights, qkv, context, squares, token):
    rows = grad.shape[0]
    tps, _, width = context.shape
    depth = 2 * D // GROUP
    return pl.pallas_call(
        attention_backward_kernel,
        grid=(tps,),
        in_specs=[
            scalar_spec(),
            whole((rows, D)),
            whole((rows // PATCH, D)),
            whole((rows, D)),
            whole((rows, D)),
            whole((1, D)),
            attention_spec(weights),
            pl.BlockSpec((1, 3, rows, width), lambda j: (j, 0, 0, 0)),
            pl.BlockSpec((1, rows, width), lambda j: (j, 0, 0)),
            whole(squares.shape),
            anywhere(),
        ],
        out_specs=[
            whole((tps, rows, width)),
            whole((rows // PATCH, D)),
            whole((rows // PATCH, D + 128)),
            whole((1, D)),
            halves_spec(depth, 2 * width),
            halves_spec(depth, 2 * width),
        ],
        out_shape=[
            jax.ShapeDtypeStruct((tps, rows, width), BF16),
            jax.ShapeDtypeStruct((rows // PATCH, D), F32),
            jax.ShapeDtypeStruct((rows // PATCH, D + 128), BF16),
            jax.ShapeDtypeStruct((1, D), F32),
            halves_shape(tps, depth, 2 * width),
            halves_shape(tps, depth, 2 * width),
        ],
        scratch_shapes=[
            pltpu.VMEM((D, rows), BF16),
            pltpu.VMEM((rows, D), BF16),
            pltpu.VMEM((rows, D), F32),
            pltpu.VMEM((rows, width), BF16),
            pltpu.VMEM((rows, 3 * width), BF16),
        ],
        compiler_params=params(),
        name="attention_backward",
        cost_estimate=pl.CostEstimate(
            flops=4 * rows * D * D * 4, bytes_accessed=26 << 20, transcendentals=rows * 2048
        ),
    )(core, grad, mixer_rows, inputs, normed, gain, weights, qkv, context, squares, token)


def shifted(block, distance):
    devices = range(lax.axis_size(SEQ))
    route = [(i - distance, i) for i in devices if i - distance in devices]
    return lax.ppermute(block, SEQ, route)


def rms_scale(values):
    return values * inverse_rms(values)


def sequence_first(positions, lengths):
    offsets = jnp.cumsum(lengths) - lengths
    chosen = jnp.where(offsets[None, :] <= positions[:, None], offsets[None, :], 0)
    return jnp.max(chosen, axis=1)


def causal_conv(padded, weight, positions, first):
    count = positions.shape[0]
    total = jnp.zeros((count, padded.shape[1]), jnp.float32)
    for offset in range(CONV):
        lag = CONV - 1 - offset
        keep = (positions - lag >= first).astype(jnp.float32)[:, None]
        total = total + weight[offset][None, :] * padded[offset : offset + count] * keep
    return total


def front_part(padded, step_raw, conv_weight, step_bias, decay_log, positions, first):
    activated = jax.nn.silu(causal_conv(padded, conv_weight, positions, first))
    inner = activated.shape[1] - 2 * STATE
    count = positions.shape[0]
    inner_vals = activated[:, :inner].reshape(count, inner // HEAD_DIM, HEAD_DIM)
    bmatrix = activated[:, inner : inner + STATE]
    cmatrix = activated[:, inner + STATE :]
    steps = jax.nn.softplus(step_raw + step_bias[None, :])
    rates = -jnp.exp(decay_log)
    return (inner_vals, bmatrix, cmatrix, steps, rates)


def block_summary(inner_vals, bmatrix, steps, rates, positions, first):
    logs = jnp.cumsum(steps * rates[None, :], axis=0)
    final = logs[-1]
    in_last = (first == first[-1]).astype(jnp.float32)[:, None]
    weights = jnp.exp(final[None, :] - logs) * in_last * steps
    carried = jnp.exp(final) * (first[-1] < positions[0]).astype(jnp.float32)
    states = jnp.einsum("sh,shp,sn->hpn", weights, inner_vals, bmatrix, precision=highest)
    return (carried, states)


def block_output(inner_vals, bmatrix, cmatrix, steps, rates, skip_gain, incoming, positions, first):
    logs = jnp.cumsum(steps * rates[None, :], axis=0)
    count = positions.shape[0]
    same = (first[:, None] == first[None, :]) & (positions[None, :] <= positions[:, None])
    diff = logs.T[:, :, None] - logs.T[:, None, :]
    decay = jnp.where(same[None], jnp.exp(jnp.where(same[None], diff, 0.0)), 0.0)
    inner_prod = jnp.dot(cmatrix, bmatrix.T, precision=highest, preferred_element_type=jnp.float32)
    mixing = decay * inner_prod[None] * steps.T[:, None, :]
    within = jnp.einsum("hts,shp->thp", mixing, inner_vals, precision=highest)
    carry = jnp.exp(logs) * (first < positions[0]).astype(jnp.float32)[:, None]
    remote = jnp.einsum("tn,hpn->thp", cmatrix, incoming, precision=highest) * carry[:, :, None]
    result = within + remote + skip_gain[None, :, None] * inner_vals
    return result.reshape(count, -1)


def product(left, right, form):
    return jnp.einsum(form, left, right, preferred_element_type=jnp.float32)


def norm_backward(grad, values, gain):
    scale = inverse_rms(values)
    normed = values * scale
    scaled = grad * gain[None, :]
    result = scale * (scaled - normed * jnp.mean(scaled * normed, axis=-1, keepdims=True))
    return (result, jnp.sum(grad * normed, axis=0))


def high_low(values):
    high = values.astype(BF16)
    low = (values - high.astype(F32)).astype(BF16)
    return high, low


def reached(factors, states, distance):
    heads = factors.shape[0]
    columns = jnp.broadcast_to(factors[:, None], (heads, STATE))
    high, low = high_low(columns)
    packed = jnp.concatenate([states.reshape(-1, STATE).astype(BF16), high, low], axis=0)
    return reached_from(packed, distance).reshape(states.shape)


def reached_from(packed, distance):
    count = lax.axis_size(SEQ)
    heads = packed.shape[0] // (HEAD_DIM + 2)
    total = jnp.zeros((heads, HEAD_DIM, STATE), F32)
    chain = jnp.ones((heads, 1, 1), F32)
    for hop in range(1, count // 2 + 1):
        step = hop * distance
        route = [(i, i + step) for i in range(count) if 0 <= i + step < count]
        got = lax.ppermute(packed, SEQ, route).astype(F32)
        total = total + chain * got[: -2 * heads].reshape(total.shape)
        factor = (got[-2 * heads : -heads] + got[-heads:])[:, :1]
        chain = chain * factor[:, :, None]
    return total.reshape(-1, STATE)


def tied(array, *tokens):
    zero = sum(t[(0,) * t.ndim].astype(F32) * 0.0 for t in tokens)
    return (array.astype(F32) + zero).astype(array.dtype)


def swap(array, axis):
    return lax.ppermute(array, axis, [(0, 1), (1, 0)])


def picked(array, axis, index):
    return lax.dynamic_index_in_dim(array, index, axis, False)


def parallel_params(axes):
    return pltpu.CompilerParams(
        dimension_semantics=("arbitrary",) * axes, vmem_limit_bytes=32 * 1024 * 1024
    )


def first_sum_kernel(place_ref, *refs):
    ins, outs = refs[:8], refs[-4:]
    for k in range(4):
        total = ins[2 * k][...].astype(F32) + ins[2 * k + 1][...].astype(F32)
        outs[k][...] = total.reshape(outs[k].shape).astype(BF16)


def first_sum(place, own, got, tokens=()):
    _, _, tps, rows, cols = own.shape
    half = rows // 2
    block = (1, 1, 1, half, cols)
    maps = [
        lambda t, i, p: (i, 1 - p[1], t, 0, 0),
        lambda t, i, p: (i, p[1], t, 0, 0),
        lambda t, i, p: (1 - p[0], i, t, 1, 0),
        lambda t, i, p: (p[0], i, t, 1, 0),
    ]
    specs = [pl.BlockSpec(block, m) for m in maps for _ in range(2)]
    return pl.pallas_call(
        first_sum_kernel,
        grid_spec=pltpu.PrefetchScalarGridSpec(
            num_scalar_prefetch=1,
            grid=(tps, 2),
            in_specs=specs + [anywhere() for _ in tokens],
            out_specs=[
                pl.BlockSpec((1, 1, half, cols), lambda t, i, p: (i, t, 0, 0)) for _ in range(4)
            ],
        ),
        out_shape=[jax.ShapeDtypeStruct((2, tps, half, cols), BF16) for _ in range(4)],
        compiler_params=parallel_params(2),
        name="first_sum",
        cost_estimate=pl.CostEstimate(
            flops=own.size, bytes_accessed=6 * own.size, transcendentals=0
        ),
    )(place, *([own, got] * 4), *tokens)


def second_sum_kernel(place_ref, *refs):
    ins, outs = refs[:8], refs[-4:]
    for k in range(4):
        total = ins[2 * k][...].astype(F32) + ins[2 * k + 1][...].astype(F32)
        outs[k][...] = total.reshape(outs[k].shape).astype(BF16)


def second_sum(place, kept_one, got_one, kept_two, got_two, tokens=()):
    _, tps, half, cols = kept_one.shape
    block = (1, 1, half, cols)
    maps = [
        lambda t, p: (1 - p[0], t, 0, 0),
        lambda t, p: (p[0], t, 0, 0),
        lambda t, p: (1 - p[1], t, 0, 0),
        lambda t, p: (p[1], t, 0, 0),
    ]
    return pl.pallas_call(
        second_sum_kernel,
        grid_spec=pltpu.PrefetchScalarGridSpec(
            num_scalar_prefetch=1,
            grid=(tps,),
            in_specs=[pl.BlockSpec(block, m) for m in maps for _ in range(2)]
            + [anywhere() for _ in tokens],
            out_specs=[pl.BlockSpec((1, half, cols), lambda t, p: (t, 0, 0)) for _ in range(4)],
        ),
        out_shape=[jax.ShapeDtypeStruct((tps, half, cols), BF16) for _ in range(4)],
        compiler_params=parallel_params(1),
        name="second_sum",
        cost_estimate=pl.CostEstimate(
            flops=2 * kept_one.size, bytes_accessed=12 * kept_one.size, transcendentals=0
        ),
    )(place, *([kept_one, got_one] * 2), *([kept_two, got_two] * 2), *tokens)


def third_sum_kernel(one_ref, two_ref, three_ref, four_ref, *refs):
    out_ref = refs[-2]
    half = one_ref.shape[1]
    out_ref[0, :half] = (one_ref[0].astype(F32) + two_ref[0].astype(F32)).astype(BF16)
    out_ref[0, half:] = (three_ref[0].astype(F32) + four_ref[0].astype(F32)).astype(BF16)


def third_sum(kept_one, got_one, kept_two, got_two, carried):
    tps, half, cols = kept_one.shape
    return pl.pallas_call(
        third_sum_kernel,
        grid=(tps,),
        in_specs=[pl.BlockSpec((1, half, cols), lambda t: (t, 0, 0)) for _ in range(4)]
        + [anywhere()],
        out_specs=[pl.BlockSpec((1, 2 * half, cols), lambda t: (t, 0, 0)), anywhere()],
        out_shape=[
            jax.ShapeDtypeStruct((tps, 2 * half, cols), BF16),
            jax.ShapeDtypeStruct(carried.shape, carried.dtype),
        ],
        input_output_aliases={4: 1},
        compiler_params=parallel_params(1),
        name="third_sum",
        cost_estimate=pl.CostEstimate(
            flops=2 * kept_one.size, bytes_accessed=12 * kept_one.size, transcendentals=0
        ),
    )(kept_one, got_one, kept_two, got_two, carried)


def reduce_first(place, own, other, tokens=()):
    return first_sum(place, own, swap(other, "c"), tokens)


def reduce_second(place, sums, tokens=()):
    send_one, keep_one, send_two, keep_two = sums
    return second_sum(
        place, keep_one, swap(send_one, "b"), keep_two, swap(send_two, "a"), tokens
    )


def reduce_third(sums, carried):
    send_one, keep_one, send_two, keep_two = sums
    return third_sum(keep_one, swap(send_one, "a"), keep_two, swap(send_two, "b"), carried)


def over_groups(part):
    return lax.psum(part, "g") if lax.axis_size("g") > 1 else part


def reduce_last(summed):
    return over_groups(lax.psum_scatter(summed, "tp", scatter_dimension=0))


def exchange_last(summed):
    pieces = lax.all_to_all(summed, "tp", 0, 0)
    return over_groups(jnp.sum(pieces.astype(F32), axis=0).astype(BF16))


def unpack_kernel(
    grads_ref,
    expand_ref,
    shrink_ref,
    input_ref,
    output_ref,
    gate_ref,
    inner_ref,
    mixer_ref,
    state_ref,
):
    wide = grads_ref.shape[2]
    deep = D // GROUP
    width = input_ref.shape[2]

    def rows(low, count):
        return grads_ref[0, low : low + count].astype(F32)

    down = wide // GROUP
    for p in range(PIECES):
        base = 3 * deep * p
        for i in range(2):
            expand_ref[i, :, p * wide : (p + 1) * wide] = rows(base + i * deep, deep)
        for i in range(D // wide):
            shrink_ref[p, 0, :, i * wide : (i + 1) * wide] = rows(base + 2 * deep + i * down, down)
    base = 3 * deep * PIECES
    for k in range(3):
        part = rows(base + (k % 2) * deep, deep)
        input_ref[k] = part[:, (k // 2) * width : (k // 2 + 1) * width]
    part = rows(base + deep, deep)[:, width:]
    out_rows = width // GROUP
    for i in range(D // width):
        output_ref[:, i * width : (i + 1) * width] = part[i * out_rows : (i + 1) * out_rows]
    base = base + 2 * deep
    gate_ref[...] = rows(base, deep)
    inner_ref[...] = rows(base + deep, deep)
    for i in range(D // wide):
        mixer_ref[:, i * wide : (i + 1) * wide] = rows(base + 2 * deep + i * down, down)
    state = rows(base + 3 * deep, deep // 2)
    half = wide // 2
    for i in range(2):
        state_ref[i * deep // 2 : (i + 1) * deep // 2] = state[:, i * half : (i + 1) * half]


def unpack(grads, tps):
    _, total, wide = grads.shape
    deep, width, down = D // GROUP, D // tps, wide // GROUP
    shapes = [
        (2, D, PIECES * wide),
        (PIECES, GROUP, down, D),
        (3, D, width),
        (width, D),
        (D, wide),
        (D, wide),
        (wide, D),
        (D, wide // 2),
    ]
    specs = [
        pl.BlockSpec((2, deep, PIECES * wide), lambda j: (0, j, 0)),
        pl.BlockSpec((PIECES, 1, down, D), lambda j: (0, j, 0, 0)),
        pl.BlockSpec((3, deep, width), lambda j: (0, j, 0)),
        pl.BlockSpec((width // GROUP, D), lambda j: (j, 0)),
        pl.BlockSpec((deep, wide), lambda j: (j, 0)),
        pl.BlockSpec((deep, wide), lambda j: (j, 0)),
        pl.BlockSpec((down, D), lambda j: (j, 0)),
        pl.BlockSpec((deep, wide // 2), lambda j: (j, 0)),
    ]
    outs = pl.pallas_call(
        unpack_kernel,
        grid=(GROUP,),
        in_specs=[pl.BlockSpec((1, total, wide), lambda j: (j, 0, 0))],
        out_specs=specs,
        out_shape=[jax.ShapeDtypeStruct(shape, F32) for shape in shapes],
        compiler_params=parallel_params(1),
        name="unpack",
        cost_estimate=pl.CostEstimate(
            flops=grads.size, bytes_accessed=6 * grads.size, transcendentals=0
        ),
    )(grads)
    outs = list(outs)
    outs[1] = outs[1].reshape(PIECES * wide, D)
    return outs


def exact(left, right, dims):
    return lax.dot_general(
        left, right, (dims, ((), ())), precision=highest, preferred_element_type=F32
    )


NN, NT, TN = ((1,), (0,)), ((1,), (1,)), ((0,), (0,))


def column(array, index):
    lane = lax.broadcasted_iota(jnp.int32, array.shape, 1)
    return jnp.sum(jnp.where(lane == index, array, 0.0), axis=1, keepdims=True)


def by_head(pair, one, two):
    lane = lax.broadcasted_iota(jnp.int32, pair, 1)
    return jnp.where(lane < HEAD_DIM, one, two)


def only_head(array, j):
    lane = lax.broadcasted_iota(jnp.int32, array.shape, 1)
    return jnp.where((lane // HEAD_DIM) == j, array, 0.0)


def pair_of(ref, q):
    return ref[:, pl.ds(pl.multiple_of(q * 128, 128), 128)]


def gate_backward_kernel(
    returned_ref,
    weight_ref,
    gain_ref,
    gate_ref,
    mixed_ref,
    cmat_ref,
    reach_ref,
    factor_ref,
    token_ref,
    mix_ref,
    gate_back_ref,
    gain_grad_ref,
    out_grad_ref,
    packed_ref,
):
    back = returned_ref[:, :D]
    extra = returned_ref[:, D:].astype(F32)
    lane = lax.broadcasted_iota(jnp.int32, extra.shape, 1)
    squares = jnp.sum(jnp.where(lane % 64 == 0, extra, 0.0), axis=1, keepdims=True)
    dots = jnp.sum(jnp.where(lane % 64 == 32, extra, 0.0), axis=1, keepdims=True)
    scale = lax.rsqrt(squares / DI + epsilon)
    grad = mm_nt(back, weight_ref[...])
    gate = gate_ref[...]
    mixed = mixed_ref[...]
    gain = gain_ref[...]
    sigma = 1.0 / (1.0 + jnp.exp(-gate))
    act = gate * sigma
    normal = mixed * act * scale
    mix_ref[...] = (normal * gain).astype(BF16)
    gain_grad_ref[...] = jnp.sum(grad * normal, axis=0, keepdims=True)
    gated_grad = scale * (grad * gain - normal * (dots / DI))
    out_grad_ref[...] = gated_grad * act
    gate_back_ref[...] = (gated_grad * mixed * sigma * (1.0 + gate * (1.0 - sigma))).astype(BF16)
    reach = reach_ref[...]
    cmat = cmat_ref[...]
    width = gate.shape[1]
    for q in range(width // 128):
        part = out_grad_ref[:, q * 128 : (q + 1) * 128]
        part = part * by_head(part.shape, column(reach, 2 * q), column(reach, 2 * q + 1))
        packed_ref[q * 128 : (q + 1) * 128] = exact(part, cmat, TN).astype(BF16)
    packed_ref[width:] = factor_ref[...]


def gate_backward(returned, weight, gain, gate, mixed, cmat, reach, factors, token):
    count, width = gate.shape
    args = (returned, weight, gain, gate, mixed, cmat, reach, factors)
    shapes = [
        jax.ShapeDtypeStruct((count, width), BF16),
        jax.ShapeDtypeStruct((count, width), BF16),
        jax.ShapeDtypeStruct((1, width), F32),
        jax.ShapeDtypeStruct((count, width), F32),
        jax.ShapeDtypeStruct((width + factors.shape[0], STATE), BF16),
    ]
    return pl.pallas_call(
        gate_backward_kernel,
        grid=(1,),
        in_specs=[whole(a.shape) for a in args] + [anywhere()],
        out_specs=[whole(o.shape) for o in shapes],
        out_shape=shapes,
        compiler_params=params(),
        name="gate_backward",
        cost_estimate=pl.CostEstimate(
            flops=2 * count * D * width, bytes_accessed=6 << 20, transcendentals=count * width
        ),
    )(*args, token)


def chunk_backward_kernel(
    grad_ref,
    inner_ref,
    bmat_ref,
    cmat_ref,
    logs_ref,
    logs_row_ref,
    steps_row_ref,
    first_ref,
    first_row_ref,
    reach_ref,
    skip_ref,
    incoming_ref,
    token_ref,
    other_token_ref,
    inner_grad_ref,
    bmat_grad_ref,
    cmat_grad_ref,
    logs_grad_ref,
    logs_row_grad_ref,
    steps_row_grad_ref,
    skip_grad_ref,
    product_ref,
    product_grad_ref,
):
    count = grad_ref.shape[0]
    bmat, cmat = bmat_ref[...], cmat_ref[...]
    product_ref[...] = exact(cmat, bmat, NT)
    product_grad_ref[...] = jnp.zeros_like(product_grad_ref)
    cmat_grad_ref[...] = jnp.zeros_like(cmat_grad_ref)
    logs_grad_ref[...] = jnp.zeros_like(logs_grad_ref)
    skip_grad_ref[...] = jnp.zeros_like(skip_grad_ref)

    def one_pair(q, carry):
        inner = pair_of(inner_ref, q)
        grad = pair_of(grad_ref, q)
        incoming = incoming_ref[pl.ds(pl.multiple_of(q * 128, 128), 128), :]
        reading = exact(cmat, incoming, NT)
        row = lax.broadcasted_iota(jnp.int32, (count, count), 0)
        col = lax.broadcasted_iota(jnp.int32, (count, count), 1)
        same = (first_ref[...] == first_row_ref[...]) & (col <= row)
        logs = logs_ref[...]
        reach = reach_ref[...]
        skip = skip_ref[...]
        total = jnp.zeros_like(inner)
        reaches = []
        for j in range(2):
            h = 2 * q + j
            own_grad = only_head(grad, j)
            steps = steps_row_ref[pl.ds(h, 1), :]
            diff = column(logs, h) - logs_row_ref[pl.ds(h, 1), :]
            decay = jnp.where(same, jnp.exp(jnp.where(same, diff, 0.0)), 0.0)
            both = exact(own_grad, inner, NT) * decay
            mixing = decay * product_ref[...]
            product_grad_ref[...] += both * steps
            used = both * product_ref[...]
            total = total + exact(mixing * steps, own_grad, TN)
            over_rows = jnp.sum(used, axis=0, keepdims=True)
            reached_here = column(reach, h)
            reaches.append(reached_here)
            logs_grad = jnp.sum(used * steps, axis=1, keepdims=True)
            logs_grad = logs_grad + reached_here * jnp.sum(
                own_grad * reading, axis=1, keepdims=True
            )
            lane = lax.broadcasted_iota(jnp.int32, logs.shape, 1)
            logs_grad_ref[...] += jnp.where(lane == h, logs_grad, 0.0)
            logs_row_grad_ref[pl.ds(h, 1), :] = -steps * over_rows
            steps_row_grad_ref[pl.ds(h, 1), :] = over_rows
            lane = lax.broadcasted_iota(jnp.int32, skip.shape, 1)
            gained = jnp.sum(jnp.sum(own_grad * inner, axis=1, keepdims=True), axis=0, keepdims=True)
            skip_grad_ref[...] += jnp.where(lane == h, gained, 0.0)
        gains = by_head((1, 128), column(skip, 2 * q), column(skip, 2 * q + 1))
        inner_grad_ref[:, pl.ds(pl.multiple_of(q * 128, 128), 128)] = total + gains * grad
        weighted = grad * by_head(grad.shape, reaches[0], reaches[1])
        cmat_grad_ref[...] += exact(weighted, incoming, NN)
        return carry

    lax.fori_loop(0, grad_ref.shape[1] // 128, one_pair, 0)
    cmat_grad_ref[...] += exact(product_grad_ref[...], bmat, NN)
    bmat_grad_ref[...] = exact(product_grad_ref[...], cmat, TN)


def chunk_backward(args, *tokens):
    count, width = args[0].shape
    heads = args[5].shape[0]
    shapes = [
        jax.ShapeDtypeStruct((count, width), F32),
        jax.ShapeDtypeStruct((count, STATE), F32),
        jax.ShapeDtypeStruct((count, STATE), F32),
        jax.ShapeDtypeStruct((count, heads), F32),
        jax.ShapeDtypeStruct((heads, count), F32),
        jax.ShapeDtypeStruct((heads, count), F32),
        jax.ShapeDtypeStruct((1, heads), F32),
    ]
    return pl.pallas_call(
        chunk_backward_kernel,
        grid=(1,),
        in_specs=[whole(a.shape) for a in args] + [anywhere() for _ in tokens],
        out_specs=[whole(o.shape) for o in shapes],
        out_shape=shapes,
        scratch_shapes=[pltpu.VMEM((count, count), F32), pltpu.VMEM((count, count), F32)],
        compiler_params=params(),
        name="chunk_backward",
        cost_estimate=pl.CostEstimate(
            flops=24 * count * count * width, bytes_accessed=4 << 20, transcendentals=count * count * heads
        ),
    )(*args, *tokens)


def front_backward_kernel(hops, *refs):
    front_backward_body(refs[:hops], *refs[hops:])


def front_backward_body(
    got_refs,
    incoming_ref,
    inner_ref,
    bmat_ref,
    logs_ref,
    steps_ref,
    steps_row_ref,
    raw_row_ref,
    last_ref,
    factor_ref,
    rate_ref,
    bias_ref,
    inner_grad_ref,
    bmat_grad_ref,
    cmat_grad_ref,
    logs_grad_ref,
    logs_row_grad_ref,
    steps_row_grad_ref,
    padded_ref,
    conv_ref,
    keep_ref,
    token_ref,
    raw_grad_ref,
    head_grad_ref,
    conv_grad_ref,
    step_back_ref,
    bias_grad_ref,
    decay_grad_ref,
    act_grad_ref,
    logs_total_ref,
    steps_total_ref,
    padded_grad_ref,
    later_ref,
):
    count, width = inner_ref.shape
    heads = width // HEAD_DIM
    chain = jnp.ones((heads, STATE), F32)
    for k, got_ref in enumerate(got_refs):
        for h in range(heads):
            at = slice(h * HEAD_DIM, (h + 1) * HEAD_DIM)
            part = chain[h : h + 1] * got_ref[at, :].astype(F32)
            later_ref[at, :] = part if k == 0 else later_ref[at, :] + part
        factors = got_ref[width : width + 2 * heads, :].astype(F32)
        chain = chain * (factors[:heads] + factors[heads:])
    bmat = bmat_ref[...]
    logs, steps, last = logs_ref[...], steps_ref[...], last_ref[...]
    final = logs[count - 1 : count, :]
    fading = jnp.exp(final - logs) * last
    weights = fading * steps
    logs_total_ref[...] = logs_grad_ref[...]
    steps_total_ref[...] = jnp.zeros_like(steps_total_ref)
    bmat_total = bmat_grad_ref[...]
    lane = lax.broadcasted_iota(jnp.int32, logs.shape, 1)
    row = lax.broadcasted_iota(jnp.int32, logs.shape, 0)
    for q in range(width // 128):
        cols = slice(q * 128, (q + 1) * 128)
        later = later_ref[cols, :]
        inner = inner_ref[:, cols]
        reading = exact(bmat, later, NT)
        spread = by_head(inner.shape, column(weights, 2 * q), column(weights, 2 * q + 1))
        act_grad_ref[:, cols] = inner_grad_ref[:, cols] + spread * reading
        bmat_total = bmat_total + exact(inner * spread, later, NN)
        crossing = jnp.sum(later * incoming_ref[cols, :], axis=1, keepdims=True)
        for j in range(2):
            h = 2 * q + j
            gained = jnp.sum(only_head(inner * reading, j), axis=1, keepdims=True)
            part = lax.broadcasted_iota(jnp.int32, crossing.shape, 0) // HEAD_DIM == j
            crossed = jnp.sum(jnp.where(part, crossing, 0.0), axis=0, keepdims=True)
            crossed = crossed * column(factor_ref[...], h)
            steps_total_ref[...] += jnp.where(lane == h, fading * gained, 0.0)
            moved = column(weights, h) * gained
            ending = jnp.sum(moved, axis=0, keepdims=True) + crossed
            change = jnp.where(row == count - 1, ending - moved, -moved)
            logs_total_ref[...] += jnp.where(lane == h, change, 0.0)
    act_grad_ref[:, width : width + STATE] = bmat_total
    act_grad_ref[:, width + STATE :] = cmat_grad_ref[...]
    t = lax.broadcasted_iota(jnp.int32, (count, count), 0)
    u = lax.broadcasted_iota(jnp.int32, (count, count), 1)
    after = (t >= u).astype(F32)
    here = (t == u).astype(F32)
    reverse = exact(logs_total_ref[...], after, TN) + exact(logs_row_grad_ref[...], after, NN)
    rate = rate_ref[...]
    steps_grad = steps_row_grad_ref[...] + exact(steps_total_ref[...], here, TN) + rate * reverse
    decay_grad_ref[...] = rate * jnp.sum(steps_row_ref[...] * reverse, axis=1, keepdims=True)
    raw = raw_row_ref[...] + bias_ref[...]
    step_grad = steps_grad / (1.0 + jnp.exp(-raw))
    bias_grad_ref[...] = jnp.sum(step_grad, axis=1, keepdims=True)
    step_back_ref[...] = step_grad.astype(BF16)
    top = 8 - (CONV - 1)
    pre = jnp.zeros(act_grad_ref.shape, F32)
    keep = keep_ref[...]
    for k in range(CONV):
        kept = column(keep, k)
        pre = pre + conv_ref[k : k + 1, :] * padded_ref[top + k : top + k + count, :] * kept
    sigma = 1.0 / (1.0 + jnp.exp(-pre))
    act_grad_ref[...] = act_grad_ref[...] * sigma * (1.0 + pre * (1.0 - sigma))
    padded_grad_ref[...] = jnp.zeros_like(padded_grad_ref)
    for k in range(CONV):
        kept = act_grad_ref[...] * column(keep, k)
        conv_grad_ref[k : k + 1, :] = jnp.sum(
            kept * padded_ref[top + k : top + k + count, :], axis=0, keepdims=True
        )
        padded_grad_ref[top + k : top + k + count, :] += conv_ref[k : k + 1, :] * kept
    raw_grad_ref[...] = padded_grad_ref[8:, :]
    head_grad_ref[...] = padded_grad_ref[:8, :]


def front_backward(gots, args, token):
    count, heads = args[3].shape
    wide = args[17].shape[1]
    shapes = [
        jax.ShapeDtypeStruct((count, wide), F32),
        jax.ShapeDtypeStruct((8, wide), F32),
        jax.ShapeDtypeStruct((CONV, wide), F32),
        jax.ShapeDtypeStruct((heads, count), BF16),
        jax.ShapeDtypeStruct((heads, 1), F32),
        jax.ShapeDtypeStruct((heads, 1), F32),
    ]
    return pl.pallas_call(
        functools.partial(front_backward_kernel, len(gots)),
        grid=(1,),
        in_specs=[whole(a.shape) for a in gots + args] + [anywhere()],
        out_specs=[whole(o.shape) for o in shapes],
        out_shape=shapes,
        scratch_shapes=[
            pltpu.VMEM((count, wide), F32),
            pltpu.VMEM((count, heads), F32),
            pltpu.VMEM((count, heads), F32),
            pltpu.VMEM((count + 8, wide), F32),
            pltpu.VMEM(args[0].shape, F32),
        ],
        compiler_params=params(),
        name="front_backward",
        cost_estimate=pl.CostEstimate(
            flops=24 * count * STATE * wide, bytes_accessed=8 << 20, transcendentals=2 * count * wide
        ),
    )(*gots, *args, token)


def project_backward_kernel(
    mine_ref,
    gate_back_ref,
    inner_back_ref,
    state_back_ref,
    step_back_ref,
    gate_ref,
    inner_ref,
    state_ref,
    step_ref,
    rows_ref,
    normed_ref,
    gain_ref,
    own_ref,
    token_ref,
    blocks_ref,
    gain_grad_ref,
    step_grad_ref,
    total_ref,
):
    grad = mm_nt(gate_back_ref[...], gate_ref[...])
    grad = grad + mm_nt(inner_back_ref[...], inner_ref[...])
    grad = grad + mm_nt(state_back_ref[...], state_ref[...])
    grad = grad + mm_tn(step_back_ref[...], step_ref[...])
    step_grad_ref[...] = mm(step_back_ref[...], normed_ref[...])
    values = rows_ref[...].astype(F32)
    scale = inverse_rms(values)
    normal = values * scale
    gain_grad_ref[...] = jnp.sum(grad * normal, axis=0, keepdims=True)
    scaled = grad * gain_ref[...]
    total_ref[...] = scale * (scaled - normal * jnp.mean(scaled * normal, axis=-1, keepdims=True))
    share = own_ref.shape[0]
    at = pl.ds(pl.multiple_of(mine_ref[0] * share, share), share)
    total_ref[at, :] += own_ref[...]
    width = blocks_ref.shape[2]
    for i in range(blocks_ref.shape[0]):
        blocks_ref[i] = total_ref[:, i * width : (i + 1) * width].astype(BF16)


def project_backward(mine, args, tps, token):
    count = args[0].shape[0]
    heads = args[3].shape[0]
    shapes = [
        jax.ShapeDtypeStruct((tps, count, D // tps), BF16),
        jax.ShapeDtypeStruct((1, D), F32),
        jax.ShapeDtypeStruct((heads, D), F32),
    ]
    return pl.pallas_call(
        project_backward_kernel,
        grid=(1,),
        in_specs=[scalar_spec()] + [whole(a.shape) for a in args] + [anywhere()],
        out_specs=[whole(o.shape) for o in shapes],
        out_shape=shapes,
        scratch_shapes=[pltpu.VMEM((count, D), F32)],
        compiler_params=params(),
        name="project_backward",
        cost_estimate=pl.CostEstimate(
            flops=2 * count * D * 1288, bytes_accessed=6 << 20, transcendentals=count
        ),
    )(mine, *args, token)


def mixer_weight_grads_kernel(
    core_ref,
    normed_ref,
    gate_ref,
    inner_ref,
    state_ref,
    mix_ref,
    back_ref,
    token_ref,
    own_ref,
    other_ref,
):
    core = core_ref[0]
    normed = normed_ref[...]
    deep = D // GROUP
    wide = gate_ref.shape[1]
    put_halves(core, mm_tn(normed, gate_ref[...]), own_ref, other_ref, 0, deep)
    put_halves(core, mm_tn(normed, inner_ref[...]), own_ref, other_ref, deep, 2 * deep)
    rows = wide // GROUP
    mix = mix_ref[...]
    for i in range(D // wide):
        low = 2 * deep + i * rows
        grad = mm_tn(mix, back_ref[:, i * wide : (i + 1) * wide])
        put_halves(core, grad, own_ref, other_ref, low, low + rows)
    low = own_ref.shape[3] - deep // 2
    own, other = core_halves(core, mm_tn(normed, state_ref[...]).astype(BF16))
    for i in range(2):
        cols = slice(i * wide // 2, (i + 1) * wide // 2)
        rows_in = slice(i * deep // 2, (i + 1) * deep // 2)
        own_ref[:, :, 0, low:, cols] = own[:, :, rows_in]
        other_ref[:, :, 0, low:, cols] = other[:, :, rows_in]


def mixer_weight_grads(core, normed, gate, inner, state, mix, back, token):
    wide = gate.shape[1]
    deep = D // GROUP
    depth = 2 * deep + D // GROUP + deep // 2
    args = (normed, gate, inner, state, mix, back)
    return pl.pallas_call(
        mixer_weight_grads_kernel,
        grid=(1,),
        in_specs=[scalar_spec()] + [whole(a.shape) for a in args] + [anywhere()],
        out_specs=[halves_spec(depth, wide)] * 2,
        out_shape=[halves_shape(1, depth, wide)] * 2,
        compiler_params=params(),
        name="mixer_weight_grads",
        cost_estimate=pl.CostEstimate(
            flops=8 * normed.shape[0] * D * wide, bytes_accessed=8 << 20, transcendentals=0
        ),
    )(core, *args, token)


def shards(
    patches,
    byte_embed,
    seq_lengths,
    norm_global,
    proj_gate,
    proj_inner,
    proj_state,
    proj_step,
    step_bias,
    decay_log,
    conv_inner,
    conv_state,
    skip_gain,
    mixer_gain,
    proj_mixer,
    norm_attn,
    attn_input,
    attn_output,
    norm_ffn,
    expand_weight,
    shrink_weight,
    grad_output,
):
    count, quarter = patches.shape
    tps = lax.axis_size("tp")
    mine = lax.axis_index("tp")
    here = lax.axis_index(SEQ)
    core = lax.axis_index("c").reshape(1)
    tail = CONV - 1
    inner_width = proj_inner.shape[1]
    share = count // tps
    total_rows = byte_embed.shape[0]
    rows = total_rows // tps

    narrow = D // GROUP
    slot = lax.axis_index(INNER)

    def folded(array, width):
        rows_in = array.shape[0]
        return array.reshape(rows_in, -1, width).transpose(1, 0, 2).reshape(-1, width)

    attn_in_part = lax.dynamic_slice_in_dim(attn_input, slot * narrow, narrow, 1)
    out_rows = attn_output.shape[0] // GROUP
    attn_out_part = lax.dynamic_slice_in_dim(attn_output, slot * out_rows, out_rows, 0)
    attn_out_part = folded(attn_out_part, quarter)
    hidden_width = expand_weight.shape[2]
    wide = hidden_width // PIECES
    down_rows = wide // GROUP
    ffn_parts = []
    for p in range(PIECES):
        up_part = lax.dynamic_slice(
            expand_weight, (0, slot * narrow, p * wide), (2, narrow, wide)
        )
        down_part = lax.dynamic_slice_in_dim(
            shrink_weight, p * wide + slot * down_rows, down_rows, 0
        )
        ffn_parts.append([up_part.reshape(-1, wide), folded(down_part, wide)])
    attn_parts = [
        jnp.concatenate([attn_in_part[0], attn_in_part[2]], axis=1),
        jnp.concatenate([attn_in_part[1], attn_out_part], axis=1),
    ]
    weights_line = lax.all_gather(jnp.concatenate(attn_parts + ffn_parts[0], axis=0), "tp")
    last_part = jnp.concatenate(ffn_parts[1], axis=0)
    place = jnp.stack([lax.axis_index("a"), lax.axis_index("b")]).astype(jnp.int32)

    def to_rows(array):
        return lax.all_to_all(array.reshape(tps, rows, quarter), "tp", 0, 0)

    def to_columns(blocks):
        return lax.all_to_all(blocks, "tp", 0, 0).reshape(total_rows, quarter)

    positions = here * count + jnp.arange(count, dtype=jnp.int32)
    first = sequence_first(positions, seq_lengths)
    patch_rows = lax.all_gather(patches, "tp", axis=1, tiled=True)
    embed_rows = to_rows(byte_embed)
    cot_rows = to_rows(grad_output)
    global_in = patch_rows.astype(jnp.float32)
    normed = (rms_scale(global_in) * norm_global[None, :]).astype(jnp.bfloat16)
    gate_vals = product(normed, proj_gate, "rd,dc->rc")
    inner_raw = product(normed, proj_inner, "rd,dc->rc")
    state_raw = product(normed, proj_state, "rd,dc->rc")
    step_raw = product(normed, proj_step, "rd,dc->rc")
    raw = jnp.concatenate([inner_raw, state_raw], axis=1)
    before = shifted(raw[count - tail :], 1)
    padded = jnp.concatenate([before, raw], axis=0)
    conv_weight = jnp.concatenate([conv_inner, conv_state], axis=1)

    inner_vals, bmatrix, cmatrix, steps, rates = front_part(
        padded, step_raw, conv_weight, step_bias, decay_log, positions, first
    )
    carried, states = block_summary(inner_vals, bmatrix, steps, rates, positions, first)
    weights = lax.all_gather(tied(weights_line, states), INNER)
    incoming = reached(carried, states, 1)
    mixed = block_output(
        inner_vals, bmatrix, cmatrix, steps, rates, skip_gain, incoming, positions, first
    )
    gate_act = jax.nn.silu(gate_vals)
    gated = mixed * gate_act
    squares = jnp.sum(gated * gated, axis=1, keepdims=True)
    partial = product((gated * mixer_gain[None, :]).astype(BF16), proj_mixer, "rc,cd->rd")
    square_high, square_low = high_low(jnp.broadcast_to(squares, (count, 64)))
    partial = partial + embed_rows[0, 0, 0].astype(F32) * 0.0
    sent = jnp.concatenate([partial.astype(BF16), square_high, square_low], axis=1)
    summed = jnp.sum(
        lax.all_to_all(sent.reshape(tps, share, -1), "tp", 0, 0).astype(F32), axis=0
    )
    own_squares = summed[:, D : D + 1] + summed[:, D + 64 : D + 65]
    last_part = tied(last_part, own_squares)
    last_line = lax.all_to_all(
        jnp.broadcast_to(last_part[None], (tps,) + last_part.shape), "tp", 0, 0
    )
    last_weights = lax.all_gather(last_line, INNER)
    mixer_rows = summed[:, :D] * lax.rsqrt(own_squares / DI + epsilon)
    own_patches = lax.dynamic_slice_in_dim(patch_rows, mine * share, share, 0)
    global_out = own_patches.astype(F32) + mixer_rows

    logs = jnp.cumsum(steps * rates[None, :], axis=0)
    from_before = (first < positions[0]).astype(F32)[:, None]
    reach = jnp.exp(logs) * from_before
    factor_high, factor_low = high_low(jnp.broadcast_to(carried[:, None], (carried.size, STATE)))
    factors = jnp.concatenate([factor_high, factor_low], axis=0)
    flat_inner = inner_vals.reshape(count, -1)
    flat_incoming = incoming.reshape(-1, STATE)
    keep = jnp.stack(
        [(positions - (CONV - 1 - k) >= first).astype(F32) for k in range(CONV)], axis=1
    )
    logs_row, steps_row, raw_row = logs.T, steps.T, step_raw.T
    last = (first == first[-1]).astype(F32)[:, None]
    rate_column, bias_column = rates[:, None], step_bias[:, None]
    wide_padded = jnp.pad(padded, ((8 - tail, 0), (0, 0)))
    step_weight = proj_step.T
    prepared = (
        reach, factors, keep, logs_row, steps_row, raw_row, last, rate_column, bias_column,
        wide_padded, step_weight, flat_inner, flat_incoming,
    )

    hidden, attn_in, attn_normed, qkv, context = attention_forward(
        embed_rows, global_out[:, None, :], norm_attn[None, :], weights, prepared
    )
    ffn_normed, ffn_turned, cot_whole, out_acc, normed_acc, own_first, other_first = (
        feed_forward_first(core, hidden, cot_rows, norm_ffn[None, :], weights)
    )
    first_one = reduce_first(place, own_first, other_first)
    first_two = reduce_second(place, first_one)
    layer_blocks, hidden_grad, norm_ffn_part, last_grad = feed_forward_last(
        core,
        hidden,
        cot_whole,
        norm_ffn[None, :],
        last_weights,
        ffn_normed,
        ffn_turned,
        out_acc,
        normed_acc,
        first_two[0],
    )
    layer_output = to_columns(layer_blocks)
    first_three, hidden_grad = reduce_third(first_two, hidden_grad)
    embed_blocks, own_grad, payload, norm_attn_part, own_attn, other_attn = attention_backward(
        core,
        hidden_grad,
        mixer_rows,
        attn_in,
        attn_normed,
        norm_attn[None, :],
        weights,
        qkv,
        context,
        own_squares,
        layer_output,
    )
    last_three = lax.psum_scatter(last_grad, INNER, scatter_dimension=0)
    embed_columns = to_columns(embed_blocks)
    embed_grad = embed_columns.astype(F32)

    attn_one = reduce_first(place, own_attn, other_attn)
    returned = lax.all_gather(payload, "tp", axis=0, tiled=True)
    mix_back_in = returned[:, :D]
    mix_low, gate_back, mixer_gain_grad, mixed_grad, packed = gate_backward(
        returned,
        proj_mixer,
        mixer_gain[None, :],
        gate_vals,
        mixed,
        cmatrix,
        reach,
        factors,
        attn_one[0],
    )
    chunk_grads = chunk_backward(
        (
            mixed_grad,
            flat_inner,
            bmatrix,
            cmatrix,
            logs,
            logs_row,
            steps_row,
            first[:, None],
            first[None, :],
            reach,
            skip_gain[None, :],
            flat_incoming,
        ),
        attn_one[0],
        own_attn,
    )
    ffn_sums = tied(jnp.concatenate([first_three, last_three], axis=1), chunk_grads[6])
    ffn_part = reduce_last(ffn_sums)
    attn_two = reduce_second(place, attn_one, (chunk_grads[0],))
    skip_gain_grad = chunk_grads[6][0]
    devices = lax.axis_size(SEQ)
    gots = tuple(
        lax.ppermute(packed, SEQ, [(i + hop, i) for i in range(devices - hop)])
        for hop in range(1, devices // 2 + 1)
    )
    raw_grad, head_grad, conv_grad, step_back, step_bias_grad, decay_log_grad = front_backward(
        gots,
        (
            flat_incoming,
            flat_inner,
            bmatrix,
            logs,
            steps,
            steps_row,
            raw_row,
            last,
            carried[None, :],
            rate_column,
            bias_column,
        )
        + tuple(chunk_grads[:6])
        + (
            wide_padded,
            conv_weight,
            keep,
        ),
        attn_two[1],
    )
    step_bias_grad, decay_log_grad = step_bias_grad[:, 0], decay_log_grad[:, 0]
    tail_grad = shifted(head_grad, -1)
    raw_grad = jnp.concatenate(
        [raw_grad[: count - 8], raw_grad[count - 8 :] + tail_grad], axis=0
    ).astype(BF16)
    inner_back, state_back = raw_grad[:, :inner_width], raw_grad[:, inner_width:]
    own_mixer, other_mixer = mixer_weight_grads(
        core, normed, gate_back, inner_back, state_back, mix_low, mix_back_in, attn_two[1]
    )
    mixer_one = reduce_first(place, own_mixer, other_mixer)
    attn_three, mixer_kept = reduce_third(attn_two, mixer_one[1])
    attn_part = reduce_last(tied(attn_three, ffn_part))
    mixer_two = reduce_second(place, (mixer_one[0], mixer_kept) + tuple(mixer_one[2:]))
    mixer_three, step_back = reduce_third(mixer_two, step_back)
    mixer_three = mixer_three[0]
    mixer_part = over_groups(mixer_three)
    state_rows = lax.all_gather(mixer_part[3 * narrow :], "tp")
    state_rows = jnp.sum(state_rows.astype(F32), axis=0).astype(BF16)
    columns, norm_global_part, step_grad = project_backward(
        mine.reshape(1),
        (
            gate_back,
            inner_back,
            state_back,
            step_back,
            proj_gate,
            proj_inner,
            proj_state,
            step_weight,
            patch_rows,
            normed,
            norm_global[None, :],
            own_grad,
        ),
        tps,
        state_rows,
    )
    norm_global_part = norm_global_part[0]
    shared = jnp.concatenate(
        [
            conv_grad[:, inner_width:].reshape(-1),
            norm_attn_part[0],
            norm_ffn_part[0],
            norm_global_part,
        ]
    ).reshape(-1, quarter)
    shared_high, shared_low = high_low(shared)
    shared_rows = jnp.concatenate([shared_high, shared_low], axis=0)
    returned = lax.all_to_all(
        jnp.concatenate(
            [columns, jnp.broadcast_to(shared_rows[None], (tps,) + shared_rows.shape)], axis=1
        ),
        "tp",
        0,
        0,
    )
    returned = jnp.sum(returned.astype(F32), axis=0)
    patch_grad = returned[:count]
    shared = returned[count : count + shared.shape[0]] + returned[count + shared.shape[0] :]
    shared = shared.reshape(-1)
    held = conv_state.size
    shared = (
        shared[:held].reshape(conv_state.shape),
        shared[held : held + D],
        shared[held + D : held + 2 * D],
        shared[held + 2 * D :],
    )
    (
        conv_state_grad,
        norm_attn_grad,
        norm_ffn_grad,
        norm_global_grad,
        proj_step_grad,
        step_bias_grad,
        decay_log_grad,
        conv_inner_grad,
        skip_gain_grad,
        mixer_gain_grad,
    ) = lax.psum(
        shared
        + (
            step_grad.T,
            step_bias_grad,
            decay_log_grad,
            conv_grad[:, :inner_width],
            skip_gain_grad,
            mixer_gain_grad[0],
        ),
        SEQ,
    )
    ffn_depth, attn_depth = 3 * narrow, 2 * narrow
    all_grads = lax.all_gather(
        jnp.concatenate([ffn_part, attn_part, mixer_part[: 3 * narrow], state_rows]), INNER
    )
    (
        expand_grad,
        shrink_grad,
        attn_input_grad,
        attn_output_grad,
        proj_gate_grad,
        proj_inner_grad,
        proj_mixer_grad,
        proj_state_grad,
    ) = unpack(all_grads, tps)
    return (
        layer_output,
        embed_grad,
        patch_grad,
        norm_global_grad,
        proj_gate_grad,
        proj_inner_grad,
        proj_state_grad,
        proj_step_grad,
        step_bias_grad,
        decay_log_grad,
        conv_inner_grad,
        conv_state_grad,
        skip_gain_grad,
        mixer_gain_grad,
        proj_mixer_grad,
        norm_attn_grad,
        attn_input_grad,
        attn_output_grad,
        norm_ffn_grad,
        expand_grad,
        shrink_grad,
    )


def solution(mesh):
    seq, tps = mesh.shape["seq"], mesh.shape["tp"]
    fine = Mesh(mesh.devices.reshape(seq // GROUP, 2, 2, 2, tps), SEQ + ("tp",))
    rows_cols = P(SEQ, "tp")
    last = P(None, "tp")
    lead = P("tp", None)
    return jax.shard_map(
        shards,
        mesh=fine,
        in_specs=(
            rows_cols,
            rows_cols,
            P(),
            P(),
            last,
            last,
            P(),
            last,
            P("tp"),
            P("tp"),
            last,
            P(),
            P("tp"),
            P("tp"),
            lead,
            P(),
            P(None, None, "tp"),
            lead,
            P(),
            P(None, None, "tp"),
            lead,
            rows_cols,
        ),
        out_specs=(
            rows_cols,
            rows_cols,
            rows_cols,
            P(),
            last,
            last,
            P(),
            last,
            P("tp"),
            P("tp"),
            last,
            P(),
            P("tp"),
            P("tp"),
            lead,
            P(),
            P(None, None, "tp"),
            lead,
            P(),
            P(None, None, "tp"),
            lead,
        ),
        check_vma=False,
    )
```

```python
import functools

import jax
import jax.numpy as jnp
from jax import lax
from jax.experimental import pallas as pl
from jax.experimental.pallas import tpu as pltpu
from jax.sharding import Mesh, PartitionSpec as P

D = 1024
HEAD_DIM = 64
STATE = 128
HEADS_A = 16
CONV = 4
PATCH = 8
DI = 2048
GROUP = 8
TILE = 128
PIECES = 2

epsilon = 1e-05
highest = lax.Precision.HIGHEST
F32 = jnp.float32
BF16 = jnp.bfloat16
SEQ = ("g", "a", "b", "c")
INNER = ("a", "b", "c")


def mm(left, right):
    return lax.dot_general(left, right, (((1,), (0,)), ((), ())), preferred_element_type=F32)


def mm_nt(left, right):
    return lax.dot_general(left, right, (((1,), (1,)), ((), ())), preferred_element_type=F32)


def mm_tn(left, right):
    return lax.dot_general(left, right, (((0,), (0,)), ((), ())), preferred_element_type=F32)


def inverse_rms(values):
    return lax.rsqrt(jnp.mean(values * values, axis=-1, keepdims=True) + epsilon)


def params(limit=60):
    return pltpu.CompilerParams(
        dimension_semantics=("arbitrary",), vmem_limit_bytes=limit * 1024 * 1024
    )


def whole(shape):
    return pl.BlockSpec(shape, lambda j: (0,) * len(shape))


def scalar_spec():
    return pl.BlockSpec(memory_space=pltpu.SMEM)


def halves_shape(tps, depth, wide):
    return jax.ShapeDtypeStruct((2, 2, tps, depth, wide), BF16)


def halves_spec(depth, wide):
    return pl.BlockSpec((2, 2, 1, depth, wide), lambda j: (0, 0, j, 0, 0))


def anywhere():
    return pl.BlockSpec(memory_space=pl.ANY)


def weight_specs(weights, first):
    parts, _, _, wide = weights.shape
    block = (parts, 1, D // GROUP, wide)
    return [
        pl.BlockSpec(block, functools.partial(lambda k, j: (0, j, k, 0), first + k))
        for k in range(3)
    ]


def attention_spec(weights):
    parts, _, _, wide = weights.shape
    return pl.BlockSpec((parts, 1, 2 * D // GROUP, wide), lambda j: (0, j, 0, 0))


def attention_view(weight_ref, k, width):
    deep = D // weight_ref.shape[0]
    rows = slice((k % 2) * deep, (k % 2 + 1) * deep)
    return weight_ref.at[:, 0, rows, (k // 2) * width : (k // 2 + 1) * width]


def head_mask(width):
    lane = lax.broadcasted_iota(jnp.int32, (1, width), 1) // (D // HEADS_A)
    return [lane == h for h in range(width // (D // HEADS_A))]


def split_heads(tile, masks):
    zero = jnp.zeros_like(tile)
    return jnp.concatenate([jnp.where(m, tile, zero) for m in masks], axis=0)


def tile_mask(heads):
    row = lax.broadcasted_iota(jnp.int32, (heads * TILE, TILE), 0) % TILE
    col = lax.broadcasted_iota(jnp.int32, (heads * TILE, TILE), 1)
    return (row // PATCH == col // PATCH) & (col <= row)


def tile_probs(query_split, keys, keep):
    scores = mm_nt(query_split, keys) * ((D // HEADS_A) ** -0.5)
    scores = jnp.where(keep, scores, -1e30)
    expo = jnp.exp(scores - jnp.max(scores, axis=-1, keepdims=True))
    return expo * (1.0 / jnp.sum(expo, axis=-1, keepdims=True))


def beside(stacked, heads):
    return jnp.concatenate([stacked[h * TILE : (h + 1) * TILE] for h in range(heads)], axis=1)


def attention_forward_kernel(
    embed_ref, global_ref, gain_ref, weight_ref, *refs
):
    hidden_ref, input_ref, normed_ref, qkv_ref, context_ref = refs[-5:]
    step = pl.program_id(0)
    blocks, rows, width = embed_ref.shape
    parts = weight_ref.shape[0]

    @pl.when(step == 0)
    def _():
        embed = jnp.concatenate([embed_ref[i] for i in range(blocks)], axis=1).astype(F32)
        spread = jnp.broadcast_to(global_ref[...], (rows // PATCH, PATCH, D)).reshape(rows, D)
        total = embed + spread
        hidden_ref[...] = total
        low = total.astype(BF16)
        input_ref[...] = low
        values = low.astype(F32)
        normed_ref[...] = (values * inverse_rms(values) * gain_ref[...]).astype(BF16)

    normed = normed_ref[...]
    for k in range(3):
        weight = attention_view(weight_ref, k, width)[...].reshape(D, width)
        qkv_ref[0, k] = mm(normed, weight).astype(BF16)
    masks = head_mask(width)
    heads = len(masks)
    keep = tile_mask(heads)
    for r in range(rows // TILE):
        at = slice(r * TILE, (r + 1) * TILE)
        query = split_heads(qkv_ref[0, 0, at], masks)
        probs = tile_probs(query, qkv_ref[0, 1, at], keep).astype(BF16)
        values = split_heads(qkv_ref[0, 2, at], masks)
        context_ref[0, at] = mm(beside(probs, heads), values).astype(BF16)
    context = context_ref[0]
    piece = width // parts
    outward = attention_view(weight_ref, 3, width)
    for c in range(D // width):
        weight = outward[:, c * piece : (c + 1) * piece].reshape(width, width)
        cols = slice(c * width, (c + 1) * width)
        hidden_ref[:, cols] += mm(context, weight)


def attention_forward(embed, global_rows, gain, weights, tokens):
    blocks, rows, width = embed.shape
    tps = weights.shape[1]
    return pl.pallas_call(
        attention_forward_kernel,
        grid=(tps,),
        in_specs=[
            whole((blocks, rows, width)),
            whole((rows // PATCH, 1, D)),
            whole((1, D)),
            attention_spec(weights),
            *(anywhere() for _ in tokens),
        ],
        out_specs=[
            whole((rows, D)),
            whole((rows, D)),
            whole((rows, D)),
            pl.BlockSpec((1, 3, rows, width), lambda j: (j, 0, 0, 0)),
            pl.BlockSpec((1, rows, width), lambda j: (j, 0, 0)),
        ],
        out_shape=[
            jax.ShapeDtypeStruct((rows, D), F32),
            jax.ShapeDtypeStruct((rows, D), BF16),
            jax.ShapeDtypeStruct((rows, D), BF16),
            jax.ShapeDtypeStruct((tps, 3, rows, width), BF16),
            jax.ShapeDtypeStruct((tps, rows, width), BF16),
        ],
        compiler_params=params(),
        name="attention_forward",
        cost_estimate=pl.CostEstimate(
            flops=2 * rows * D * D * 4, bytes_accessed=14 << 20, transcendentals=rows * 2048
        ),
    )(embed, global_rows, gain, weights, *tokens)


def core_halves(core, grad):
    parts = grad.reshape((2, 2, 2, grad.shape[0] // GROUP) + grad.shape[1:])
    mine = jnp.where(core == 0, parts[:, :, 0], parts[:, :, 1])
    other = jnp.where(core == 0, parts[:, :, 1], parts[:, :, 0])
    return mine, other


def put_halves(core, grad, own_ref, other_ref, low, high, cols=slice(None)):
    own, other = core_halves(core, grad.astype(BF16))
    own_ref[:, :, 0, low:high, cols] = own
    other_ref[:, :, 0, low:high, cols] = other


def put_whole(core, grad, grad_ref, low, high):
    parts = grad_ref.shape[0]
    grad_ref[:, 0, low:high] = grad.astype(BF16).reshape((parts, -1) + grad.shape[1:])


def feed_forward_step(
    core_ref, weight_refs, cot, normed_ref, turned_ref, out_acc, normed_acc, put
):
    parts, _, _, wide = weight_refs[0].shape
    deep = D // parts
    core = core_ref[0]
    normed = normed_ref[...]
    gate_weight = weight_refs[0][:, 0].reshape(D, wide)
    up_weight = weight_refs[1][:, 0].reshape(D, wide)
    piece = wide // parts
    folds = D // wide
    down_weight = jnp.concatenate(
        [
            weight_refs[2][:, 0, i * piece : (i + 1) * piece].reshape(wide, wide)
            for i in range(folds)
        ],
        axis=1,
    )
    gate = mm(normed, gate_weight)
    up = mm(normed, up_weight)
    sigma = 1.0 / (1.0 + jnp.exp(-gate))
    swish = gate * sigma
    activ = (swish * up).astype(BF16)
    out_acc[...] += mm(activ, down_weight)
    shrink = mm_tn(activ, cot)
    for i in range(folds):
        low = 2 * deep + i * piece
        put(core, shrink[:, i * wide : (i + 1) * wide], low, low + piece)
    dactiv = mm_nt(cot, down_weight)
    dgate = (dactiv * up * sigma * (1.0 + gate * (1.0 - sigma))).astype(BF16)
    dup = (dactiv * swish).astype(BF16)
    normed_acc[...] += mm_nt(dgate, gate_weight) + mm_nt(dup, up_weight)
    turned = turned_ref[...]
    put(core, mm(turned, dgate), 0, deep)
    put(core, mm(turned, dup), deep, 2 * deep)


def feed_forward_first_kernel(
    core_ref,
    hidden_ref,
    cot_ref,
    gain_ref,
    gate_ref,
    up_ref,
    down_ref,
    normed_ref,
    turned_ref,
    cot_out,
    out_acc,
    normed_acc,
    own_ref,
    other_ref,
):
    blocks, _, width = cot_ref.shape

    @pl.when(pl.program_id(0) == 0)
    def _():
        values = hidden_ref[...].astype(BF16).astype(F32)
        normed = (values * inverse_rms(values) * gain_ref[...]).astype(BF16)
        normed_ref[...] = normed
        turned_ref[...] = normed.astype(F32).T.astype(BF16)
        for i in range(blocks):
            cot_out[:, i * width : (i + 1) * width] = cot_ref[i]
        out_acc[...] = hidden_ref[...]
        normed_acc[...] = jnp.zeros_like(normed_acc)

    def put(core, grad, low, high):
        put_halves(core, grad, own_ref, other_ref, low, high)

    feed_forward_step(
        core_ref,
        (gate_ref, up_ref, down_ref),
        cot_out[...],
        normed_ref,
        turned_ref,
        out_acc,
        normed_acc,
        put,
    )


def feed_forward_last_kernel(
    core_ref,
    hidden_ref,
    cot_ref,
    gain_ref,
    gate_ref,
    up_ref,
    down_ref,
    normed_ref,
    turned_ref,
    out_in,
    normed_in,
    token_ref,
    layer_ref,
    grad_ref,
    gain_grad_ref,
    weight_grad_ref,
    out_acc,
    normed_acc,
):
    step = pl.program_id(0)
    blocks, _, width = layer_ref.shape

    @pl.when(step == 0)
    def _():
        out_acc[...] = out_in[...]
        normed_acc[...] = normed_in[...]

    def put(core, grad, low, high):
        put_whole(core, grad, weight_grad_ref, low, high)

    feed_forward_step(
        core_ref,
        (gate_ref, up_ref, down_ref),
        cot_ref[...],
        normed_ref,
        turned_ref,
        out_acc,
        normed_acc,
        put,
    )

    @pl.when(step == pl.num_programs(0) - 1)
    def _():
        layer = out_acc[...].astype(BF16)
        for i in range(blocks):
            layer_ref[i] = layer[:, i * width : (i + 1) * width]
        values = hidden_ref[...].astype(BF16).astype(F32)
        scale = inverse_rms(values)
        normal = values * scale
        grad = normed_acc[...]
        gain_grad_ref[...] = jnp.sum(grad * normal, axis=0, keepdims=True)
        scaled = grad * gain_ref[...]
        back = scale * (scaled - normal * jnp.mean(scaled * normal, axis=-1, keepdims=True))
        grad_ref[...] = cot_ref[...].astype(F32) + back


def feed_forward_cost(rows, weights):
    _, tps, _, wide = weights.shape
    return pl.CostEstimate(
        flops=18 * rows * D * wide * tps,
        bytes_accessed=12 * D * wide * tps + 16 * rows * D,
        transcendentals=rows * wide * tps,
    )


def feed_forward_first(core, hidden, cot, gain, weights):
    rows = hidden.shape[0]
    _, tps, _, wide = weights.shape
    depth = 3 * D // GROUP
    return pl.pallas_call(
        feed_forward_first_kernel,
        grid=(tps,),
        in_specs=[
            scalar_spec(),
            whole((rows, D)),
            whole(cot.shape),
            whole((1, D)),
            *weight_specs(weights, 2),
        ],
        out_specs=[
            whole((rows, D)),
            whole((D, rows)),
            whole((rows, D)),
            whole((rows, D)),
            whole((rows, D)),
            halves_spec(depth, wide),
            halves_spec(depth, wide),
        ],
        out_shape=[
            jax.ShapeDtypeStruct((rows, D), BF16),
            jax.ShapeDtypeStruct((D, rows), BF16),
            jax.ShapeDtypeStruct((rows, D), BF16),
            jax.ShapeDtypeStruct((rows, D), F32),
            jax.ShapeDtypeStruct((rows, D), F32),
            halves_shape(tps, depth, wide),
            halves_shape(tps, depth, wide),
        ],
        compiler_params=params(),
        name="feed_forward_first",
        cost_estimate=feed_forward_cost(rows, weights),
    )(core, hidden, cot, gain, weights, weights, weights)


def feed_forward_last(
    core, hidden, cot, gain, weights, normed, turned, out_in, normed_in, token
):
    rows = hidden.shape[0]
    _, tps, _, wide = weights.shape
    depth = 3 * D // GROUP
    width = D // tps
    return pl.pallas_call(
        feed_forward_last_kernel,
        grid=(tps,),
        in_specs=[
            scalar_spec(),
            whole((rows, D)),
            whole((rows, D)),
            whole((1, D)),
            *weight_specs(weights, 0),
            whole((rows, D)),
            whole((D, rows)),
            whole((rows, D)),
            whole((rows, D)),
            anywhere(),
        ],
        out_specs=[
            whole((tps, rows, width)),
            whole((rows, D)),
            whole((1, D)),
            pl.BlockSpec((GROUP, 1, depth, wide), lambda j: (0, j, 0, 0)),
        ],
        out_shape=[
            jax.ShapeDtypeStruct((tps, rows, width), BF16),
            jax.ShapeDtypeStruct((rows, D), F32),
            jax.ShapeDtypeStruct((1, D), F32),
            jax.ShapeDtypeStruct((GROUP, tps, depth, wide), BF16),
        ],
        scratch_shapes=[pltpu.VMEM((rows, D), F32), pltpu.VMEM((rows, D), F32)],
        compiler_params=params(),
        name="feed_forward_last",
        cost_estimate=feed_forward_cost(rows, weights),
    )(core, hidden, cot, gain, weights, weights, weights, normed, turned, out_in, normed_in, token)


def attention_backward_kernel(
    core_ref,
    grad_ref,
    mixer_ref,
    input_ref,
    normed_ref,
    gain_ref,
    weight_ref,
    qkv_ref,
    context_ref,
    squares_ref,
    token_ref,
    embed_ref,
    global_ref,
    payload_ref,
    gain_grad_ref,
    own_ref,
    other_ref,
    turned_ref,
    low_ref,
    normed_acc,
    context_grad_ref,
    qkv_grad_ref,
):
    step = pl.program_id(0)
    rows = grad_ref.shape[0]
    blocks, _, width = embed_ref.shape
    parts = weight_ref.shape[0]
    deep = D // parts
    scaling = (D // HEADS_A) ** -0.5
    core = core_ref[0]

    @pl.when(step == 0)
    def _():
        turned_ref[...] = normed_ref[...].astype(F32).T.astype(BF16)
        low_ref[...] = grad_ref[...].astype(BF16)
        normed_acc[...] = jnp.zeros_like(normed_acc)

    low = low_ref[...]
    context = context_ref[0]
    piece = width // parts
    total = jnp.zeros((rows, width), F32)
    outward = attention_view(weight_ref, 3, width)
    for c in range(D // width):
        first = deep + c * piece
        weight = outward[:, c * piece : (c + 1) * piece].reshape(width, width)
        columns = low[:, c * width : (c + 1) * width]
        total = total + mm_nt(columns, weight)
        put_halves(
            core,
            mm_tn(context, columns),
            own_ref,
            other_ref,
            first,
            first + piece,
            slice(width, 2 * width),
        )
    context_grad_ref[...] = total.astype(BF16)
    masks = head_mask(width)
    heads = len(masks)
    keep = tile_mask(heads)
    for r in range(rows // TILE):
        at = slice(r * TILE, (r + 1) * TILE)
        query = split_heads(qkv_ref[0, 0, at], masks)
        keys = qkv_ref[0, 1, at]
        probs = tile_probs(query, keys, keep)
        dcontext = split_heads(context_grad_ref[at], masks)
        dprobs = mm_nt(dcontext, qkv_ref[0, 2, at])
        dvalues = mm_tn(probs.astype(BF16), dcontext)
        inner = jnp.sum(dprobs * probs, axis=-1, keepdims=True)
        dscores = (probs * (dprobs - inner)).astype(BF16)
        dquery = mm(beside(dscores, heads), split_heads(keys, masks)) * scaling
        dkeys = mm_tn(dscores, query) * scaling
        qkv_grad_ref[at, :width] = dquery.astype(BF16)
        qkv_grad_ref[at, width : 2 * width] = dkeys.astype(BF16)
        qkv_grad_ref[at, 2 * width :] = dvalues.astype(BF16)
    turned = turned_ref[...]
    for k in range(3):
        part = qkv_grad_ref[:, k * width : (k + 1) * width]
        weight = attention_view(weight_ref, k, width)[...].reshape(D, width)
        normed_acc[...] += mm_nt(part, weight)
        first = (k % 2) * deep
        put_halves(
            core,
            mm(turned, part),
            own_ref,
            other_ref,
            first,
            first + deep,
            slice((k // 2) * width, (k // 2 + 1) * width),
        )

    @pl.when(step == pl.num_programs(0) - 1)
    def _():
        values = input_ref[...].astype(F32)
        scale = inverse_rms(values)
        normal = values * scale
        grad = normed_acc[...]
        gain_grad_ref[...] = jnp.sum(grad * normal, axis=0, keepdims=True)
        scaled = grad * gain_ref[...]
        back = scale * (scaled - normal * jnp.mean(scaled * normal, axis=-1, keepdims=True))
        result = grad_ref[...] + back
        for i in range(blocks):
            embed_ref[i] = result[:, i * width : (i + 1) * width].astype(BF16)
        patch = jnp.sum(result.reshape(rows // PATCH, PATCH, D), axis=1)
        global_ref[...] = patch
        dots = jnp.sum(patch * mixer_ref[...], axis=1, keepdims=True)
        payload_ref[:, :D] = patch.astype(BF16)
        lane = lax.broadcasted_iota(jnp.int32, (patch.shape[0], 128), 1)
        values = jnp.where(lane % 64 < 32, squares_ref[...], dots)
        high = values.astype(BF16).astype(F32)
        payload_ref[:, D:] = jnp.where(lane < 64, high, values - high).astype(BF16)


def attention_backward(core, grad, mixer_rows, inputs, normed, gain, weights, qkv, context, squares, token):
    rows = grad.shape[0]
    tps, _, width = context.shape
    depth = 2 * D // GROUP
    return pl.pallas_call(
        attention_backward_kernel,
        grid=(tps,),
        in_specs=[
            scalar_spec(),
            whole((rows, D)),
            whole((rows // PATCH, D)),
            whole((rows, D)),
            whole((rows, D)),
            whole((1, D)),
            attention_spec(weights),
            pl.BlockSpec((1, 3, rows, width), lambda j: (j, 0, 0, 0)),
            pl.BlockSpec((1, rows, width), lambda j: (j, 0, 0)),
            whole(squares.shape),
            anywhere(),
        ],
        out_specs=[
            whole((tps, rows, width)),
            whole((rows // PATCH, D)),
            whole((rows // PATCH, D + 128)),
            whole((1, D)),
            halves_spec(depth, 2 * width),
            halves_spec(depth, 2 * width),
        ],
        out_shape=[
            jax.ShapeDtypeStruct((tps, rows, width), BF16),
            jax.ShapeDtypeStruct((rows // PATCH, D), F32),
            jax.ShapeDtypeStruct((rows // PATCH, D + 128), BF16),
            jax.ShapeDtypeStruct((1, D), F32),
            halves_shape(tps, depth, 2 * width),
            halves_shape(tps, depth, 2 * width),
        ],
        scratch_shapes=[
            pltpu.VMEM((D, rows), BF16),
            pltpu.VMEM((rows, D), BF16),
            pltpu.VMEM((rows, D), F32),
            pltpu.VMEM((rows, width), BF16),
            pltpu.VMEM((rows, 3 * width), BF16),
        ],
        compiler_params=params(),
        name="attention_backward",
        cost_estimate=pl.CostEstimate(
            flops=4 * rows * D * D * 4, bytes_accessed=26 << 20, transcendentals=rows * 2048
        ),
    )(core, grad, mixer_rows, inputs, normed, gain, weights, qkv, context, squares, token)


def shifted(block, distance):
    devices = range(lax.axis_size(SEQ))
    route = [(i - distance, i) for i in devices if i - distance in devices]
    return lax.ppermute(block, SEQ, route)


def rms_scale(values):
    return values * inverse_rms(values)


def sequence_first(positions, lengths):
    offsets = jnp.cumsum(lengths) - lengths
    chosen = jnp.where(offsets[None, :] <= positions[:, None], offsets[None, :], 0)
    return jnp.max(chosen, axis=1)


def causal_conv(padded, weight, positions, first):
    count = positions.shape[0]
    total = jnp.zeros((count, padded.shape[1]), jnp.float32)
    for offset in range(CONV):
        lag = CONV - 1 - offset
        keep = (positions - lag >= first).astype(jnp.float32)[:, None]
        total = total + weight[offset][None, :] * padded[offset : offset + count] * keep
    return total


def front_part(padded, step_raw, conv_weight, step_bias, decay_log, positions, first):
    activated = jax.nn.silu(causal_conv(padded, conv_weight, positions, first))
    inner = activated.shape[1] - 2 * STATE
    count = positions.shape[0]
    inner_vals = activated[:, :inner].reshape(count, inner // HEAD_DIM, HEAD_DIM)
    bmatrix = activated[:, inner : inner + STATE]
    cmatrix = activated[:, inner + STATE :]
    steps = jax.nn.softplus(step_raw + step_bias[None, :])
    rates = -jnp.exp(decay_log)
    return (inner_vals, bmatrix, cmatrix, steps, rates)


def block_summary(inner_vals, bmatrix, steps, rates, positions, first):
    logs = jnp.cumsum(steps * rates[None, :], axis=0)
    final = logs[-1]
    in_last = (first == first[-1]).astype(jnp.float32)[:, None]
    weights = jnp.exp(final[None, :] - logs) * in_last * steps
    carried = jnp.exp(final) * (first[-1] < positions[0]).astype(jnp.float32)
    states = jnp.einsum("sh,shp,sn->hpn", weights, inner_vals, bmatrix, precision=highest)
    return (carried, states)


def block_output(inner_vals, bmatrix, cmatrix, steps, rates, skip_gain, incoming, positions, first):
    logs = jnp.cumsum(steps * rates[None, :], axis=0)
    count = positions.shape[0]
    same = (first[:, None] == first[None, :]) & (positions[None, :] <= positions[:, None])
    diff = logs.T[:, :, None] - logs.T[:, None, :]
    decay = jnp.where(same[None], jnp.exp(jnp.where(same[None], diff, 0.0)), 0.0)
    inner_prod = jnp.dot(cmatrix, bmatrix.T, precision=highest, preferred_element_type=jnp.float32)
    mixing = decay * inner_prod[None] * steps.T[:, None, :]
    within = jnp.einsum("hts,shp->thp", mixing, inner_vals, precision=highest)
    carry = jnp.exp(logs) * (first < positions[0]).astype(jnp.float32)[:, None]
    remote = jnp.einsum("tn,hpn->thp", cmatrix, incoming, precision=highest) * carry[:, :, None]
    result = within + remote + skip_gain[None, :, None] * inner_vals
    return result.reshape(count, -1)


def product(left, right, form):
    return jnp.einsum(form, left, right, preferred_element_type=jnp.float32)


def norm_backward(grad, values, gain):
    scale = inverse_rms(values)
    normed = values * scale
    scaled = grad * gain[None, :]
    result = scale * (scaled - normed * jnp.mean(scaled * normed, axis=-1, keepdims=True))
    return (result, jnp.sum(grad * normed, axis=0))


def high_low(values):
    high = values.astype(BF16)
    low = (values - high.astype(F32)).astype(BF16)
    return high, low


def reached(factors, states, distance):
    heads = factors.shape[0]
    columns = jnp.broadcast_to(factors[:, None], (heads, STATE))
    high, low = high_low(columns)
    packed = jnp.concatenate([states.reshape(-1, STATE).astype(BF16), high, low], axis=0)
    return reached_from(packed, distance).reshape(states.shape)


def reached_from(packed, distance):
    count = lax.axis_size(SEQ)
    heads = packed.shape[0] // (HEAD_DIM + 2)
    total = jnp.zeros((heads, HEAD_DIM, STATE), F32)
    chain = jnp.ones((heads, 1, 1), F32)
    for hop in range(1, count // 2 + 1):
        step = hop * distance
        route = [(i, i + step) for i in range(count) if 0 <= i + step < count]
        got = lax.ppermute(packed, SEQ, route).astype(F32)
        total = total + chain * got[: -2 * heads].reshape(total.shape)
        factor = (got[-2 * heads : -heads] + got[-heads:])[:, :1]
        chain = chain * factor[:, :, None]
    return total.reshape(-1, STATE)


def tied(array, *tokens):
    return pl.pallas_call(
        lambda *refs: None,
        in_specs=[anywhere()] * (1 + len(tokens)),
        out_specs=anywhere(),
        out_shape=jax.ShapeDtypeStruct(array.shape, array.dtype),
        input_output_aliases={0: 0},
        name="tied",
        cost_estimate=pl.CostEstimate(flops=0, bytes_accessed=0, transcendentals=0),
    )(array, *tokens)


def swap(array, axis):
    return lax.ppermute(array, axis, [(0, 1), (1, 0)])


def picked(array, axis, index):
    return lax.dynamic_index_in_dim(array, index, axis, False)


def parallel_params(axes):
    return pltpu.CompilerParams(
        dimension_semantics=("arbitrary",) * axes, vmem_limit_bytes=32 * 1024 * 1024
    )


def first_sum_kernel(place_ref, *refs):
    ins, outs = refs[:8], refs[-4:]
    for k in range(4):
        total = ins[2 * k][...].astype(F32) + ins[2 * k + 1][...].astype(F32)
        outs[k][...] = total.reshape(outs[k].shape).astype(BF16)


def first_sum(place, own, got, tokens=()):
    _, _, tps, rows, cols = own.shape
    half = rows // 2
    block = (1, 1, 1, half, cols)
    maps = [
        lambda t, i, p: (i, 1 - p[1], t, 0, 0),
        lambda t, i, p: (i, p[1], t, 0, 0),
        lambda t, i, p: (1 - p[0], i, t, 1, 0),
        lambda t, i, p: (p[0], i, t, 1, 0),
    ]
    specs = [pl.BlockSpec(block, m) for m in maps for _ in range(2)]
    return pl.pallas_call(
        first_sum_kernel,
        grid_spec=pltpu.PrefetchScalarGridSpec(
            num_scalar_prefetch=1,
            grid=(tps, 2),
            in_specs=specs + [anywhere() for _ in tokens],
            out_specs=[
                pl.BlockSpec((1, 1, half, cols), lambda t, i, p: (i, t, 0, 0)) for _ in range(4)
            ],
        ),
        out_shape=[jax.ShapeDtypeStruct((2, tps, half, cols), BF16) for _ in range(4)],
        compiler_params=parallel_params(2),
        name="first_sum",
        cost_estimate=pl.CostEstimate(
            flops=own.size, bytes_accessed=6 * own.size, transcendentals=0
        ),
    )(place, *([own, got] * 4), *tokens)


def second_sum_kernel(place_ref, *refs):
    ins, outs = refs[:8], refs[-4:]
    for k in range(4):
        total = ins[2 * k][...].astype(F32) + ins[2 * k + 1][...].astype(F32)
        outs[k][...] = total.reshape(outs[k].shape).astype(BF16)


def second_sum(place, kept_one, got_one, kept_two, got_two, tokens=()):
    _, tps, half, cols = kept_one.shape
    block = (1, 1, half, cols)
    maps = [
        lambda t, p: (1 - p[0], t, 0, 0),
        lambda t, p: (p[0], t, 0, 0),
        lambda t, p: (1 - p[1], t, 0, 0),
        lambda t, p: (p[1], t, 0, 0),
    ]
    return pl.pallas_call(
        second_sum_kernel,
        grid_spec=pltpu.PrefetchScalarGridSpec(
            num_scalar_prefetch=1,
            grid=(tps,),
            in_specs=[pl.BlockSpec(block, m) for m in maps for _ in range(2)]
            + [anywhere() for _ in tokens],
            out_specs=[pl.BlockSpec((1, half, cols), lambda t, p: (t, 0, 0)) for _ in range(4)],
        ),
        out_shape=[jax.ShapeDtypeStruct((tps, half, cols), BF16) for _ in range(4)],
        compiler_params=parallel_params(1),
        name="second_sum",
        cost_estimate=pl.CostEstimate(
            flops=2 * kept_one.size, bytes_accessed=12 * kept_one.size, transcendentals=0
        ),
    )(place, *([kept_one, got_one] * 2), *([kept_two, got_two] * 2), *tokens)


def third_sum_kernel(one_ref, two_ref, three_ref, four_ref, *refs):
    out_ref = refs[-2]
    half = one_ref.shape[1]
    out_ref[0, :half] = (one_ref[0].astype(F32) + two_ref[0].astype(F32)).astype(BF16)
    out_ref[0, half:] = (three_ref[0].astype(F32) + four_ref[0].astype(F32)).astype(BF16)


def third_sum(kept_one, got_one, kept_two, got_two, carried):
    tps, half, cols = kept_one.shape
    return pl.pallas_call(
        third_sum_kernel,
        grid=(tps,),
        in_specs=[pl.BlockSpec((1, half, cols), lambda t: (t, 0, 0)) for _ in range(4)]
        + [anywhere()],
        out_specs=[pl.BlockSpec((1, 2 * half, cols), lambda t: (t, 0, 0)), anywhere()],
        out_shape=[
            jax.ShapeDtypeStruct((tps, 2 * half, cols), BF16),
            jax.ShapeDtypeStruct(carried.shape, carried.dtype),
        ],
        input_output_aliases={4: 1},
        compiler_params=parallel_params(1),
        name="third_sum",
        cost_estimate=pl.CostEstimate(
            flops=2 * kept_one.size, bytes_accessed=12 * kept_one.size, transcendentals=0
        ),
    )(kept_one, got_one, kept_two, got_two, carried)


def reduce_first(place, own, other, tokens=()):
    return first_sum(place, own, swap(other, "c"), tokens)


def reduce_second(place, sums, tokens=()):
    send_one, keep_one, send_two, keep_two = sums
    return second_sum(
        place, keep_one, swap(send_one, "b"), keep_two, swap(send_two, "a"), tokens
    )


def reduce_third(sums, carried):
    send_one, keep_one, send_two, keep_two = sums
    return third_sum(keep_one, swap(send_one, "a"), keep_two, swap(send_two, "b"), carried)


def over_groups(part):
    return lax.psum(part, "g") if lax.axis_size("g") > 1 else part


def reduce_last(summed):
    return over_groups(lax.psum_scatter(summed, "tp", scatter_dimension=0))


def exchange_last(summed):
    pieces = lax.all_to_all(summed, "tp", 0, 0)
    return over_groups(jnp.sum(pieces.astype(F32), axis=0).astype(BF16))


def unpack_kernel(
    grads_ref,
    expand_ref,
    shrink_ref,
    input_ref,
    output_ref,
    gate_ref,
    inner_ref,
    mixer_ref,
    state_ref,
):
    wide = grads_ref.shape[2]
    deep = D // GROUP
    width = input_ref.shape[2]

    def rows(low, count):
        return grads_ref[0, low : low + count].astype(F32)

    down = wide // GROUP
    for p in range(PIECES):
        base = 3 * deep * p
        for i in range(2):
            expand_ref[i, :, p * wide : (p + 1) * wide] = rows(base + i * deep, deep)
        for i in range(D // wide):
            shrink_ref[p, 0, :, i * wide : (i + 1) * wide] = rows(base + 2 * deep + i * down, down)
    base = 3 * deep * PIECES
    for k in range(3):
        part = rows(base + (k % 2) * deep, deep)
        input_ref[k] = part[:, (k // 2) * width : (k // 2 + 1) * width]
    part = rows(base + deep, deep)[:, width:]
    out_rows = width // GROUP
    for i in range(D // width):
        output_ref[:, i * width : (i + 1) * width] = part[i * out_rows : (i + 1) * out_rows]
    base = base + 2 * deep
    gate_ref[...] = rows(base, deep)
    inner_ref[...] = rows(base + deep, deep)
    for i in range(D // wide):
        mixer_ref[:, i * wide : (i + 1) * wide] = rows(base + 2 * deep + i * down, down)
    state = rows(base + 3 * deep, deep // 2)
    half = wide // 2
    for i in range(2):
        state_ref[i * deep // 2 : (i + 1) * deep // 2] = state[:, i * half : (i + 1) * half]


def unpack(grads, tps):
    _, total, wide = grads.shape
    deep, width, down = D // GROUP, D // tps, wide // GROUP
    shapes = [
        (2, D, PIECES * wide),
        (PIECES, GROUP, down, D),
        (3, D, width),
        (width, D),
        (D, wide),
        (D, wide),
        (wide, D),
        (D, wide // 2),
    ]
    specs = [
        pl.BlockSpec((2, deep, PIECES * wide), lambda j: (0, j, 0)),
        pl.BlockSpec((PIECES, 1, down, D), lambda j: (0, j, 0, 0)),
        pl.BlockSpec((3, deep, width), lambda j: (0, j, 0)),
        pl.BlockSpec((width // GROUP, D), lambda j: (j, 0)),
        pl.BlockSpec((deep, wide), lambda j: (j, 0)),
        pl.BlockSpec((deep, wide), lambda j: (j, 0)),
        pl.BlockSpec((down, D), lambda j: (j, 0)),
        pl.BlockSpec((deep, wide // 2), lambda j: (j, 0)),
    ]
    outs = pl.pallas_call(
        unpack_kernel,
        grid=(GROUP,),
        in_specs=[pl.BlockSpec((1, total, wide), lambda j: (j, 0, 0))],
        out_specs=specs,
        out_shape=[jax.ShapeDtypeStruct(shape, F32) for shape in shapes],
        compiler_params=parallel_params(1),
        name="unpack",
        cost_estimate=pl.CostEstimate(
            flops=grads.size, bytes_accessed=6 * grads.size, transcendentals=0
        ),
    )(grads)
    outs = list(outs)
    outs[1] = outs[1].reshape(PIECES * wide, D)
    return outs


def exact(left, right, dims):
    return lax.dot_general(
        left, right, (dims, ((), ())), precision=highest, preferred_element_type=F32
    )


NN, NT, TN = ((1,), (0,)), ((1,), (1,)), ((0,), (0,))


def column(array, index):
    lane = lax.broadcasted_iota(jnp.int32, array.shape, 1)
    return jnp.sum(jnp.where(lane == index, array, 0.0), axis=1, keepdims=True)


def by_head(pair, one, two):
    lane = lax.broadcasted_iota(jnp.int32, pair, 1)
    return jnp.where(lane < HEAD_DIM, one, two)


def only_head(array, j):
    lane = lax.broadcasted_iota(jnp.int32, array.shape, 1)
    return jnp.where((lane // HEAD_DIM) == j, array, 0.0)


def pair_of(ref, q):
    return ref[:, pl.ds(pl.multiple_of(q * 128, 128), 128)]


def gate_backward_kernel(
    returned_ref,
    weight_ref,
    gain_ref,
    gate_ref,
    mixed_ref,
    cmat_ref,
    reach_ref,
    factor_ref,
    token_ref,
    mix_ref,
    gate_back_ref,
    gain_grad_ref,
    out_grad_ref,
    packed_ref,
):
    back = returned_ref[:, :D]
    extra = returned_ref[:, D:].astype(F32)
    lane = lax.broadcasted_iota(jnp.int32, extra.shape, 1)
    squares = jnp.sum(jnp.where(lane % 64 == 0, extra, 0.0), axis=1, keepdims=True)
    dots = jnp.sum(jnp.where(lane % 64 == 32, extra, 0.0), axis=1, keepdims=True)
    scale = lax.rsqrt(squares / DI + epsilon)
    grad = mm_nt(back, weight_ref[...])
    gate = gate_ref[...]
    mixed = mixed_ref[...]
    gain = gain_ref[...]
    sigma = 1.0 / (1.0 + jnp.exp(-gate))
    act = gate * sigma
    normal = mixed * act * scale
    mix_ref[...] = (normal * gain).astype(BF16)
    gain_grad_ref[...] = jnp.sum(grad * normal, axis=0, keepdims=True)
    gated_grad = scale * (grad * gain - normal * (dots / DI))
    out_grad_ref[...] = gated_grad * act
    gate_back_ref[...] = (gated_grad * mixed * sigma * (1.0 + gate * (1.0 - sigma))).astype(BF16)
    reach = reach_ref[...]
    cmat = cmat_ref[...]
    width = gate.shape[1]
    for q in range(width // 128):
        part = out_grad_ref[:, q * 128 : (q + 1) * 128]
        part = part * by_head(part.shape, column(reach, 2 * q), column(reach, 2 * q + 1))
        packed_ref[q * 128 : (q + 1) * 128] = exact(part, cmat, TN).astype(BF16)
    packed_ref[width:] = factor_ref[...]


def gate_backward(returned, weight, gain, gate, mixed, cmat, reach, factors, token):
    count, width = gate.shape
    args = (returned, weight, gain, gate, mixed, cmat, reach, factors)
    shapes = [
        jax.ShapeDtypeStruct((count, width), BF16),
        jax.ShapeDtypeStruct((count, width), BF16),
        jax.ShapeDtypeStruct((1, width), F32),
        jax.ShapeDtypeStruct((count, width), F32),
        jax.ShapeDtypeStruct((width + factors.shape[0], STATE), BF16),
    ]
    return pl.pallas_call(
        gate_backward_kernel,
        grid=(1,),
        in_specs=[whole(a.shape) for a in args] + [anywhere()],
        out_specs=[whole(o.shape) for o in shapes],
        out_shape=shapes,
        compiler_params=params(),
        name="gate_backward",
        cost_estimate=pl.CostEstimate(
            flops=2 * count * D * width, bytes_accessed=6 << 20, transcendentals=count * width
        ),
    )(*args, token)


def chunk_backward_kernel(
    grad_ref,
    inner_ref,
    bmat_ref,
    cmat_ref,
    logs_ref,
    logs_row_ref,
    steps_row_ref,
    first_ref,
    first_row_ref,
    reach_ref,
    skip_ref,
    incoming_ref,
    token_ref,
    other_token_ref,
    inner_grad_ref,
    bmat_grad_ref,
    cmat_grad_ref,
    logs_grad_ref,
    logs_row_grad_ref,
    steps_row_grad_ref,
    skip_grad_ref,
    product_ref,
    product_grad_ref,
):
    count = grad_ref.shape[0]
    bmat, cmat = bmat_ref[...], cmat_ref[...]
    product_ref[...] = exact(cmat, bmat, NT)
    product_grad_ref[...] = jnp.zeros_like(product_grad_ref)
    cmat_grad_ref[...] = jnp.zeros_like(cmat_grad_ref)
    logs_grad_ref[...] = jnp.zeros_like(logs_grad_ref)
    skip_grad_ref[...] = jnp.zeros_like(skip_grad_ref)

    def one_pair(q, carry):
        inner = pair_of(inner_ref, q)
        grad = pair_of(grad_ref, q)
        incoming = incoming_ref[pl.ds(pl.multiple_of(q * 128, 128), 128), :]
        reading = exact(cmat, incoming, NT)
        row = lax.broadcasted_iota(jnp.int32, (count, count), 0)
        col = lax.broadcasted_iota(jnp.int32, (count, count), 1)
        same = (first_ref[...] == first_row_ref[...]) & (col <= row)
        logs = logs_ref[...]
        reach = reach_ref[...]
        skip = skip_ref[...]
        total = jnp.zeros_like(inner)
        reaches = []
        for j in range(2):
            h = 2 * q + j
            own_grad = only_head(grad, j)
            steps = steps_row_ref[pl.ds(h, 1), :]
            diff = column(logs, h) - logs_row_ref[pl.ds(h, 1), :]
            decay = jnp.where(same, jnp.exp(jnp.where(same, diff, 0.0)), 0.0)
            both = exact(own_grad, inner, NT) * decay
            mixing = decay * product_ref[...]
            product_grad_ref[...] += both * steps
            used = both * product_ref[...]
            total = total + exact(mixing * steps, own_grad, TN)
            over_rows = jnp.sum(used, axis=0, keepdims=True)
            reached_here = column(reach, h)
            reaches.append(reached_here)
            logs_grad = jnp.sum(used * steps, axis=1, keepdims=True)
            logs_grad = logs_grad + reached_here * jnp.sum(
                own_grad * reading, axis=1, keepdims=True
            )
            lane = lax.broadcasted_iota(jnp.int32, logs.shape, 1)
            logs_grad_ref[...] += jnp.where(lane == h, logs_grad, 0.0)
            logs_row_grad_ref[pl.ds(h, 1), :] = -steps * over_rows
            steps_row_grad_ref[pl.ds(h, 1), :] = over_rows
            lane = lax.broadcasted_iota(jnp.int32, skip.shape, 1)
            gained = jnp.sum(jnp.sum(own_grad * inner, axis=1, keepdims=True), axis=0, keepdims=True)
            skip_grad_ref[...] += jnp.where(lane == h, gained, 0.0)
        gains = by_head((1, 128), column(skip, 2 * q), column(skip, 2 * q + 1))
        inner_grad_ref[:, pl.ds(pl.multiple_of(q * 128, 128), 128)] = total + gains * grad
        weighted = grad * by_head(grad.shape, reaches[0], reaches[1])
        cmat_grad_ref[...] += exact(weighted, incoming, NN)
        return carry

    lax.fori_loop(0, grad_ref.shape[1] // 128, one_pair, 0)
    cmat_grad_ref[...] += exact(product_grad_ref[...], bmat, NN)
    bmat_grad_ref[...] = exact(product_grad_ref[...], cmat, TN)


def chunk_backward(args, *tokens):
    count, width = args[0].shape
    heads = args[5].shape[0]
    shapes = [
        jax.ShapeDtypeStruct((count, width), F32),
        jax.ShapeDtypeStruct((count, STATE), F32),
        jax.ShapeDtypeStruct((count, STATE), F32),
        jax.ShapeDtypeStruct((count, heads), F32),
        jax.ShapeDtypeStruct((heads, count), F32),
        jax.ShapeDtypeStruct((heads, count), F32),
        jax.ShapeDtypeStruct((1, heads), F32),
    ]
    return pl.pallas_call(
        chunk_backward_kernel,
        grid=(1,),
        in_specs=[whole(a.shape) for a in args] + [anywhere() for _ in tokens],
        out_specs=[whole(o.shape) for o in shapes],
        out_shape=shapes,
        scratch_shapes=[pltpu.VMEM((count, count), F32), pltpu.VMEM((count, count), F32)],
        compiler_params=params(),
        name="chunk_backward",
        cost_estimate=pl.CostEstimate(
            flops=24 * count * count * width, bytes_accessed=4 << 20, transcendentals=count * count * heads
        ),
    )(*args, *tokens)


def front_backward_kernel(hops, *refs):
    front_backward_body(refs[:hops], *refs[hops:])


def front_backward_body(
    got_refs,
    incoming_ref,
    inner_ref,
    bmat_ref,
    logs_ref,
    steps_ref,
    steps_row_ref,
    raw_row_ref,
    last_ref,
    factor_ref,
    rate_ref,
    bias_ref,
    inner_grad_ref,
    bmat_grad_ref,
    cmat_grad_ref,
    logs_grad_ref,
    logs_row_grad_ref,
    steps_row_grad_ref,
    padded_ref,
    conv_ref,
    keep_ref,
    token_ref,
    raw_grad_ref,
    head_grad_ref,
    conv_grad_ref,
    step_back_ref,
    bias_grad_ref,
    decay_grad_ref,
    act_grad_ref,
    logs_total_ref,
    steps_total_ref,
    padded_grad_ref,
    later_ref,
):
    count, width = inner_ref.shape
    heads = width // HEAD_DIM
    chain = jnp.ones((heads, STATE), F32)
    for k, got_ref in enumerate(got_refs):
        for h in range(heads):
            at = slice(h * HEAD_DIM, (h + 1) * HEAD_DIM)
            part = chain[h : h + 1] * got_ref[at, :].astype(F32)
            later_ref[at, :] = part if k == 0 else later_ref[at, :] + part
        factors = got_ref[width : width + 2 * heads, :].astype(F32)
        chain = chain * (factors[:heads] + factors[heads:])
    bmat = bmat_ref[...]
    logs, steps, last = logs_ref[...], steps_ref[...], last_ref[...]
    final = logs[count - 1 : count, :]
    fading = jnp.exp(final - logs) * last
    weights = fading * steps
    logs_total_ref[...] = logs_grad_ref[...]
    steps_total_ref[...] = jnp.zeros_like(steps_total_ref)
    bmat_total = bmat_grad_ref[...]
    lane = lax.broadcasted_iota(jnp.int32, logs.shape, 1)
    row = lax.broadcasted_iota(jnp.int32, logs.shape, 0)
    for q in range(width // 128):
        cols = slice(q * 128, (q + 1) * 128)
        later = later_ref[cols, :]
        inner = inner_ref[:, cols]
        reading = exact(bmat, later, NT)
        spread = by_head(inner.shape, column(weights, 2 * q), column(weights, 2 * q + 1))
        act_grad_ref[:, cols] = inner_grad_ref[:, cols] + spread * reading
        bmat_total = bmat_total + exact(inner * spread, later, NN)
        crossing = jnp.sum(later * incoming_ref[cols, :], axis=1, keepdims=True)
        for j in range(2):
            h = 2 * q + j
            gained = jnp.sum(only_head(inner * reading, j), axis=1, keepdims=True)
            part = lax.broadcasted_iota(jnp.int32, crossing.shape, 0) // HEAD_DIM == j
            crossed = jnp.sum(jnp.where(part, crossing, 0.0), axis=0, keepdims=True)
            crossed = crossed * column(factor_ref[...], h)
            steps_total_ref[...] += jnp.where(lane == h, fading * gained, 0.0)
            moved = column(weights, h) * gained
            ending = jnp.sum(moved, axis=0, keepdims=True) + crossed
            change = jnp.where(row == count - 1, ending - moved, -moved)
            logs_total_ref[...] += jnp.where(lane == h, change, 0.0)
    act_grad_ref[:, width : width + STATE] = bmat_total
    act_grad_ref[:, width + STATE :] = cmat_grad_ref[...]
    t = lax.broadcasted_iota(jnp.int32, (count, count), 0)
    u = lax.broadcasted_iota(jnp.int32, (count, count), 1)
    after = (t >= u).astype(F32)
    here = (t == u).astype(F32)
    reverse = exact(logs_total_ref[...], after, TN) + exact(logs_row_grad_ref[...], after, NN)
    rate = rate_ref[...]
    steps_grad = steps_row_grad_ref[...] + exact(steps_total_ref[...], here, TN) + rate * reverse
    decay_grad_ref[...] = rate * jnp.sum(steps_row_ref[...] * reverse, axis=1, keepdims=True)
    raw = raw_row_ref[...] + bias_ref[...]
    step_grad = steps_grad / (1.0 + jnp.exp(-raw))
    bias_grad_ref[...] = jnp.sum(step_grad, axis=1, keepdims=True)
    step_back_ref[...] = step_grad.astype(BF16)
    top = 8 - (CONV - 1)
    pre = jnp.zeros(act_grad_ref.shape, F32)
    keep = keep_ref[...]
    for k in range(CONV):
        kept = column(keep, k)
        pre = pre + conv_ref[k : k + 1, :] * padded_ref[top + k : top + k + count, :] * kept
    sigma = 1.0 / (1.0 + jnp.exp(-pre))
    act_grad_ref[...] = act_grad_ref[...] * sigma * (1.0 + pre * (1.0 - sigma))
    padded_grad_ref[...] = jnp.zeros_like(padded_grad_ref)
    for k in range(CONV):
        kept = act_grad_ref[...] * column(keep, k)
        conv_grad_ref[k : k + 1, :] = jnp.sum(
            kept * padded_ref[top + k : top + k + count, :], axis=0, keepdims=True
        )
        padded_grad_ref[top + k : top + k + count, :] += conv_ref[k : k + 1, :] * kept
    raw_grad_ref[...] = padded_grad_ref[8:, :]
    head_grad_ref[...] = padded_grad_ref[:8, :]


def front_backward(gots, args, token):
    count, heads = args[3].shape
    wide = args[17].shape[1]
    shapes = [
        jax.ShapeDtypeStruct((count, wide), F32),
        jax.ShapeDtypeStruct((8, wide), F32),
        jax.ShapeDtypeStruct((CONV, wide), F32),
        jax.ShapeDtypeStruct((heads, count), BF16),
        jax.ShapeDtypeStruct((heads, 1), F32),
        jax.ShapeDtypeStruct((heads, 1), F32),
    ]
    return pl.pallas_call(
        functools.partial(front_backward_kernel, len(gots)),
        grid=(1,),
        in_specs=[whole(a.shape) for a in gots + args] + [anywhere()],
        out_specs=[whole(o.shape) for o in shapes],
        out_shape=shapes,
        scratch_shapes=[
            pltpu.VMEM((count, wide), F32),
            pltpu.VMEM((count, heads), F32),
            pltpu.VMEM((count, heads), F32),
            pltpu.VMEM((count + 8, wide), F32),
            pltpu.VMEM(args[0].shape, F32),
        ],
        compiler_params=params(),
        name="front_backward",
        cost_estimate=pl.CostEstimate(
            flops=24 * count * STATE * wide, bytes_accessed=8 << 20, transcendentals=2 * count * wide
        ),
    )(*gots, *args, token)


def project_backward_kernel(
    mine_ref,
    gate_back_ref,
    inner_back_ref,
    state_back_ref,
    step_back_ref,
    gate_ref,
    inner_ref,
    state_ref,
    step_ref,
    rows_ref,
    normed_ref,
    gain_ref,
    own_ref,
    token_ref,
    blocks_ref,
    gain_grad_ref,
    step_grad_ref,
    total_ref,
):
    grad = mm_nt(gate_back_ref[...], gate_ref[...])
    grad = grad + mm_nt(inner_back_ref[...], inner_ref[...])
    grad = grad + mm_nt(state_back_ref[...], state_ref[...])
    grad = grad + mm_tn(step_back_ref[...], step_ref[...])
    step_grad_ref[...] = mm(step_back_ref[...], normed_ref[...])
    values = rows_ref[...].astype(F32)
    scale = inverse_rms(values)
    normal = values * scale
    gain_grad_ref[...] = jnp.sum(grad * normal, axis=0, keepdims=True)
    scaled = grad * gain_ref[...]
    total_ref[...] = scale * (scaled - normal * jnp.mean(scaled * normal, axis=-1, keepdims=True))
    share = own_ref.shape[0]
    at = pl.ds(pl.multiple_of(mine_ref[0] * share, share), share)
    total_ref[at, :] += own_ref[...]
    width = blocks_ref.shape[2]
    for i in range(blocks_ref.shape[0]):
        blocks_ref[i] = total_ref[:, i * width : (i + 1) * width].astype(BF16)


def project_backward(mine, args, tps, token):
    count = args[0].shape[0]
    heads = args[3].shape[0]
    shapes = [
        jax.ShapeDtypeStruct((tps, count, D // tps), BF16),
        jax.ShapeDtypeStruct((1, D), F32),
        jax.ShapeDtypeStruct((heads, D), F32),
    ]
    return pl.pallas_call(
        project_backward_kernel,
        grid=(1,),
        in_specs=[scalar_spec()] + [whole(a.shape) for a in args] + [anywhere()],
        out_specs=[whole(o.shape) for o in shapes],
        out_shape=shapes,
        scratch_shapes=[pltpu.VMEM((count, D), F32)],
        compiler_params=params(),
        name="project_backward",
        cost_estimate=pl.CostEstimate(
            flops=2 * count * D * 1288, bytes_accessed=6 << 20, transcendentals=count
        ),
    )(mine, *args, token)


def mixer_weight_grads_kernel(
    core_ref,
    normed_ref,
    gate_ref,
    inner_ref,
    state_ref,
    mix_ref,
    back_ref,
    token_ref,
    own_ref,
    other_ref,
):
    core = core_ref[0]
    normed = normed_ref[...]
    deep = D // GROUP
    wide = gate_ref.shape[1]
    put_halves(core, mm_tn(normed, gate_ref[...]), own_ref, other_ref, 0, deep)
    put_halves(core, mm_tn(normed, inner_ref[...]), own_ref, other_ref, deep, 2 * deep)
    rows = wide // GROUP
    mix = mix_ref[...]
    for i in range(D // wide):
        low = 2 * deep + i * rows
        grad = mm_tn(mix, back_ref[:, i * wide : (i + 1) * wide])
        put_halves(core, grad, own_ref, other_ref, low, low + rows)
    low = own_ref.shape[3] - deep // 2
    own, other = core_halves(core, mm_tn(normed, state_ref[...]).astype(BF16))
    for i in range(2):
        cols = slice(i * wide // 2, (i + 1) * wide // 2)
        rows_in = slice(i * deep // 2, (i + 1) * deep // 2)
        own_ref[:, :, 0, low:, cols] = own[:, :, rows_in]
        other_ref[:, :, 0, low:, cols] = other[:, :, rows_in]


def mixer_weight_grads(core, normed, gate, inner, state, mix, back, token):
    wide = gate.shape[1]
    deep = D // GROUP
    depth = 2 * deep + D // GROUP + deep // 2
    args = (normed, gate, inner, state, mix, back)
    return pl.pallas_call(
        mixer_weight_grads_kernel,
        grid=(1,),
        in_specs=[scalar_spec()] + [whole(a.shape) for a in args] + [anywhere()],
        out_specs=[halves_spec(depth, wide)] * 2,
        out_shape=[halves_shape(1, depth, wide)] * 2,
        compiler_params=params(),
        name="mixer_weight_grads",
        cost_estimate=pl.CostEstimate(
            flops=8 * normed.shape[0] * D * wide, bytes_accessed=8 << 20, transcendentals=0
        ),
    )(core, *args, token)


def shards(
    patches,
    byte_embed,
    seq_lengths,
    norm_global,
    proj_gate,
    proj_inner,
    proj_state,
    proj_step,
    step_bias,
    decay_log,
    conv_inner,
    conv_state,
    skip_gain,
    mixer_gain,
    proj_mixer,
    norm_attn,
    attn_input,
    attn_output,
    norm_ffn,
    expand_weight,
    shrink_weight,
    grad_output,
):
    count, quarter = patches.shape
    tps = lax.axis_size("tp")
    mine = lax.axis_index("tp")
    here = lax.axis_index(SEQ)
    core = lax.axis_index("c").reshape(1)
    tail = CONV - 1
    inner_width = proj_inner.shape[1]
    share = count // tps
    total_rows = byte_embed.shape[0]
    rows = total_rows // tps

    narrow = D // GROUP
    slot = lax.axis_index(INNER)

    def folded(array, width):
        rows_in = array.shape[0]
        return array.reshape(rows_in, -1, width).transpose(1, 0, 2).reshape(-1, width)

    attn_in_part = lax.dynamic_slice_in_dim(attn_input, slot * narrow, narrow, 1)
    out_rows = attn_output.shape[0] // GROUP
    attn_out_part = lax.dynamic_slice_in_dim(attn_output, slot * out_rows, out_rows, 0)
    attn_out_part = folded(attn_out_part, quarter)
    hidden_width = expand_weight.shape[2]
    wide = hidden_width // PIECES
    down_rows = wide // GROUP
    ffn_parts = []
    for p in range(PIECES):
        up_part = lax.dynamic_slice(
            expand_weight, (0, slot * narrow, p * wide), (2, narrow, wide)
        )
        down_part = lax.dynamic_slice_in_dim(
            shrink_weight, p * wide + slot * down_rows, down_rows, 0
        )
        ffn_parts.append([up_part.reshape(-1, wide), folded(down_part, wide)])
    attn_parts = [
        jnp.concatenate([attn_in_part[0], attn_in_part[2]], axis=1),
        jnp.concatenate([attn_in_part[1], attn_out_part], axis=1),
    ]
    weights_line = lax.all_gather(jnp.concatenate(attn_parts + ffn_parts[0], axis=0), "tp")
    last_part = jnp.concatenate(ffn_parts[1], axis=0)
    place = jnp.stack([lax.axis_index("a"), lax.axis_index("b")]).astype(jnp.int32)

    def to_rows(array):
        return lax.all_to_all(array.reshape(tps, rows, quarter), "tp", 0, 0)

    def to_columns(blocks):
        return lax.all_to_all(blocks, "tp", 0, 0).reshape(total_rows, quarter)

    positions = here * count + jnp.arange(count, dtype=jnp.int32)
    first = sequence_first(positions, seq_lengths)
    patch_rows = lax.all_gather(patches, "tp", axis=1, tiled=True)
    embed_rows = to_rows(byte_embed)
    cot_rows = to_rows(grad_output)
    global_in = patch_rows.astype(jnp.float32)
    normed = (rms_scale(global_in) * norm_global[None, :]).astype(jnp.bfloat16)
    gate_vals = product(normed, proj_gate, "rd,dc->rc")
    inner_raw = product(normed, proj_inner, "rd,dc->rc")
    state_raw = product(normed, proj_state, "rd,dc->rc")
    step_raw = product(normed, proj_step, "rd,dc->rc")
    raw = jnp.concatenate([inner_raw, state_raw], axis=1)
    before = shifted(raw[count - tail :], 1)
    padded = jnp.concatenate([before, raw], axis=0)
    conv_weight = jnp.concatenate([conv_inner, conv_state], axis=1)

    inner_vals, bmatrix, cmatrix, steps, rates = front_part(
        padded, step_raw, conv_weight, step_bias, decay_log, positions, first
    )
    carried, states = block_summary(inner_vals, bmatrix, steps, rates, positions, first)
    weights = lax.all_gather(tied(weights_line, states), INNER)
    incoming = reached(carried, states, 1)
    mixed = block_output(
        inner_vals, bmatrix, cmatrix, steps, rates, skip_gain, incoming, positions, first
    )
    gate_act = jax.nn.silu(gate_vals)
    gated = mixed * gate_act
    squares = jnp.sum(gated * gated, axis=1, keepdims=True)
    partial = product((gated * mixer_gain[None, :]).astype(BF16), proj_mixer, "rc,cd->rd")
    square_high, square_low = high_low(jnp.broadcast_to(squares, (count, 64)))
    partial = partial + embed_rows[0, 0, 0].astype(F32) * 0.0
    sent = jnp.concatenate([partial.astype(BF16), square_high, square_low], axis=1)
    summed = jnp.sum(
        lax.all_to_all(sent.reshape(tps, share, -1), "tp", 0, 0).astype(F32), axis=0
    )
    own_squares = summed[:, D : D + 1] + summed[:, D + 64 : D + 65]
    last_part = tied(last_part, own_squares)
    last_line = lax.all_to_all(
        jnp.broadcast_to(last_part[None], (tps,) + last_part.shape), "tp", 0, 0
    )
    last_weights = lax.all_gather(last_line, INNER)
    mixer_rows = summed[:, :D] * lax.rsqrt(own_squares / DI + epsilon)
    own_patches = lax.dynamic_slice_in_dim(patch_rows, mine * share, share, 0)
    global_out = own_patches.astype(F32) + mixer_rows

    logs = jnp.cumsum(steps * rates[None, :], axis=0)
    from_before = (first < positions[0]).astype(F32)[:, None]
    reach = jnp.exp(logs) * from_before
    factor_high, factor_low = high_low(jnp.broadcast_to(carried[:, None], (carried.size, STATE)))
    factors = jnp.concatenate([factor_high, factor_low], axis=0)
    flat_inner = inner_vals.reshape(count, -1)
    flat_incoming = incoming.reshape(-1, STATE)
    keep = jnp.stack(
        [(positions - (CONV - 1 - k) >= first).astype(F32) for k in range(CONV)], axis=1
    )
    logs_row, steps_row, raw_row = logs.T, steps.T, step_raw.T
    last = (first == first[-1]).astype(F32)[:, None]
    rate_column, bias_column = rates[:, None], step_bias[:, None]
    wide_padded = jnp.pad(padded, ((8 - tail, 0), (0, 0)))
    step_weight = proj_step.T
    prepared = (
        reach, factors, keep, logs_row, steps_row, raw_row, last, rate_column, bias_column,
        wide_padded, step_weight, flat_inner, flat_incoming,
    )

    hidden, attn_in, attn_normed, qkv, context = attention_forward(
        embed_rows, global_out[:, None, :], norm_attn[None, :], weights, prepared
    )
    ffn_normed, ffn_turned, cot_whole, out_acc, normed_acc, own_first, other_first = (
        feed_forward_first(core, hidden, cot_rows, norm_ffn[None, :], weights)
    )
    first_one = reduce_first(place, own_first, other_first)
    first_two = reduce_second(place, first_one)
    layer_blocks, hidden_grad, norm_ffn_part, last_grad = feed_forward_last(
        core,
        hidden,
        cot_whole,
        norm_ffn[None, :],
        last_weights,
        ffn_normed,
        ffn_turned,
        out_acc,
        normed_acc,
        first_two[0],
    )
    layer_output = to_columns(layer_blocks)
    first_three, hidden_grad = reduce_third(first_two, hidden_grad)
    embed_blocks, own_grad, payload, norm_attn_part, own_attn, other_attn = attention_backward(
        core,
        hidden_grad,
        mixer_rows,
        attn_in,
        attn_normed,
        norm_attn[None, :],
        weights,
        qkv,
        context,
        own_squares,
        layer_output,
    )
    last_three = lax.psum_scatter(last_grad, INNER, scatter_dimension=0)
    embed_columns = to_columns(embed_blocks)
    embed_grad = embed_columns.astype(F32)

    attn_one = reduce_first(place, own_attn, other_attn)
    returned = lax.all_gather(payload, "tp", axis=0, tiled=True)
    mix_back_in = returned[:, :D]
    mix_low, gate_back, mixer_gain_grad, mixed_grad, packed = gate_backward(
        returned,
        proj_mixer,
        mixer_gain[None, :],
        gate_vals,
        mixed,
        cmatrix,
        reach,
        factors,
        attn_one[0],
    )
    chunk_grads = chunk_backward(
        (
            mixed_grad,
            flat_inner,
            bmatrix,
            cmatrix,
            logs,
            logs_row,
            steps_row,
            first[:, None],
            first[None, :],
            reach,
            skip_gain[None, :],
            flat_incoming,
        ),
        attn_one[0],
        own_attn,
    )
    ffn_sums = tied(jnp.concatenate([first_three, last_three], axis=1), chunk_grads[6])
    ffn_part = reduce_last(ffn_sums)
    attn_two = reduce_second(place, attn_one, (chunk_grads[0],))
    skip_gain_grad = chunk_grads[6][0]
    devices = lax.axis_size(SEQ)
    gots = tuple(
        lax.ppermute(packed, SEQ, [(i + hop, i) for i in range(devices - hop)])
        for hop in range(1, devices // 2 + 1)
    )
    raw_grad, head_grad, conv_grad, step_back, step_bias_grad, decay_log_grad = front_backward(
        gots,
        (
            flat_incoming,
            flat_inner,
            bmatrix,
            logs,
            steps,
            steps_row,
            raw_row,
            last,
            carried[None, :],
            rate_column,
            bias_column,
        )
        + tuple(chunk_grads[:6])
        + (
            wide_padded,
            conv_weight,
            keep,
        ),
        attn_two[1],
    )
    step_bias_grad, decay_log_grad = step_bias_grad[:, 0], decay_log_grad[:, 0]
    tail_grad = shifted(head_grad, -1)
    raw_grad = jnp.concatenate(
        [raw_grad[: count - 8], raw_grad[count - 8 :] + tail_grad], axis=0
    ).astype(BF16)
    inner_back, state_back = raw_grad[:, :inner_width], raw_grad[:, inner_width:]
    own_mixer, other_mixer = mixer_weight_grads(
        core, normed, gate_back, inner_back, state_back, mix_low, mix_back_in, attn_two[1]
    )
    mixer_one = reduce_first(place, own_mixer, other_mixer)
    attn_three, mixer_kept = reduce_third(attn_two, mixer_one[1])
    attn_part = reduce_last(tied(attn_three, ffn_part))
    mixer_two = reduce_second(place, (mixer_one[0], mixer_kept) + tuple(mixer_one[2:]))
    mixer_three, step_back = reduce_third(mixer_two, step_back)
    mixer_three = mixer_three[0]
    mixer_part = over_groups(mixer_three)
    state_rows = lax.all_gather(mixer_part[3 * narrow :], "tp")
    state_rows = jnp.sum(state_rows.astype(F32), axis=0).astype(BF16)
    columns, norm_global_part, step_grad = project_backward(
        mine.reshape(1),
        (
            gate_back,
            inner_back,
            state_back,
            step_back,
            proj_gate,
            proj_inner,
            proj_state,
            step_weight,
            patch_rows,
            normed,
            norm_global[None, :],
            own_grad,
        ),
        tps,
        state_rows,
    )
    norm_global_part = norm_global_part[0]
    shared = jnp.concatenate(
        [
            conv_grad[:, inner_width:].reshape(-1),
            norm_attn_part[0],
            norm_ffn_part[0],
            norm_global_part,
        ]
    ).reshape(-1, quarter)
    shared_high, shared_low = high_low(shared)
    shared_rows = jnp.concatenate([shared_high, shared_low], axis=0)
    returned = lax.all_to_all(
        jnp.concatenate(
            [columns, jnp.broadcast_to(shared_rows[None], (tps,) + shared_rows.shape)], axis=1
        ),
        "tp",
        0,
        0,
    )
    returned = jnp.sum(returned.astype(F32), axis=0)
    patch_grad = returned[:count]
    shared = returned[count : count + shared.shape[0]] + returned[count + shared.shape[0] :]
    shared = shared.reshape(-1)
    held = conv_state.size
    shared = (
        shared[:held].reshape(conv_state.shape),
        shared[held : held + D],
        shared[held + D : held + 2 * D],
        shared[held + 2 * D :],
    )
    (
        conv_state_grad,
        norm_attn_grad,
        norm_ffn_grad,
        norm_global_grad,
        proj_step_grad,
        step_bias_grad,
        decay_log_grad,
        conv_inner_grad,
        skip_gain_grad,
        mixer_gain_grad,
    ) = lax.psum(
        shared
        + (
            step_grad.T,
            step_bias_grad,
            decay_log_grad,
            conv_grad[:, :inner_width],
            skip_gain_grad,
            mixer_gain_grad[0],
        ),
        SEQ,
    )
    ffn_depth, attn_depth = 3 * narrow, 2 * narrow
    all_grads = lax.all_gather(
        jnp.concatenate([ffn_part, attn_part, mixer_part[: 3 * narrow], state_rows]), INNER
    )
    (
        expand_grad,
        shrink_grad,
        attn_input_grad,
        attn_output_grad,
        proj_gate_grad,
        proj_inner_grad,
        proj_mixer_grad,
        proj_state_grad,
    ) = unpack(all_grads, tps)
    return (
        layer_output,
        embed_grad,
        patch_grad,
        norm_global_grad,
        proj_gate_grad,
        proj_inner_grad,
        proj_state_grad,
        proj_step_grad,
        step_bias_grad,
        decay_log_grad,
        conv_inner_grad,
        conv_state_grad,
        skip_gain_grad,
        mixer_gain_grad,
        proj_mixer_grad,
        norm_attn_grad,
        attn_input_grad,
        attn_output_grad,
        norm_ffn_grad,
        expand_grad,
        shrink_grad,
    )


def solution(mesh):
    seq, tps = mesh.shape["seq"], mesh.shape["tp"]
    fine = Mesh(mesh.devices.reshape(seq // GROUP, 2, 2, 2, tps), SEQ + ("tp",))
    rows_cols = P(SEQ, "tp")
    last = P(None, "tp")
    lead = P("tp", None)
    return jax.shard_map(
        shards,
        mesh=fine,
        in_specs=(
            rows_cols,
            rows_cols,
            P(),
            P(),
            last,
            last,
            P(),
            last,
            P("tp"),
            P("tp"),
            last,
            P(),
            P("tp"),
            P("tp"),
            lead,
            P(),
            P(None, None, "tp"),
            lead,
            P(),
            P(None, None, "tp"),
            lead,
            rows_cols,
        ),
        out_specs=(
            rows_cols,
            rows_cols,
            rows_cols,
            P(),
            last,
            last,
            P(),
            last,
            P("tp"),
            P("tp"),
            last,
            P(),
            P("tp"),
            P("tp"),
            lead,
            P(),
            P(None, None, "tp"),
            lead,
            P(),
            P(None, None, "tp"),
            lead,
        ),
        check_vma=False,
    )
```
